32 devices in a mesh: ctx: 16 (over z, x, core), ws: 2 (over y).
Axes of the slice: x: 2, y: 2, z: 4, core: 2. Of those that a mesh axis runs over, the one named last changes fastest.
Arguments:
- tokens: bfloat16 [2, 2048, 960], P('ws', 'ctx'), may hold values from -6 to 6
- cotangent: bfloat16 [2, 2048, 960], P('ws', 'ctx'), may hold values from -6 to 6
- w_query: bfloat16 [960, 960], P('ws'), may hold values from -0.1875 to 0.1875
- key_weight: bfloat16 [960, 320], P('ws'), may hold values from -0.1875 to 0.1875
- value_weight: bfloat16 [960, 320], P('ws'), may hold values from -0.1875 to 0.1875
- w_out: bfloat16 [960, 960], P('ws'), may hold values from -3.5 to 3.5
- w_gate: bfloat16 [960, 2560], P('ws'), may hold values from -0.1875 to 0.1875
- w_up: bfloat16 [960, 2560], P('ws'), may hold values from -0.1875 to 0.1875
- w_down: bfloat16 [2560, 960], P('ws'), may hold values from -0.125 to 0.125
- gain_attn: bfloat16 [960], P('ws'), may hold values from 0.5 to 1.5
- gain_ffn: bfloat16 [960], P('ws'), may hold values from 0.5 to 1.5
- block_order: int32 [32], replicated, may hold values from 0 to 31, each once
- sel_mid: int32 [2, 1536], P('ws'), may hold values from 0 to 127, as said below
- live_mid: int32 [2, 1536], P('ws'), may hold values from 0 to 1, as said below
- sel_last: int32 [2, 1024], P('ws'), may hold values from 0 to 127, as said below
- live_last: int32 [2, 1024], P('ws'), may hold values from 0 to 1, as said below
Outputs:
- output: bfloat16 [2, 2048, 960], P('ws', 'ctx')
- grad_tokens: float32 [2, 2048, 960], P('ws', 'ctx')
- query_weight_gradient: float32 [960, 960], P('ws')
- grad_key: float32 [960, 320], P('ws')
- grad_value: float32 [960, 320], P('ws')
- grad_out: float32 [960, 960], P('ws')
- grad_gate: float32 [960, 2560], P('ws')
- grad_up: float32 [960, 2560], P('ws')
- grad_down: float32 [2560, 960], P('ws')
- grad_gain_attn: float32 [960], P('ws')
- grad_gain_ffn: float32 [960], P('ws')
The draws below stay inside these ranges and needn't reach their ends.
Inputs may be any that keep to these rules, and one draw needn't show every extreme that they name: `sel_mid`: within a group each device's run of 96 slots names distinct local rows of that device. `live_mid`: in each device's run the live slots come first; every device has at least half of its 96 slots live and one device of each group has all live. `sel_last`: each device's run of 64 slots equals the first 64 slots of its run in sel_mid. `live_last`: in each device's run the live slots come first, are also live at step two, number at least half of 64; one device of each group has all live.
All inputs are finite; a program needn't handle non-finite values.
Results may differ from the reference program's by a relative error of at most 0.04.
Values may be sent and summed in bfloat16 or wider, within the bound.
No kernel may reach another device: no remote copies, remote signals or barrier semaphores. Data moves between devices by JAX's collectives and lax.ppermute only.
A program may use at most 320 MiB of HBM per device.

```python
import jax
import jax.numpy as jnp
from jax import lax

MODEL_WIDTH = 960
FF = 2560
QUERY_HEADS = 15
KEY_VALUE_HEADS = 5
HEAD_SIZE = 64
TOK_DEV = 128
BLK = 64
CONT = 1024
GROUPS = 2
TOKG = 2048
NBLK = 32
CAP1 = 96
CAP2 = 64
SLOTS1 = 1536
SLOTS2 = 1024


def pick_slots(key):
    base_key = jax.random.fold_in(key, 7)
    dev_count = SLOTS1 // CAP1
    subkeys = jax.random.split(base_key, 4)
    spread = jax.random.randint(subkeys[0], (GROUPS, dev_count, TOK_DEV), 0, 32768)
    scores = spread * TOK_DEV + jnp.arange(TOK_DEV, dtype=jnp.int32)[None, None, :]
    row_order = jnp.argsort(scores, axis=-1, stable=True).astype(jnp.int32)
    floor_mid = (CAP1 + 1) // 2
    count_mid = floor_mid + jax.random.randint(subkeys[1], (GROUPS, dev_count), 0, CAP1 - floor_mid + 1)
    fullest = jax.random.randint(subkeys[2], (GROUPS, 1), 0, dev_count)
    chosen = jnp.arange(dev_count, dtype=jnp.int32)[None, :] == fullest
    count_mid = jnp.where(chosen, CAP1, count_mid)
    floor_last = (CAP2 + 1) // 2
    count_room = jnp.minimum(count_mid, CAP2) - floor_last + 1
    count_last = floor_last + jax.random.randint(subkeys[3], (GROUPS, dev_count), 0, 1048576) % count_room
    count_last = jnp.where(chosen, CAP2, count_last)
    sel_mid = row_order[:, :, :CAP1].reshape(GROUPS, SLOTS1)
    live_mid = (jnp.arange(CAP1, dtype=jnp.int32)[None, None, :] < count_mid[:, :, None]).astype(jnp.int32).reshape(GROUPS, SLOTS1)
    sel_last = row_order[:, :, :CAP2].reshape(GROUPS, SLOTS2)
    live_last = (jnp.arange(CAP2, dtype=jnp.int32)[None, None, :] < count_last[:, :, None]).astype(jnp.int32).reshape(GROUPS, SLOTS2)
    return (sel_mid, live_mid, sel_last, live_last)


def draw_sel_mid(key, part):
    return pick_slots(key)[0]


def draw_live_mid(key, part):
    return pick_slots(key)[1]


def draw_sel_last(key, part):
    return pick_slots(key)[2]


def draw_live_last(key, part):
    return pick_slots(key)[3]


def level_of(own_key, dims, cuts, least, largest):
    def one(position, blocks):
        heights = jax.random.uniform(jax.random.fold_in(jax.random.fold_in(own_key, 6), position), (blocks,), jnp.float32, least / len(cuts), largest / len(cuts))
        return jnp.repeat(jnp.exp(heights), dims[position] // blocks).reshape((-1,) + (1,) * (len(dims) - position - 1))

    loudness = one(*cuts[0])
    for cut in cuts[1:]:
        loudness = loudness * one(*cut)
    return loudness


def normal_values(key, shape, width, bound, pieces=(), kind=jnp.bfloat16):
    loudness = level_of(key, shape, pieces, -0.22, 0.18) if pieces else 1.0
    result = jax.random.normal(key, shape, jnp.float32) * width * loudness
    return jnp.minimum(jnp.maximum(result, -bound), bound).astype(kind)


def setup_inputs(seed: int = 0) -> dict:
    streams_of = jax.random.split(jax.random.key(seed), 17)
    return {
        "tokens": normal_values(streams_of[0], (GROUPS, TOKG, MODEL_WIDTH), 1.0, 6.0, ((0, 2), (1, 16))),
        "cotangent": normal_values(streams_of[1], (GROUPS, TOKG, MODEL_WIDTH), 1.0, 6.0, ((0, 2), (1, 16))),
        "w_query": normal_values(streams_of[2], (MODEL_WIDTH, QUERY_HEADS * HEAD_SIZE), MODEL_WIDTH ** -0.5, 0.1875, ((0, 2),)),
        "key_weight": normal_values(streams_of[3], (MODEL_WIDTH, KEY_VALUE_HEADS * HEAD_SIZE), MODEL_WIDTH ** -0.5, 0.1875, ((0, 2),)),
        "value_weight": normal_values(streams_of[4], (MODEL_WIDTH, KEY_VALUE_HEADS * HEAD_SIZE), MODEL_WIDTH ** -0.5, 0.1875, ((0, 2),)),
        "w_out": normal_values(streams_of[5], (QUERY_HEADS * HEAD_SIZE, MODEL_WIDTH), (max(1, QUERY_HEADS * HEAD_SIZE * 8 // TOKG)) ** -0.5, 3.5, ((0, 2),)),
        "w_gate": normal_values(streams_of[6], (MODEL_WIDTH, FF), MODEL_WIDTH ** -0.5, 0.1875, ((0, 2),)),
        "w_up": normal_values(streams_of[7], (MODEL_WIDTH, FF), MODEL_WIDTH ** -0.5, 0.1875, ((0, 2),)),
        "w_down": normal_values(streams_of[8], (FF, MODEL_WIDTH), FF ** -0.5, 0.125, ((0, 2),)),
        "gain_attn": jnp.clip(1.0 + 0.1 * jax.random.normal(streams_of[9], (MODEL_WIDTH,), jnp.float32), 0.5, 1.5).astype(jnp.bfloat16),
        "gain_ffn": jnp.clip(1.0 + 0.1 * jax.random.normal(streams_of[10], (MODEL_WIDTH,), jnp.float32), 0.5, 1.5).astype(jnp.bfloat16),
        "block_order": jax.random.permutation(streams_of[11], NBLK).astype(jnp.int32),
        "sel_mid": draw_sel_mid(jax.random.fold_in(streams_of[16], 71), 0),
        "live_mid": draw_live_mid(jax.random.fold_in(streams_of[16], 71), 0),
        "sel_last": draw_sel_last(jax.random.fold_in(streams_of[16], 71), 0),
        "live_last": draw_live_last(jax.random.fold_in(streams_of[16], 71), 0),
    }


EPSILON = 1e-05
ROPE_BASE = 10000.0
MASK_FLOOR = -1e+30
PRECISE = lax.Precision.HIGHEST

@jax.custom_vjp
def lower_precision(v):
    return lax.optimization_barrier(v.astype(jnp.bfloat16)).astype(jnp.float32)

@jax.custom_vjp
def low_back(v):
    return v

def low_keep(v):
    return (lower_precision(v), None)

def low_pass(kept, grad):
    return (grad,)

def back_keep(v):
    return (v, None)

def back_low(kept, grad):
    return (lower_precision(grad),)
lower_precision.defvjp(low_keep, low_pass)
low_back.defvjp(back_keep, back_low)

def matmul(left, right):
    return jnp.dot(left, right, precision=PRECISE, preferred_element_type=jnp.float32)

def rms_normed(values):
    return values * lax.rsqrt(lax.optimization_barrier(jnp.mean(values * values, axis=-1, keepdims=True)) + EPSILON)

def rotary_embedding(values, token_positions, head_count):
    total_row_count = values.shape[0]
    shaped = values.reshape(total_row_count, head_count, HEAD_SIZE)
    half_size = HEAD_SIZE // 2
    frequency = ROPE_BASE ** (-jnp.arange(half_size, dtype=jnp.float32) / half_size)
    angles = token_positions.astype(jnp.float32)[:, None] * frequency[None, :]
    cosine = jnp.cos(angles)[:, None, :]
    sine_part = jnp.sin(angles)[:, None, :]
    front = shaped[..., :half_size]
    behind = shaped[..., half_size:]
    turned = jnp.concatenate([front * cosine - behind * sine_part, behind * cosine + front * sine_part], axis=-1)
    return turned.reshape(total_row_count, head_count * HEAD_SIZE)

def segment_of(token_positions, prompt):
    return jnp.where(token_positions < prompt, 0, 1 + (token_positions - prompt) // CONT)

def visible(query_places, key_places, key_live, prompt):
    query_seg = segment_of(query_places, prompt)
    key_seg = segment_of(key_places, prompt)
    earlier = key_places[None, :] <= query_places[:, None]
    shared = (key_seg[None, :] == 0) | (key_seg[None, :] == query_seg[:, None])
    itself = key_places[None, :] == query_places[:, None]
    return earlier & shared & ((key_live[None, :] > 0) | itself)

def block_size(total_row_count, upper_limit):
    block_length = total_row_count
    while block_length > upper_limit and block_length % 2 == 0:
        block_length = block_length // 2
    return block_length

def attention(query_matrix, rotated_keys, values_lower_precision, token_positions, live_mask, prompt):
    total_row_count = query_matrix.shape[0]
    queries_per_group = QUERY_HEADS // KEY_VALUE_HEADS
    attention_score_scale = HEAD_SIZE ** (-0.5)
    query_length = block_size(total_row_count, 512)
    query_block_list = query_matrix.reshape(total_row_count // query_length, query_length, KEY_VALUE_HEADS, queries_per_group, HEAD_SIZE)
    place_blocks = token_positions.reshape(total_row_count // query_length, query_length)
    key_head_rows = rotated_keys.reshape(total_row_count, KEY_VALUE_HEADS, HEAD_SIZE)
    value_head_rows = values_lower_precision.reshape(total_row_count, KEY_VALUE_HEADS, HEAD_SIZE)

    def one_block(query_pair):
        query_part, query_places = query_pair
        scores = jnp.einsum('qhgd,khd->hgqk', query_part, key_head_rows, precision=PRECISE)
        scores = low_back(scores * attention_score_scale)
        allowed = visible(query_places, token_positions, live_mask, prompt)
        scores = jnp.where(allowed[None, None], scores, MASK_FLOOR)
        weights = jax.nn.softmax(scores, axis=-1)
        return jnp.einsum('hgqk,khd->qhgd', lower_precision(weights), value_head_rows, precision=PRECISE)
    mixed_rows = lax.map(jax.checkpoint(one_block), (query_block_list, place_blocks))
    return mixed_rows.reshape(total_row_count, QUERY_HEADS * HEAD_SIZE)

def recursion_block(current, token_positions, live_mask, params, prompt):
    w_query, key_weight, value_weight, w_out, w_gate, w_up, w_down, gain_attn, gain_ffn = params
    normed = lower_precision(rms_normed(current) * gain_attn)
    query_lin = low_back(matmul(normed, w_query))
    key_linear = low_back(matmul(normed, key_weight))
    values_lower_precision = lower_precision(low_back(matmul(normed, value_weight)))
    query_matrix = lower_precision(rotary_embedding(query_lin, token_positions, QUERY_HEADS))
    rotated_keys = lower_precision(rotary_embedding(key_linear, token_positions, KEY_VALUE_HEADS))
    mixed_low = lower_precision(low_back(attention(query_matrix, rotated_keys, values_lower_precision, token_positions, live_mask, prompt)))
    middle = current + low_back(matmul(mixed_low, w_out))
    second = lower_precision(rms_normed(middle) * gain_ffn)
    gate_lin = low_back(matmul(second, w_gate))
    up_lin = low_back(matmul(second, w_up))
    hidden = lower_precision(jax.nn.silu(gate_lin) * up_lin)
    return middle + low_back(matmul(hidden, w_down))

def slot_rows(selection, capacity):
    owners = jnp.arange(selection.shape[0], dtype=jnp.int32) // capacity
    return (owners * TOK_DEV + selection).astype(jnp.int32)

def whole_layer(tokens_wide, params, token_positions, sel_mid, live_mid, sel_last, live_last):
    all_rows = token_positions.shape[0]
    prompt = all_rows // 2
    results = []
    for group_id in range(GROUPS):
        hidden_state = tokens_wide[group_id]
        step_plans = [(jnp.arange(all_rows, dtype=jnp.int32), jnp.ones((all_rows,), jnp.int32)), (slot_rows(sel_mid[group_id], CAP1), live_mid[group_id]), (slot_rows(sel_last[group_id], CAP2), live_last[group_id])]
        for picked, live_mask in step_plans:
            current = hidden_state[picked]
            updated = recursion_block(current, token_positions[picked], live_mask, params, prompt)
            hidden_state = hidden_state.at[picked].set(jnp.where(live_mask[:, None] > 0, updated, current))
        results.append(hidden_state)
    return jnp.stack(results)

def reference(tokens, cotangent, w_query, key_weight, value_weight, w_out, w_gate, w_up, w_down, gain_attn, gain_ffn, block_order, sel_mid, live_mid, sel_last, live_last):
    token_positions = (block_order[:, None] * BLK + jnp.arange(BLK, dtype=jnp.int32)[None, :]).reshape(-1).astype(jnp.int32)
    params = tuple((weight.astype(jnp.float32) for weight in (w_query, key_weight, value_weight, w_out, w_gate, w_up, w_down, gain_attn, gain_ffn)))

    def forward(tokens_wide, *weights):
        return whole_layer(tokens_wide, weights, token_positions, sel_mid, live_mid, sel_last, live_last)
    output, pullback = jax.vjp(forward, tokens.astype(jnp.float32), *params)
    grad_terms = pullback(cotangent.astype(jnp.float32))
    return (output.astype(jnp.bfloat16), grad_terms[0], grad_terms[1], grad_terms[2], grad_terms[3], grad_terms[4], grad_terms[5], grad_terms[6], grad_terms[7], grad_terms[8], grad_terms[9])
```

```python
import functools

import jax
import jax.numpy as jnp
from jax import lax
from jax.experimental import pallas as pl
from jax.experimental.pallas import tpu as pltpu
from jax.sharding import PartitionSpec as P

QUERY_HEADS = 15
KEY_VALUE_HEADS = 5
HEAD_SIZE = 64
SHARE = QUERY_HEADS // KEY_VALUE_HEADS
BLK = 64
CONT_BITS = 10
EPSILON = 1e-05
ROPE_BASE = 10000.0
MASK_FLOOR = -1e30
SCALE = HEAD_SIZE ** (-0.5)

BF = jnp.bfloat16
F32 = jnp.float32
AXES = ("ctx", "ws")
FF_CHUNK = 512
VMEM_LIMIT = 60 * 1024 * 1024

Y_BIT, C_BIT, X_BIT, Z1_BIT, Z2_BIT = 1, 2, 4, 8, 16
NEAR = (0, X_BIT, Y_BIT, Z1_BIT, X_BIT | Y_BIT | Z1_BIT, X_BIT | Y_BIT, Y_BIT | Z1_BIT, Z1_BIT | X_BIT)


def hop(value, mask):
    return lax.ppermute(value, AXES, [(i, i ^ mask) for i in range(32)])


def swap_place(i):
    y, z2 = i & 1, (i >> 4) & 1
    return (i & ~(Y_BIT | Z2_BIT)) | (Z2_BIT if y else 0) | (Y_BIT if z2 else 0)


def move(value):
    return lax.ppermute(value, AXES, [(i, swap_place(i)) for i in range(32)])


def ctx_mask(mask):
    return (
        (1 if mask & C_BIT else 0)
        | (2 if mask & X_BIT else 0)
        | (4 if mask & Z1_BIT else 0)
        | (8 if mask & Y_BIT else 0)
    )


NT = (((1,), (1,)), ((), ()))
TN = (((0,), (0,)), ((), ()))
NN = (((1,), (0,)), ((), ()))


def mm(left, right, dims=NN, precision=None):
    return lax.dot_general(left, right, dims, precision=precision, preferred_element_type=F32)


def normed_rows(values):
    inverse = lax.rsqrt(jnp.mean(values * values, axis=-1, keepdims=True) + EPSILON)
    return values * inverse, inverse


def norm_back(grad_in, normed, inverse, gain):
    scaled = grad_in * gain
    return inverse * (scaled - normed * jnp.mean(scaled * normed, axis=-1, keepdims=True))


def turn(values, cosine, sine, back=False):
    rows, width = values.shape
    lane = lax.broadcasted_iota(jnp.int32, (rows, 128), 1)
    first = (lane & (HEAD_SIZE - 1)) < HEAD_SIZE // 2
    if back:
        sine = -sine
    pieces = []
    for start in range(0, width, 128):
        wide = min(128, width - start)
        part = values[:, start : start + wide]
        if wide < 128:
            part = jnp.concatenate([part, jnp.zeros((rows, 128 - wide), F32)], axis=1)
        other = jnp.where(first, pltpu.roll(part, 96, 1), pltpu.roll(part, 32, 1))
        pieces.append((part * cosine + other * sine)[:, :wide])
    return jnp.concatenate(pieces, axis=1)


def vm():
    return pl.BlockSpec(memory_space=pltpu.VMEM)


def sm():
    return pl.BlockSpec(memory_space=pltpu.SMEM)


def hbm():
    return pl.BlockSpec(memory_space=pl.ANY)


def shaped(shape, dtype):
    return jax.ShapeDtypeStruct(shape, dtype)


def params(**kw):
    return pltpu.CompilerParams(vmem_limit_bytes=VMEM_LIMIT, **kw)


def estimate(flops, nbytes):
    return pl.CostEstimate(flops=int(flops), bytes_accessed=int(nbytes), transcendentals=0)


class Weight:
    def __init__(self, shape, arrays, offsets):
        self.shape, self.arrays, self.offsets = shape, arrays, offsets


def start_weights(weights, refs, buffers, sems, coords):
    copies, at = [], 0
    for weight, buffer in zip(weights, buffers, strict=True):
        mine = []
        for offset in weight.offsets:
            ref = refs[at]
            row, col = offset(coords)
            rows, cols = ref.shape
            if not isinstance(row, int):
                row = pl.multiple_of(row, 16)
            if cols == buffer.shape[1]:
                target = buffer.at[pl.ds(row, rows), :]
            else:
                target = buffer.at[pl.ds(row, rows), pl.ds(pl.multiple_of(col, 128), cols)]
            copy = pltpu.make_async_copy(ref, target, sems.at[at])
            copy.start()
            mine.append(copy)
            at += 1
        copies.append(mine)
    return copies


def wait_all(copies):
    for copy in copies:
        copy.wait()


def read_coords(ref):
    return [ref[i] for i in range(4)]


def project(x, gain, wq, wk, wv, cosine, sine, first_ref, q_ref, kv_ref):
    normed, _ = normed_rows(x)
    first_in = (normed * gain).astype(BF)
    first_ref[...] = first_in
    key = turn(mm(first_in, wk[...]), cosine, sine)
    value = mm(first_in, wv[...])
    for h in range(KEY_VALUE_HEADS):
        at = slice(h * HEAD_SIZE, (h + 1) * HEAD_SIZE)
        kv_ref[:, h * 128 : (h + 1) * 128] = jnp.concatenate(
            [key[:, at], value[:, at]], axis=1
        ).astype(BF)
    query = (turn(mm(first_in, wq[...]), cosine, sine).astype(BF) * SCALE).astype(BF)
    wide = SHARE * HEAD_SIZE
    for h in range(KEY_VALUE_HEADS):
        q_ref[h] = query[:, h * wide : (h + 1) * wide]


def first_kernel(weights, n_pieces, coords_ref, x_ref, gain_ref, cos_ref, sin_ref, *rest):
    refs, rest = rest[:n_pieces], rest[n_pieces:]
    first_ref, q_ref, kv_ref, wq, wk, wv, sems = rest
    copies = start_weights(weights, refs, (wq, wk, wv), sems, read_coords(coords_ref))
    for mine in copies:
        wait_all(mine)
    project(
        x_ref[...].astype(F32), gain_ref[...], wq, wk, wv, cos_ref[...], sin_ref[...],
        first_ref, q_ref, kv_ref,
    )


def weight_scratch(weights):
    return [pltpu.VMEM(w.shape, BF) for w in weights]


def pieces_of(weights):
    return [a for w in weights for a in w.arrays]


def first_call(coords, tokens, gain, cosine, sine, weights):
    rows, width = tokens.shape
    kv_width = weights[1].shape[1]
    arrays = pieces_of(weights)
    return pl.pallas_call(
        functools.partial(first_kernel, weights, len(arrays)),
        name="first_projection",
        out_shape=(
            shaped((rows, width), BF),
            shaped((KEY_VALUE_HEADS, rows, SHARE * HEAD_SIZE), BF),
            shaped((rows, 2 * kv_width), BF),
        ),
        in_specs=[sm()] + [vm()] * 4 + [hbm()] * len(arrays),
        out_specs=(vm(), vm(), vm()),
        scratch_shapes=weight_scratch(weights) + [pltpu.SemaphoreType.DMA((len(arrays),))],
        compiler_params=params(),
        cost_estimate=estimate(2 * rows * width * 1600, 4e6),
    )(coords, tokens, gain, cosine, sine, *arrays)


def padded_heads(wide_rows, left):
    rows = wide_rows.shape[0]
    blank = jnp.zeros((rows, HEAD_SIZE), wide_rows.dtype)
    stacked = []
    for j in range(SHARE):
        part = wide_rows[:, j * HEAD_SIZE : (j + 1) * HEAD_SIZE]
        stacked.append(jnp.concatenate([part, blank] if left else [blank, part], axis=1))
    return jnp.concatenate(stacked, axis=0)


def attend_kernel(prompt, q_ref, a_ref, b_ref, kpos_ref, live_ref, qpos_ref, p_ref, o_ref, s_scr, bias_scr):
    rows = q_ref.shape[1]
    half = a_ref.shape[0]

    @pl.when(pl.program_id(0) == 0)
    def _():
        kpos = kpos_ref[...]
        klive = live_ref[...] > 0
        kseg = jnp.where(kpos < prompt, 0, 1 + ((kpos - prompt) >> CONT_BITS))

        def fill(i, carry):
            at = pl.ds(pl.multiple_of(i * 8, 8), 8)
            qpos = qpos_ref[at, :]
            qseg = jnp.where(qpos < prompt, 0, 1 + ((qpos - prompt) >> CONT_BITS))
            earlier = kpos <= qpos
            shared = (kseg == 0) | (kseg == qseg)
            seen = earlier & shared & (klive | (kpos == qpos))
            bias_scr[at, :] = jnp.where(seen, 0.0, MASK_FLOOR)
            return carry

        lax.fori_loop(0, rows // 8, fill, 0)

    stacked = padded_heads(q_ref[0], True)
    s_scr[:, :half] = mm(stacked, a_ref[...], NT)
    s_scr[:, half:] = mm(stacked, b_ref[...], NT)
    steps = rows // 16

    def soften(i, carry):
        at = pl.ds(pl.multiple_of(i * 16, 16), 16)
        bias_at = pl.ds(pl.multiple_of(lax.rem(i, steps) * 16, 16), 16)
        scores = s_scr[at, :] + bias_scr[bias_at, :]
        top = jnp.max(scores, axis=-1, keepdims=True)
        weights = jnp.exp(scores - top)
        mass = jnp.sum(weights, axis=-1, keepdims=True)
        p_ref[0, at, :] = (weights * (1.0 / mass)).astype(BF)
        return carry

    lax.fori_loop(0, SHARE * steps, soften, 0)
    mixed = mm(p_ref[0, :, :half], a_ref[...]) + mm(p_ref[0, :, half:], b_ref[...])
    o_ref[0] = jnp.concatenate(
        [mixed[j * rows : (j + 1) * rows, HEAD_SIZE:] for j in range(SHARE)], axis=1
    ).astype(BF)


def attend_call(query, part_a, part_b, kpos, klive, qpos, prompt):
    heads, rows, wide = query.shape
    half = part_a.shape[0]
    keys = 2 * half
    return pl.pallas_call(
        functools.partial(attend_kernel, prompt),
        name="attend",
        grid=(heads,),
        out_shape=(shaped((heads, SHARE * rows, keys), BF), shaped((heads, rows, wide), BF)),
        in_specs=[
            pl.BlockSpec((1, rows, wide), lambda h: (h, 0, 0)),
            pl.BlockSpec((half, 128), lambda h: (0, h)),
            pl.BlockSpec((half, 128), lambda h: (0, h)),
            pl.BlockSpec((1, keys), lambda h: (0, 0)),
            pl.BlockSpec((1, keys), lambda h: (0, 0)),
            pl.BlockSpec((rows, 1), lambda h: (0, 0)),
        ],
        out_specs=(
            pl.BlockSpec((1, SHARE * rows, keys), lambda h: (h, 0, 0)),
            pl.BlockSpec((1, rows, wide), lambda h: (h, 0, 0)),
        ),
        scratch_shapes=[pltpu.VMEM((SHARE * rows, keys), F32), pltpu.VMEM((rows, keys), F32)],
        compiler_params=params(dimension_semantics=("arbitrary",)),
        cost_estimate=estimate(8 * heads * SHARE * rows * keys * 128, heads * SHARE * rows * keys * 2),
    )(query, part_a, part_b, kpos, klive, qpos)


def attend_back_kernel(q_ref, do_ref, a_ref, b_ref, p_ref, dq_ref, da_ref, db_ref, dp_scr, ds_scr):
    rows = q_ref.shape[1]
    half = a_ref.shape[0]
    stacked = padded_heads(q_ref[0], True)
    grads = padded_heads(do_ref[0], False)
    dp_scr[:, :half] = mm(grads, a_ref[...], NT)
    dp_scr[:, half:] = mm(grads, b_ref[...], NT)

    def soften(i, carry):
        at = pl.ds(pl.multiple_of(i * 16, 16), 16)
        weights = p_ref[0, at, :].astype(F32)
        dp = dp_scr[at, :]
        delta = jnp.sum(weights * dp, axis=-1, keepdims=True)
        ds_scr[at, :] = (weights * (dp - delta)).astype(BF)
        return carry

    lax.fori_loop(0, SHARE * rows // 16, soften, 0)
    dq = (mm(ds_scr[:, :half], a_ref[...]) + mm(ds_scr[:, half:], b_ref[...])) * SCALE
    dq_ref[0] = jnp.concatenate(
        [dq[j * rows : (j + 1) * rows, :HEAD_SIZE] for j in range(SHARE)], axis=1
    )
    for at, out in ((slice(0, half), da_ref), (slice(half, 2 * half), db_ref)):
        turned = mm(stacked, ds_scr[:, at], TN) + mm(grads, p_ref[0, :, at], TN)
        out[...] = turned.T.astype(out.dtype)


def attend_back_call(query, d_out, part_a, part_b, weights):
    heads, rows, wide = query.shape
    half = part_a.shape[0]
    keys = 2 * half
    return pl.pallas_call(
        attend_back_kernel,
        name="attend_back",
        grid=(heads,),
        out_shape=(
            shaped((heads, rows, wide), F32),
            shaped((half, heads * 128), F32),
            shaped((half, heads * 128), BF),
        ),
        in_specs=[
            pl.BlockSpec((1, rows, wide), lambda h: (h, 0, 0)),
            pl.BlockSpec((1, rows, wide), lambda h: (h, 0, 0)),
            pl.BlockSpec((half, 128), lambda h: (0, h)),
            pl.BlockSpec((half, 128), lambda h: (0, h)),
            pl.BlockSpec((1, SHARE * rows, keys), lambda h: (h, 0, 0)),
        ],
        out_specs=(
            pl.BlockSpec((1, rows, wide), lambda h: (h, 0, 0)),
            pl.BlockSpec((half, 128), lambda h: (0, h)),
            pl.BlockSpec((half, 128), lambda h: (0, h)),
        ),
        scratch_shapes=[
            pltpu.VMEM((SHARE * rows, keys), F32),
            pltpu.VMEM((SHARE * rows, keys), BF),
        ],
        compiler_params=params(dimension_semantics=("arbitrary",)),
        cost_estimate=estimate(16 * heads * SHARE * rows * keys * 128, heads * SHARE * rows * keys * 2),
    )(query, d_out, part_a, part_b, weights)


def picks(sel_ref, total_rows):
    capacity = sel_ref.shape[1]
    row = lax.broadcasted_iota(jnp.int32, (total_rows, capacity), 0)
    return row == sel_ref[...]


def live_column(live_ref, rows):
    count = jnp.sum(live_ref[:, :].astype(F32), axis=1, keepdims=True)
    return lax.broadcasted_iota(jnp.int32, (rows, 1), 0).astype(F32) < count


def feed_forward(x, ao_ref, gain_two, wo, wg, wu, wd, waits, ao_out, mid_ref, second_ref, g_ref, u_ref, hid_ref, y_scr):
    rows = x.shape[0]
    mixed = jnp.concatenate([ao_ref[h] for h in range(KEY_VALUE_HEADS)], axis=1)
    ao_out[...] = mixed
    wait_all(waits[0])
    middle = x + mm(mixed, wo[...])
    mid_ref[...] = middle
    normed, _ = normed_rows(middle)
    second_ref[...] = (normed * gain_two).astype(BF)
    y_scr[...] = middle
    for mine in waits[1:]:
        wait_all(mine)

    def chunk(j, carry):
        at = pl.ds(pl.multiple_of(j * FF_CHUNK, FF_CHUNK), FF_CHUNK)
        second = second_ref[...]
        g = mm(second, wg[:, at])
        u = mm(second, wu[:, at])
        g_ref[:, at] = g
        u_ref[:, at] = u
        hidden = (g / (1.0 + jnp.exp(-g)) * u).astype(BF)
        hid_ref[:, at] = hidden
        y_scr[...] += mm(hidden, wd[at, :])
        return carry

    lax.fori_loop(0, wg.shape[1] // FF_CHUNK, chunk, 0)


def dense_kernel(step, weights, n_pieces, *args):
    args = list(args)
    take = lambda k: [args.pop(0) for _ in range(k)]
    coords_ref, x_ref, ao_ref, gain1_ref, gain2_ref = take(5)
    if step == 0:
        sel_ref, cos_ref, sin_ref = take(3)
    elif step == 1:
        live_ref, cos_ref, sin_ref = take(3)
    else:
        sel_ref, live2_ref, live_ref, h1_ref, h2_ref = take(5)
    refs = take(n_pieces)
    ao_out, mid_ref, second_ref, g_ref, u_ref, hid_ref = take(6)
    if step < 2:
        h_ref, next_ref, first_ref, q_ref, kv_ref = take(5)
    else:
        (out_ref,) = take(1)
    buffers = take(len(weights))
    y_scr, sems = take(2)
    waits = start_weights(weights, refs, buffers, sems, read_coords(coords_ref))
    rows = x_ref.shape[0]
    x = x_ref[...].astype(F32)
    wo, wg, wu, wd = buffers[:4]
    feed_forward(
        x, ao_ref, gain2_ref[...], wo, wg, wu, wd, waits[:4], ao_out, mid_ref, second_ref,
        g_ref, u_ref, hid_ref, y_scr,
    )
    for mine in waits[4:]:
        wait_all(mine)
    updated = y_scr[...]
    if step == 0:
        h_ref[...] = updated
        chosen = picks(sel_ref, rows).astype(F32)
        following = mm(chosen, updated, TN, lax.Precision.HIGHEST)
    else:
        updated = jnp.where(live_column(live_ref, rows), updated, x)
    if step == 1:
        h_ref[...] = updated
        following = updated[: next_ref.shape[0]]
    if step < 2:
        next_ref[...] = following
        project(
            following, gain1_ref[...], *buffers[4:], cos_ref[...], sin_ref[...],
            first_ref, q_ref, kv_ref,
        )
    else:
        slots = jnp.concatenate([updated, h2_ref[rows:, :]], axis=0).astype(BF)
        hit = picks(sel_ref, h1_ref.shape[0]) & (live2_ref[...] > 0)
        placed = mm(hit.astype(BF), slots)
        any_hit = jnp.sum(hit.astype(F32), axis=1, keepdims=True) > 0.5
        out_ref[...] = jnp.where(any_hit, placed, h1_ref[...]).astype(BF)


def dense_call(step, coords, x, mixed, gain1, gain2, extra, weights, next_rows):
    rows, width = x.shape
    hidden = weights[1].shape[1]
    arrays = pieces_of(weights)
    outs = [
        shaped((rows, width), BF),
        shaped((rows, width), F32),
        shaped((rows, width), BF),
        shaped((rows, hidden), F32),
        shaped((rows, hidden), F32),
        shaped((rows, hidden), BF),
    ]
    if step < 2:
        kv_width = weights[5].shape[1]
        outs += [
            shaped((rows, width), F32),
            shaped((next_rows, width), F32),
            shaped((next_rows, width), BF),
            shaped((KEY_VALUE_HEADS, next_rows, SHARE * HEAD_SIZE), BF),
            shaped((next_rows, 2 * kv_width), BF),
        ]
    else:
        outs += [shaped((next_rows, width), BF)]
    return pl.pallas_call(
        functools.partial(dense_kernel, step, weights, len(arrays)),
        name=f"dense_{step}",
        out_shape=tuple(outs),
        in_specs=[sm()] + [vm()] * (4 + len(extra)) + [hbm()] * len(arrays),
        out_specs=tuple(vm() for _ in outs),
        scratch_shapes=weight_scratch(weights)
        + [pltpu.VMEM((rows, width), F32), pltpu.SemaphoreType.DMA((len(arrays),))],
        compiler_params=params(),
        cost_estimate=estimate(2 * rows * 9.83e6, 2.4e7),
    )(coords, x, mixed, gain1, gain2, *extra, *arrays)


def feed_back(d_y, mid_ref, g_ref, u_ref, gain_two, wd, wg, wu, wo, waits, dyb_ref, dg_ref, du_ref, dmid_ref, dz_ref, dao_ref, sum_ref, acc_scr):
    dyb_ref[...] = d_y.astype(BF)
    acc_scr[...] = jnp.zeros_like(acc_scr)
    for mine in waits[:3]:
        wait_all(mine)

    def chunk(j, carry):
        at = pl.ds(pl.multiple_of(j * FF_CHUNK, FF_CHUNK), FF_CHUNK)
        d_hidden = mm(dyb_ref[...], wd[at, :], NT)
        g, u = g_ref[:, at], u_ref[:, at]
        sigma = 1.0 / (1.0 + jnp.exp(-g))
        d_gate = (d_hidden * u * sigma * (1.0 + g * (1.0 - sigma))).astype(BF)
        d_up = (d_hidden * (g * sigma)).astype(BF)
        dg_ref[:, at] = d_gate
        du_ref[:, at] = d_up
        acc_scr[...] += mm(d_gate, wg[:, at], NT) + mm(d_up, wu[:, at], NT)
        return carry

    lax.fori_loop(0, wg.shape[1] // FF_CHUNK, chunk, 0)
    d_second = acc_scr[...]
    normed, inverse = normed_rows(mid_ref[...])
    sum_ref[...] = jnp.sum(d_second * normed, axis=0, keepdims=True)
    d_mid = norm_back(d_second, normed, inverse, gain_two) + d_y
    dmid_ref[...] = d_mid
    d_low = d_mid.astype(BF)
    dz_ref[...] = d_low
    wait_all(waits[3])
    d_mixed = mm(d_low, wo[...], NT).astype(BF)
    wide = SHARE * HEAD_SIZE
    for h in range(KEY_VALUE_HEADS):
        dao_ref[h] = d_mixed[:, h * wide : (h + 1) * wide]


def project_back(own_ref, others, dq_ref, x, dmid_ref, gain_one, cosine, sine, wq, wk, wv, waits, dql_ref, dkl_ref, dvl_ref, sum_ref):
    total = own_ref[...].astype(F32)
    for other in others:
        total = total + other[...].astype(F32)
    d_key = jnp.concatenate(
        [total[:, h * 128 : h * 128 + HEAD_SIZE] for h in range(KEY_VALUE_HEADS)], axis=1
    )
    d_value = jnp.concatenate(
        [total[:, h * 128 + HEAD_SIZE : (h + 1) * 128] for h in range(KEY_VALUE_HEADS)], axis=1
    )
    d_query = jnp.concatenate([dq_ref[h] for h in range(KEY_VALUE_HEADS)], axis=1)
    dql_ref[...] = turn(d_query, cosine, sine, True).astype(BF)
    dkl_ref[...] = turn(d_key, cosine, sine, True).astype(BF)
    dvl_ref[...] = d_value.astype(BF)
    for mine in waits:
        wait_all(mine)
    d_first = (
        mm(dql_ref[...], wq[...], NT)
        + mm(dkl_ref[...], wk[...], NT)
        + mm(dvl_ref[...], wv[...], NT)
    )
    normed, inverse = normed_rows(x)
    sum_ref[...] = jnp.sum(d_first * normed, axis=0, keepdims=True)
    return norm_back(d_first, normed, inverse, gain_one) + dmid_ref[...]


def back_kernel(phase, weights, n_pieces, n_parts, *args):
    args = list(args)
    take = lambda k: [args.pop(0) for _ in range(k)]
    (coords_ref,) = take(1)
    if phase > 0:
        gain1_ref, cos_ref, sin_ref, x_ref, dmid_in, dq_ref = take(6)
        own_ref, *others = take(n_parts)
    if phase < 3:
        gain2_ref, mid_ref, g_ref, u_ref = take(4)
    if phase == 0:
        cot_ref, sel_ref, live3_ref = take(3)
    elif phase == 1:
        slots_ref, live3_ref, live2_ref = take(3)
    elif phase == 2:
        cot_ref, sel_ref, live2_ref = take(3)
    refs = take(n_pieces)
    if phase > 0:
        dql_ref, dkl_ref, dvl_ref, sum1_ref = take(4)
    if phase < 3:
        dyb_ref, dg_ref, du_ref, dmid_ref, dz_ref, dao_ref, sum2_ref = take(7)
    if phase == 0:
        (slots_out,) = take(1)
    elif phase == 3:
        (grad_ref,) = take(1)
    buffers = take(len(weights))
    if phase < 3:
        (acc_scr,) = take(1)
    (sems,) = take(1)
    waits = start_weights(weights, refs, buffers, sems, read_coords(coords_ref))
    at = 0
    if phase > 0:
        d_x = project_back(
            own_ref, others, dq_ref, x_ref[...].astype(F32), dmid_in, gain1_ref[...],
            cos_ref[...], sin_ref[...], *buffers[:3], waits[:3], dql_ref, dkl_ref, dvl_ref, sum1_ref,
        )
        at = 3
    if phase == 0:
        chosen = picks(sel_ref, cot_ref.shape[0]).astype(BF)
        slots = mm(chosen, cot_ref[...], TN)
        slots_out[...] = slots
        rows = mid_ref.shape[0]
        d_y = jnp.where(live_column(live3_ref, rows), slots[:rows], 0.0)
    elif phase == 1:
        rows = x_ref.shape[0]
        slots = slots_ref[...]
        head = jnp.where(live_column(live3_ref, rows), d_x, slots[:rows])
        slots = jnp.concatenate([head, slots[rows:]], axis=0)
        d_y = jnp.where(live_column(live2_ref, slots.shape[0]), slots, 0.0)
    elif phase == 2:
        hit = picks(sel_ref, cot_ref.shape[0]) & (live2_ref[...] > 0)
        placed = mm(hit.astype(F32), d_x, NN, lax.Precision.HIGHEST)
        any_hit = jnp.sum(hit.astype(F32), axis=1, keepdims=True) > 0.5
        d_y = jnp.where(any_hit, placed, cot_ref[...].astype(F32))
    else:
        grad_ref[...] = d_x
        return
    feed_back(
        d_y, mid_ref, g_ref, u_ref, gain2_ref[...], *buffers[at : at + 4], waits[at : at + 4],
        dyb_ref, dg_ref, du_ref, dmid_ref, dz_ref, dao_ref, sum2_ref, acc_scr,
    )


def back_call(phase, coords, before, parts, after, extra, weights, rows_next):
    arrays = pieces_of(weights)
    ins = list(before) + list(parts) + list(after) + list(extra)
    outs, scratch = [], weight_scratch(weights)
    if phase > 0:
        rows, width = before[3].shape
        kv_width = weights[1].shape[1]
        outs += [
            shaped((rows, width), BF),
            shaped((rows, kv_width), BF),
            shaped((rows, kv_width), BF),
            shaped((1, width), F32),
        ]
    if phase < 3:
        rows, hidden = after[2].shape
        width = after[1].shape[1]
        outs += [
            shaped((rows, width), BF),
            shaped((rows, hidden), BF),
            shaped((rows, hidden), BF),
            shaped((rows, width), F32),
            shaped((rows, width), BF),
            shaped((KEY_VALUE_HEADS, rows, SHARE * HEAD_SIZE), BF),
            shaped((1, width), F32),
        ]
        scratch += [pltpu.VMEM((rows, width), F32)]
    if phase == 0:
        outs += [shaped((rows_next, width), F32)]
    elif phase == 3:
        outs += [shaped((rows, width), F32)]
    return pl.pallas_call(
        functools.partial(back_kernel, phase, weights, len(arrays), len(parts)),
        name=f"back_{phase}",
        out_shape=tuple(outs),
        in_specs=[sm()] + [vm()] * len(ins) + [hbm()] * len(arrays),
        out_specs=tuple(vm() for _ in outs),
        scratch_shapes=scratch + [pltpu.SemaphoreType.DMA((len(arrays),))],
        compiler_params=params(),
        cost_estimate=estimate(2 * rows * 9.83e6, 2.4e7),
    )(coords, *ins, *arrays)


def stack_rows(refs, scratch):
    at = 0
    for ref in refs:
        scratch[at : at + ref.shape[0], :] = ref[...]
        at += ref.shape[0]


def put_blocks(value, x_of, coords, ref, per_row):
    y, _, x, z = coords
    depth = ref.shape[-2]
    for ya in range(2):
        for xa in range(2) if per_row else (None,):
            for za in range(4):
                row = (ya * (2 if per_row else 1) + (xa or 0)) * 4 + za
                ref[y ^ ya, (x ^ xa) if per_row else x_of, z ^ za] = value[
                    row * depth : (row + 1) * depth
                ].astype(BF)


def grad_cols_kernel(n_steps, coords_ref, *args):
    left, args = args[:n_steps], args[n_steps:]
    right, args = args[:n_steps], args[n_steps:]
    keep_ref, send_ref, l_scr, r_scr = args
    coords = read_coords(coords_ref)
    _, c, x, _ = coords
    stack_rows(left, l_scr)
    stack_rows(right, r_scr)
    block = keep_ref.shape[-1]
    for far, ref in ((1, send_ref), (0, keep_ref)):

        def body(rx, carry, far=far, ref=ref):
            start = pl.multiple_of(((c ^ far) * 2 + (x ^ rx)) * block, 128)
            value = mm(l_scr[...], r_scr[:, pl.ds(start, block)], TN)
            put_blocks(value, rx, coords, ref, False)
            return carry

        lax.fori_loop(0, 2, body, 0)


def grad_rows_kernel(n_steps, coords_ref, *args):
    left, args = args[:n_steps], args[n_steps:]
    right, args = args[:n_steps], args[n_steps:]
    keep_ref, send_ref, l_scr, r_scr = args
    coords = read_coords(coords_ref)
    y, c, x, z = coords
    stack_rows(left, l_scr)
    stack_rows(right, r_scr)
    depth = keep_ref.shape[-2]
    span = 8 * depth
    for far, ref in ((1, send_ref), (0, keep_ref)):

        def body(ry, carry, far=far, ref=ref):
            start = pl.multiple_of(((y ^ ry) * 2 + (c ^ far)) * span, 128)
            value = mm(l_scr[:, pl.ds(start, span)], r_scr[...], TN)
            for xa in range(2):
                for za in range(4):
                    row = (xa * 4 + za) * depth
                    ref[ry, x ^ xa, z ^ za] = value[row : row + depth].astype(BF)
            return carry

        lax.fori_loop(0, 2, body, 0)


def grad_mixed_kernel(n_steps, coords_ref, *args):
    groups = []
    for _ in range(6):
        groups.append(args[:n_steps])
        args = args[n_steps:]
    first, mixed, dq, dk, dv, dz = groups
    keep_ref, send_ref, first_scr, mixed_scr, q_scr, k_scr, v_scr, z_scr, val_scr = args
    coords = read_coords(coords_ref)
    _, c, x, _ = coords
    for refs, scr in zip(groups, (first_scr, mixed_scr, q_scr, k_scr, v_scr, z_scr), strict=True):
        stack_rows(refs, scr)
    block = keep_ref.shape[-1]
    edge = q_scr.shape[1] - block
    for ca in range(2):
        for xa in range(2):
            wide, left = (q_scr, first_scr) if ca == 0 else (z_scr, mixed_scr)
            thin = k_scr if ca == 0 else v_scr
            if xa == 0:
                val_scr[...] = mm(left[...], wide[:, :block], TN)
            else:
                val_scr[...] = jnp.concatenate(
                    [mm(left[...], wide[:, block:], TN), mm(first_scr[...], thin[...], TN)], axis=1
                )

            @pl.when(c == ca)
            def _(xa=xa):
                put_blocks(val_scr[...], x ^ xa, coords, keep_ref, False)

            @pl.when(c != ca)
            def _(xa=xa):
                put_blocks(val_scr[...], x ^ xa, coords, send_ref, False)


def grad_call(kind, coords, groups):
    n_steps = len(groups[0])
    rows = sum(a.shape[0] for a in groups[0])
    width, cols = groups[0][0].shape[1], groups[1][0].shape[1]
    scratch = [pltpu.VMEM((rows, g[0].shape[1]), BF) for g in groups]
    if kind == "rows":
        kernel, block = grad_rows_kernel, (width // 32, cols)
    elif kind == "cols":
        kernel, block = grad_cols_kernel, (width // 8, cols // 4)
    else:
        total = sum(g[0].shape[1] for g in groups[2:])
        kernel, block = grad_mixed_kernel, (width // 8, total // 4)
        scratch += [pltpu.VMEM((width, block[1]), F32)]
    out = shaped((2, 2, 4) + block, BF)
    ins = [a for g in groups for a in g]
    return pl.pallas_call(
        functools.partial(kernel, n_steps),
        name=f"grad_{kind}",
        out_shape=(out, out),
        in_specs=[sm()] + [vm()] * len(ins),
        out_specs=(vm(), vm()),
        scratch_shapes=scratch,
        compiler_params=params(),
        cost_estimate=estimate(2 * rows * 16 * 2 * block[0] * block[1], 1e7),
    )(coords, *ins)


def place_cols_kernel(coords_ref, near_ref, far_ref, *outs):
    _, c, x, z = read_coords(coords_ref)
    depth, block = near_ref.shape[-2:]
    target = outs[-1] if len(outs) > 1 else outs[0]
    for far, ref in ((0, near_ref), (1, far_ref)):
        for rx in range(2):
            cols = pl.ds(pl.multiple_of(((c ^ far) * 2 + (x ^ rx)) * block, 128), block)
            for rz in range(4):
                rows = pl.ds(pl.multiple_of((z ^ rz) * depth, 8), depth)
                target[rows, cols] = ref[rx, rz].astype(F32)
    if len(outs) > 1:
        at = 0
        for out in outs[:-1]:
            out[...] = target[:, at : at + out.shape[1]]
            at += out.shape[1]


def place_rows_kernel(coords_ref, near_ref, far_ref, out_ref):
    _, c, x, z = read_coords(coords_ref)
    depth = near_ref.shape[-2]
    for far, ref in ((0, near_ref), (1, far_ref)):
        for rx in range(2):
            for rz in range(4):
                row = (((c ^ far) * 2 + (x ^ rx)) * 4 + (z ^ rz)) * depth
                out_ref[pl.ds(pl.multiple_of(row, 8), depth), :] = ref[rx, rz].astype(F32)


def place_call(kind, coords, near, far, widths):
    depth, block = near.shape[-2:]
    scratch = []
    if kind == "rows":
        kernel, outs = place_rows_kernel, (shaped((16 * depth, block), F32),)
    else:
        kernel = place_cols_kernel
        outs = tuple(shaped((4 * depth, w), F32) for w in widths)
        if len(outs) > 1:
            scratch = [pltpu.VMEM((4 * depth, 4 * block), F32)]
    return pl.pallas_call(
        kernel,
        name=f"place_{kind}",
        out_shape=outs,
        in_specs=[sm(), vm(), vm()],
        out_specs=tuple(vm() for _ in outs),
        scratch_shapes=scratch,
        compiler_params=params(),
        cost_estimate=estimate(0, 1e7),
    )(coords, near, far)


def low_sum(left, right):
    return (left.astype(F32) + right.astype(F32)).astype(BF)


def gather_keys(kv, near):
    if not near:
        whole = lax.all_gather(kv, "ctx", axis=0, tiled=True)
        half = whole.shape[0] // 2
        return whole[:half], whole[half:]
    by_x, by_y, by_z = hop(kv, X_BIT), hop(kv, Y_BIT), hop(kv, Z1_BIT)
    across = hop(kv, X_BIT | Y_BIT | Z1_BIT)
    pieces = [kv, by_x, by_y, by_z, across, hop(by_x, Y_BIT), hop(by_y, Z1_BIT), hop(by_z, X_BIT)]
    part = jnp.concatenate(pieces, axis=0)
    return part, hop(part, C_BIT)


def scatter_keys(part_a, part_b, near):
    if not near:
        whole = jnp.concatenate([part_a, part_b.astype(F32)], axis=0)
        return [lax.psum_scatter(whole, "ctx", scatter_dimension=0, tiled=True)]
    total = part_a + hop(part_b, C_BIT).astype(F32)
    rows = total.shape[0] // len(NEAR)
    parts = [total[:rows]]
    low = total[rows:].astype(BF)
    for i, mask in enumerate(NEAR[1:]):
        parts.append(hop(low[i * rows : (i + 1) * rows], mask))
    return parts


def quarter(value, axis, index):
    size = value.shape[axis] // 4
    return lax.dynamic_slice_in_dim(value, index * size, size, axis)


def half_rows(value, index):
    size = value.shape[0] // 2
    return lax.dynamic_slice_in_dim(value, index * size, size, 0)


def whole_weight(own, near, coords, spread):
    rows, cols = own.shape
    shape = (2 * rows, cols)
    if not near:
        return Weight(shape, [lax.all_gather(own, "ws", axis=0, tiled=True)], [lambda k: (0, 0)])
    y, c, x, z = coords
    arrays, offsets = [own], [lambda k: (k[0] * rows, 0)]
    cut = own
    if spread is not None:
        cut = quarter(own, 1 if spread == "cols" else 0, x * 2 + (z & 1))
    mine = hop(half_rows(cut, c), Y_BIT)
    shared = [(mine, 0, 0)]
    if spread is not None:
        shared += [
            (hop(mine, X_BIT), 1, 0),
            (hop(mine, Z1_BIT), 0, 1),
            (hop(mine, X_BIT | Z1_BIT), 1, 1),
        ]
    depth, wide = mine.shape
    for far in (0, 1):
        for value, rx, rz in shared:
            arrays.append(hop(value, C_BIT) if far else value)

            def offset(k, far=far, rx=rx, rz=rz):
                ky, kc, kx, kz = k
                part = (kx ^ rx) * 2 + ((kz & 1) ^ rz)
                row = (1 - ky) * rows + (kc ^ far) * depth
                if spread == "cols":
                    return row, part * wide
                if spread == "rows":
                    return row + part * 2 * depth, 0
                return row, 0

            offsets.append(offset)
    return Weight(shape, arrays, offsets)


def reduce_blocks(keep, send, near, coords):
    if not near:
        both = lax.psum(jnp.stack([keep, send]).astype(F32), AXES)
        mine = lax.dynamic_index_in_dim(both, coords[0], 1, keepdims=False)
        return mine[0], mine[1]
    total = low_sum(keep, hop(send, C_BIT))
    total = low_sum(total[0], hop(total[1], Y_BIT))
    total = low_sum(total[0], hop(total[1], X_BIT))
    total = low_sum(total[:2], hop(total[2:], Z2_BIT))
    total = low_sum(total[0], hop(total[1], Z1_BIT))
    total = jnp.stack([total, hop(total, Z1_BIT)])
    total = jnp.concatenate([total, hop(total, Z2_BIT)])
    total = jnp.stack([total, hop(total, X_BIT)])
    return total, hop(total, C_BIT)


def sum_everywhere(value, near):
    if not near:
        return lax.psum(value, AXES)
    for mask in (C_BIT, X_BIT, Y_BIT, Z1_BIT, Z2_BIT):
        value = value + hop(value, mask)
    return value


def on_device(
    tokens, cotangent, w_query, key_weight, value_weight, w_out, w_gate, w_up, w_down,
    gain_attn, gain_ffn, block_order, sel_mid, live_mid, sel_last, live_last,
):
    ctx_count, ws_count = lax.axis_size("ctx"), lax.axis_size("ws")
    near = ctx_count == 16 and ws_count == 2
    ctx, y = lax.axis_index("ctx"), lax.axis_index("ws")
    tok_local = tokens.shape[1]
    cap_mid, cap_last = sel_mid.shape[1] // ctx_count, sel_last.shape[1] // ctx_count
    if near:
        c, x, z = ctx & 1, (ctx >> 1) & 1, ctx >> 2
        places = (y, c, x, z)
        here = (ctx & 7) | (y << 3)
        order = here ^ jnp.array([ctx_mask(m) for m in NEAR] + [ctx_mask(m) | 1 for m in NEAR], jnp.int32)
        relocate = move
    else:
        zero = jnp.int32(0)
        places = (y, zero, zero, zero)
        here = ctx
        order = jnp.arange(ctx_count, dtype=jnp.int32)
        relocate = lambda v: v
    own_first = near
    coords = jnp.stack([jnp.asarray(v, jnp.int32) for v in places])
    block_coords = coords if near else jnp.zeros((4,), jnp.int32)

    tok = relocate(tokens[0])
    plan = relocate(
        jnp.concatenate(
            [
                sel_mid.reshape(ctx_count, cap_mid),
                live_mid.reshape(ctx_count, cap_mid),
                live_last.reshape(ctx_count, cap_last),
            ],
            axis=1,
        )
    )
    weight_q = whole_weight(w_query, near, places, None)
    weight_k = whole_weight(key_weight, near, places, None)
    weight_v = whole_weight(value_weight, near, places, None)
    gains = jnp.concatenate([gain_attn.reshape(1, -1), gain_ffn.reshape(1, -1)], axis=0)
    if near:
        other = hop(gains, Y_BIT)
        gains = jnp.where(
            y == 0,
            jnp.concatenate([gains, other], axis=1),
            jnp.concatenate([other, gains], axis=1),
        )
    else:
        gains = lax.all_gather(gains, "ws", axis=1, tiled=True)
    gains = gains.astype(F32)
    gain1, gain2 = gains[0:1], gains[1:2]
    weight_g = whole_weight(w_gate, near, places, "cols")
    weight_u = whole_weight(w_up, near, places, "cols")
    weight_d = whole_weight(w_down, near, places, "rows")
    weight_o = whole_weight(w_out, near, places, None)
    cot = relocate(cotangent[0])

    per_device = tok_local // BLK
    blocks = jnp.take(block_order.reshape(ctx_count, per_device), order, axis=0)
    plan_order = jnp.take(plan, order, axis=0)
    sel_all = plan_order[:, :cap_mid]
    live_two = plan_order[:, cap_mid : 2 * cap_mid]
    live_three = plan_order[:, 2 * cap_mid :]
    place_one = (blocks[:, :, None] * BLK + jnp.arange(BLK, dtype=jnp.int32)).reshape(ctx_count, tok_local)
    place_two = sum(
        jnp.where(sel_all // BLK == k, blocks[:, k : k + 1], 0) for k in range(per_device)
    ) * BLK + sel_all % BLK
    place_three = place_two[:, :cap_last]
    if own_first:
        mine = lambda v: v[0:1]
    else:
        mine = lambda v: lax.dynamic_slice_in_dim(v, here, 1, 0)
    sel_own, live2_own, live3_own = mine(sel_all), mine(live_two), mine(live_three)
    own_places = jnp.concatenate([mine(place_one), mine(place_two)], axis=1).reshape(-1, 1)
    frequency = ROPE_BASE ** (-jnp.arange(HEAD_SIZE // 2, dtype=F32) / (HEAD_SIZE // 2))
    angles = own_places.astype(F32) * frequency[None, :]
    cosine, sine = jnp.cos(angles), jnp.sin(angles)
    cosine = jnp.concatenate([cosine] * 4, axis=1)
    sine = jnp.concatenate([-sine, sine, -sine, sine], axis=1)
    tables = [
        (cosine[:tok_local], sine[:tok_local]),
        (cosine[tok_local:], sine[tok_local:]),
        (cosine[tok_local : tok_local + cap_last], sine[tok_local : tok_local + cap_last]),
    ]
    query_places = [
        own_places[:tok_local],
        own_places[tok_local:],
        own_places[tok_local : tok_local + cap_last],
    ]
    key_places = [v.reshape(1, -1) for v in (place_one, place_two, place_three)]
    key_live = [
        jnp.ones((1, ctx_count * tok_local), jnp.int32),
        live_two.reshape(1, -1),
        live_three.reshape(1, -1),
    ]
    prompt = ctx_count * tok_local // 2

    dense_weights = (weight_o, weight_g, weight_u, weight_d)
    proj_weights = (weight_q, weight_k, weight_v)
    back_weights = (weight_d, weight_g, weight_u, weight_o)

    firsts, mixeds, seconds, hiddens = [], [], [], []
    records = []
    xs = [tok]
    first_in, query, kv = first_call(coords, tok, gain1, *tables[0], proj_weights)
    heights = []
    for step in range(3):
        part_a, part_b = gather_keys(kv, near)
        weights, mixed = attend_call(
            query, part_a, part_b, key_places[step], key_live[step], query_places[step], prompt
        )
        firsts.append(first_in)
        if step == 0:
            extra = (sel_own, *tables[1])
        elif step == 1:
            extra = (live2_own, *tables[2])
        else:
            extra = (sel_own, live2_own, live3_own, heights[0], heights[1])
        result = dense_call(
            step, coords, xs[step], mixed, gain1, gain2, extra,
            dense_weights + (proj_weights if step < 2 else ()),
            (cap_mid, cap_last, tok_local)[step],
        )
        mixed_rows, middle, second, gate, up, hidden = result[:6]
        mixeds.append(mixed_rows)
        seconds.append(second)
        hiddens.append(hidden)
        records.append((query, part_a, part_b, weights, middle, gate, up))
        if step < 2:
            height, following, first_in, query, kv = result[6:]
            heights.append(height)
            xs.append(following)
        else:
            output = relocate(result[6])

    d_firsts, d_seconds = [None] * 3, [None] * 3
    sums_one, sums_two = [], []
    slots = None
    parts, d_query, d_middle = (), None, None
    for phase in range(4):
        step = 2 - phase
        before, after = (), ()
        if phase > 0:
            before = (gain1, *tables[step + 1], xs[step + 1], d_middle, d_query)
        if phase < 3:
            after = (gain2, *records[step][4:7])
        if phase == 0:
            extra, weights = (cot, sel_own, live3_own), back_weights
        elif phase == 1:
            extra, weights = (slots, live3_own, live2_own), proj_weights + back_weights
        elif phase == 2:
            extra, weights = (cot, sel_own, live2_own), proj_weights + back_weights
        else:
            extra, weights = (), proj_weights
        result = list(back_call(phase, coords, before, parts, after, extra, weights, cap_mid))
        if phase > 0:
            *d_firsts[step + 1], total = result[:4]
            sums_one.append(total)
            result = result[4:]
        if phase < 3:
            d_low, d_gate, d_up, d_middle, d_mid_low, d_mixed, total = result[:7]
            d_seconds[step] = (d_low, d_gate, d_up, d_mid_low)
            sums_two.append(total)
            if phase == 0:
                slots = result[7]
            query, part_a, part_b, weights = records[step][:4]
            d_query, term_a, term_b = attend_back_call(query, d_mixed, part_a, part_b, weights)
            parts = scatter_keys(term_a, term_b, near)
        else:
            grad_tokens = relocate(result[0])

    column = lambda rows, i: [r[i] for r in rows]
    width = tok.shape[1]
    kv_width = key_weight.shape[1]
    hidden_width = w_gate.shape[1]
    half = width // 2
    down = grad_call("rows", block_coords, [hiddens, column(d_seconds, 0)])
    gate = grad_call("cols", block_coords, [seconds, column(d_seconds, 1)])
    up = grad_call("cols", block_coords, [seconds, column(d_seconds, 2)])
    rest = grad_call(
        "mixed", block_coords,
        [firsts, mixeds, column(d_firsts, 0), column(d_firsts, 1), column(d_firsts, 2), column(d_seconds, 3)],
    )
    grad_down = place_call("rows", block_coords, *reduce_blocks(*down, near, places), None)[0]
    grad_gate = place_call("cols", block_coords, *reduce_blocks(*gate, near, places), (hidden_width,))[0]
    grad_up = place_call("cols", block_coords, *reduce_blocks(*up, near, places), (hidden_width,))[0]
    grad_query, grad_key, grad_out, grad_value = place_call(
        "cols", block_coords, *reduce_blocks(*rest, near, places), (width, kv_width, width, kv_width)
    )
    gain_sums = sum_everywhere(jnp.concatenate([sum(sums_one), sum(sums_two)], axis=0), near)
    gain_sums = lax.dynamic_slice_in_dim(gain_sums, y * half, half, 1)
    return (
        output[None],
        grad_tokens[None],
        grad_query,
        grad_key,
        grad_value,
        grad_out,
        grad_gate,
        grad_up,
        grad_down,
        gain_sums[0],
        gain_sums[1],
    )


def solution(mesh):
    rows = P("ws", "ctx", None)
    flat = P("ws", None)
    in_specs = (rows, rows) + (flat,) * 7 + (P("ws"), P("ws"), P()) + (flat,) * 4
    out_specs = (rows, rows) + (flat,) * 7 + (P("ws"), P("ws"))
    return jax.shard_map(
        on_device, mesh=mesh, in_specs=in_specs, out_specs=out_specs, check_vma=False
    )
```

```python
import functools

import jax
import jax.numpy as jnp
from jax import lax
from jax.experimental import pallas as pl
from jax.experimental.pallas import tpu as pltpu
from jax.sharding import PartitionSpec as P

QUERY_HEADS = 15
KEY_VALUE_HEADS = 5
HEAD_SIZE = 64
SHARE = QUERY_HEADS // KEY_VALUE_HEADS
BLK = 64
CONT_BITS = 10
EPSILON = 1e-05
ROPE_BASE = 10000.0
MASK_FLOOR = -1e30
SCALE = HEAD_SIZE ** (-0.5)

BF = jnp.bfloat16
F32 = jnp.float32
AXES = ("ctx", "ws")
FF_CHUNK = 512
MIB = 1024 * 1024
VMEM_JOIN = 24 * MIB

Y_BIT, C_BIT, X_BIT, Z1_BIT, Z2_BIT = 1, 2, 4, 8, 16
NEAR = (0, X_BIT, Y_BIT, Z1_BIT, X_BIT | Y_BIT | Z1_BIT, X_BIT | Y_BIT, Y_BIT | Z1_BIT, Z1_BIT | X_BIT)


def hop(value, mask):
    return lax.ppermute(value, AXES, [(i, i ^ mask) for i in range(32)])


def swap_place(i):
    y, z2 = i & 1, (i >> 4) & 1
    return (i & ~(Y_BIT | Z2_BIT)) | (Z2_BIT if y else 0) | (Y_BIT if z2 else 0)


def move(value):
    return lax.ppermute(value, AXES, [(i, swap_place(i)) for i in range(32)])


def ctx_mask(mask):
    return (
        (1 if mask & C_BIT else 0)
        | (2 if mask & X_BIT else 0)
        | (4 if mask & Z1_BIT else 0)
        | (8 if mask & Y_BIT else 0)
    )


NT = (((1,), (1,)), ((), ()))
TN = (((0,), (0,)), ((), ()))
NN = (((1,), (0,)), ((), ()))


def mm(left, right, dims=NN, precision=None):
    return lax.dot_general(left, right, dims, precision=precision, preferred_element_type=F32)


def normed_rows(values):
    inverse = lax.rsqrt(jnp.mean(values * values, axis=-1, keepdims=True) + EPSILON)
    return values * inverse, inverse


def norm_back(grad_in, normed, inverse, gain):
    scaled = grad_in * gain
    return inverse * (scaled - normed * jnp.mean(scaled * normed, axis=-1, keepdims=True))


def turn(values, cosine, sine, back=False):
    rows, width = values.shape
    lane = lax.broadcasted_iota(jnp.int32, (rows, 128), 1)
    first = (lane & (HEAD_SIZE - 1)) < HEAD_SIZE // 2
    if back:
        sine = -sine
    pieces = []
    for start in range(0, width, 128):
        wide = min(128, width - start)
        part = values[:, start : start + wide]
        if wide < 128:
            part = jnp.concatenate([part, jnp.zeros((rows, 128 - wide), F32)], axis=1)
        other = jnp.where(first, pltpu.roll(part, 96, 1), pltpu.roll(part, 32, 1))
        pieces.append((part * cosine + other * sine)[:, :wide])
    return jnp.concatenate(pieces, axis=1)


def vm():
    return pl.BlockSpec(memory_space=pltpu.VMEM)


def sm():
    return pl.BlockSpec(memory_space=pltpu.SMEM)


def hbm():
    return pl.BlockSpec(memory_space=pl.ANY)


def shaped(shape, dtype):
    return jax.ShapeDtypeStruct(shape, dtype)


def params(mib, **kw):
    return pltpu.CompilerParams(vmem_limit_bytes=mib * MIB, **kw)


def estimate(flops, nbytes):
    return pl.CostEstimate(flops=int(flops), bytes_accessed=int(nbytes), transcendentals=0)


class Order:
    def __init__(self, token):
        self.token = token

    def take(self, *values):
        *values, self.token = lax.optimization_barrier(values + (self.token,))
        return values[0] if len(values) == 1 else values


def read_coords(ref):
    return [ref[i] for i in range(4)]


def aligned(row):
    return row if isinstance(row, int) else pl.multiple_of(row, 8)


def join_kernel(plans, n_arrays, coords_ref, *args):
    refs, outs, sems = args[:n_arrays], args[n_arrays:-1], args[-1]
    coords = read_coords(coords_ref)
    copies = []
    for out, plan in zip(outs, plans, strict=True):
        for array, index, first, rows, place in plan:
            source = refs[array] if index is None else refs[array].at[index]
            source = source.at[pl.ds(first, rows), :]
            cols = source.shape[1]
            row, col = place(*coords)
            target = out.at[pl.ds(aligned(row), rows), :]
            if cols != out.shape[1]:
                target = out.at[pl.ds(aligned(row), rows), pl.ds(pl.multiple_of(col, 128), cols)]
            copy = pltpu.make_async_copy(source, target, sems.at[len(copies)])
            copy.start()
            copies.append(copy)
    for copy in copies:
        copy.wait()


def join_call(coords, arrays, shapes, plans):
    count = sum(len(plan) for plan in plans)
    return pl.pallas_call(
        functools.partial(join_kernel, plans, len(arrays)),
        name="join_weights",
        out_shape=tuple(pltpu.VMEM(shape, BF) for shape in shapes),
        in_specs=[sm()] + [hbm()] * len(arrays),
        out_specs=tuple(vm() for _ in shapes),
        scratch_shapes=[pltpu.SemaphoreType.DMA((count,))],
        compiler_params=pltpu.CompilerParams(vmem_limit_bytes=VMEM_JOIN),
        cost_estimate=estimate(0, sum(2 * a * b for a, b in shapes)),
    )(coords, *arrays)


def pack_kernel(coords_ref, q_ref, k_ref, v_ref, gain1_ref, gain2_ref, own_ref, piece_ref):
    half, width = q_ref.shape
    kv_width = k_ref.shape[0]
    own_ref[:, :width] = q_ref[...]
    own_ref[:, width : width + kv_width] = k_ref[...].T
    own_ref[:, width + kv_width :] = v_ref[...].T
    depth = half // 2
    start = pl.multiple_of(coords_ref[1] * depth, 8)
    piece_ref[:depth, :] = own_ref[pl.ds(start, depth), :]
    blank = jnp.zeros((1, own_ref.shape[1] - 2 * half), BF)
    row = jnp.concatenate([gain1_ref[...], gain2_ref[...], blank], axis=1)
    piece_ref[depth:, :] = jnp.broadcast_to(row, (8, row.shape[1]))


def pack_call(coords, w_query, key_t, value_t, gain_attn, gain_ffn):
    half, width = w_query.shape
    total = width + 2 * key_t.shape[0]
    return pl.pallas_call(
        pack_kernel,
        name="pack",
        out_shape=(shaped((half, total), BF), shaped((half // 2 + 8, total), BF)),
        in_specs=[sm()] + [vm()] * 5,
        out_specs=(vm(), vm()),
        compiler_params=params(12),
        cost_estimate=estimate(0, 4e6),
    )(coords, w_query, key_t, value_t, gain_attn, gain_ffn)


def stack_kernel(*refs):
    out_ref = refs[-1]
    at = 0
    for ref in refs[:-1]:
        out_ref[at : at + ref.shape[0], :] = ref[...]
        at += ref.shape[0]


def stack_call(pieces):
    rows = sum(p.shape[0] for p in pieces)
    return pl.pallas_call(
        stack_kernel,
        name="stack",
        out_shape=shaped((rows, pieces[0].shape[1]), pieces[0].dtype),
        in_specs=[vm()] * len(pieces),
        out_specs=vm(),
        compiler_params=params(8),
        cost_estimate=estimate(0, 2e6),
    )(*pieces)


def split_kernel(total_ref, other_ref, *outs):
    rows = outs[0].shape[0]
    for i, out in enumerate(outs):
        at = slice(i * rows, (i + 1) * rows)
        out[...] = (total_ref[at, :] + other_ref[at, :].astype(F32)).astype(out.dtype)


def split_call(total, other):
    rows, width = total.shape[0] // len(NEAR), total.shape[1]
    outs = [shaped((rows, width), F32)] + [shaped((rows, width), BF)] * (len(NEAR) - 1)
    return pl.pallas_call(
        split_kernel,
        name="split",
        out_shape=tuple(outs),
        in_specs=[vm(), vm()],
        out_specs=tuple(vm() for _ in outs),
        compiler_params=params(10),
        cost_estimate=estimate(0, 4e6),
    )(total, other)


def project(x, gain, wqkv_ref, cosine, sine, first_ref, q_ref, kv_ref):
    normed, _ = normed_rows(x)
    first_in = (normed * gain).astype(BF)
    first_ref[...] = first_in
    rows = mm(first_in, wqkv_ref[...])
    wide = SHARE * HEAD_SIZE
    q_width = KEY_VALUE_HEADS * wide
    kv_width = KEY_VALUE_HEADS * HEAD_SIZE
    key = turn(rows[:, q_width : q_width + kv_width], cosine, sine)
    value = rows[:, q_width + kv_width :]
    for h in range(KEY_VALUE_HEADS):
        at = slice(h * HEAD_SIZE, (h + 1) * HEAD_SIZE)
        kv_ref[:, h * 128 : (h + 1) * 128] = jnp.concatenate(
            [key[:, at], value[:, at]], axis=1
        ).astype(BF)
    query = (turn(rows[:, :q_width], cosine, sine).astype(BF) * SCALE).astype(BF)
    for h in range(KEY_VALUE_HEADS):
        q_ref[h] = query[:, h * wide : (h + 1) * wide]


def first_kernel(x_ref, gain_ref, cos_ref, sin_ref, wqkv_ref, first_ref, q_ref, kv_ref):
    project(
        x_ref[...].astype(F32), gain_ref[...], wqkv_ref, cos_ref[...], sin_ref[...],
        first_ref, q_ref, kv_ref,
    )


def first_call(tokens, gain, cosine, sine, wqkv):
    rows, width = tokens.shape
    return pl.pallas_call(
        first_kernel,
        name="first_projection",
        out_shape=(
            shaped((rows, width), BF),
            shaped((KEY_VALUE_HEADS, rows, SHARE * HEAD_SIZE), BF),
            shaped((rows, KEY_VALUE_HEADS * 128), BF),
        ),
        in_specs=[vm()] * 5,
        out_specs=(vm(), vm(), vm()),
        compiler_params=params(10),
        cost_estimate=estimate(2 * rows * width * 1600, 4e6),
    )(tokens, gain, cosine, sine, wqkv)


def padded_heads(wide_rows, left):
    rows = wide_rows.shape[0]
    blank = jnp.zeros((rows, HEAD_SIZE), wide_rows.dtype)
    stacked = []
    for j in range(SHARE):
        part = wide_rows[:, j * HEAD_SIZE : (j + 1) * HEAD_SIZE]
        stacked.append(jnp.concatenate([part, blank] if left else [blank, part], axis=1))
    return jnp.concatenate(stacked, axis=0)


def attend_kernel(prompt, q_ref, a_ref, b_ref, kpos_ref, live_ref, qpos_ref, p_ref, o_ref, bias_scr):
    rows = q_ref.shape[1]
    half = a_ref.shape[0]

    @pl.when(pl.program_id(0) == 0)
    def _():
        kpos = kpos_ref[...]
        klive = live_ref[...] > 0
        kseg = jnp.where(kpos < prompt, 0, 1 + ((kpos - prompt) >> CONT_BITS))

        def fill(i, carry):
            at = pl.ds(pl.multiple_of(i * 8, 8), 8)
            qpos = qpos_ref[at, :]
            qseg = jnp.where(qpos < prompt, 0, 1 + ((qpos - prompt) >> CONT_BITS))
            earlier = kpos <= qpos
            shared = (kseg == 0) | (kseg == qseg)
            seen = earlier & shared & (klive | (kpos == qpos))
            bias_scr[at, :] = jnp.where(seen, 0.0, MASK_FLOOR)
            return carry

        lax.fori_loop(0, rows // 8, fill, 0)

    together = rows < 128
    if together:
        stacked = padded_heads(q_ref[0], True)
        all_a, all_b = mm(stacked, a_ref[...], NT), mm(stacked, b_ref[...], NT)
    blank = jnp.zeros((rows, HEAD_SIZE), BF)
    outs = []
    for j in range(SHARE):
        at = slice(j * rows, (j + 1) * rows)
        if together:
            s_a, s_b = all_a[at], all_b[at]
        else:
            part = jnp.concatenate([q_ref[0, :, j * HEAD_SIZE : (j + 1) * HEAD_SIZE], blank], axis=1)
            s_a, s_b = mm(part, a_ref[...], NT), mm(part, b_ref[...], NT)
        s_a = s_a + bias_scr[:, :half]
        s_b = s_b + bias_scr[:, half:]
        top = jnp.maximum(
            jnp.max(s_a, axis=-1, keepdims=True), jnp.max(s_b, axis=-1, keepdims=True)
        )
        w_a, w_b = jnp.exp(s_a - top), jnp.exp(s_b - top)
        mass = jnp.sum(w_a, axis=-1, keepdims=True) + jnp.sum(w_b, axis=-1, keepdims=True)
        inverse = 1.0 / mass
        p_a, p_b = (w_a * inverse).astype(BF), (w_b * inverse).astype(BF)
        p_ref[0, at, :half] = p_a
        p_ref[0, at, half:] = p_b
        if not together:
            outs.append((mm(p_a, a_ref[...]) + mm(p_b, b_ref[...]))[:, HEAD_SIZE:])
    if together:
        mixed = mm(p_ref[0, :, :half], a_ref[...]) + mm(p_ref[0, :, half:], b_ref[...])
        outs = [mixed[j * rows : (j + 1) * rows, HEAD_SIZE:] for j in range(SHARE)]
    o_ref[0] = jnp.concatenate(outs, axis=1).astype(BF)


def attend_call(query, part_a, part_b, kpos, klive, qpos, prompt):
    heads, rows, wide = query.shape
    half = part_a.shape[0]
    keys = 2 * half
    return pl.pallas_call(
        functools.partial(attend_kernel, prompt),
        name="attend",
        grid=(heads,),
        out_shape=(pltpu.HBM((heads, SHARE * rows, keys), BF), shaped((heads, rows, wide), BF)),
        in_specs=[
            pl.BlockSpec((1, rows, wide), lambda h: (h, 0, 0)),
            pl.BlockSpec((half, 128), lambda h: (0, h)),
            pl.BlockSpec((half, 128), lambda h: (0, h)),
            pl.BlockSpec((1, keys), lambda h: (0, 0)),
            pl.BlockSpec((1, keys), lambda h: (0, 0)),
            pl.BlockSpec((rows, 1), lambda h: (0, 0)),
        ],
        out_specs=(
            pl.BlockSpec((1, SHARE * rows, keys), lambda h: (h, 0, 0)),
            pl.BlockSpec((1, rows, wide), lambda h: (h, 0, 0)),
        ),
        scratch_shapes=[pltpu.VMEM((rows, keys), F32)],
        compiler_params=params(12 if keys <= 2048 else 56, dimension_semantics=("arbitrary",)),
        cost_estimate=estimate(8 * heads * SHARE * rows * keys * 128, heads * SHARE * rows * keys * 2),
    )(query, part_a, part_b, kpos, klive, qpos)


def attend_back_kernel(q_ref, do_ref, a_ref, b_ref, p_ref, dq_ref, da_ref, db_ref, dp_scr, ds_scr):
    rows = q_ref.shape[1]
    half = a_ref.shape[0]
    stacked = padded_heads(q_ref[0], True)
    grads = padded_heads(do_ref[0], False)
    dp_scr[:, :half] = mm(grads, a_ref[...], NT)
    dp_scr[:, half:] = mm(grads, b_ref[...], NT)

    for j in range(SHARE):
        at = slice(j * rows, (j + 1) * rows)
        weights = p_ref[0, at, :].astype(F32)
        dp = dp_scr[at, :]
        delta = jnp.sum(weights * dp, axis=-1, keepdims=True)
        ds_scr[at, :] = (weights * (dp - delta)).astype(BF)
    dq = (mm(ds_scr[:, :half], a_ref[...]) + mm(ds_scr[:, half:], b_ref[...])) * SCALE
    dq_ref[0] = jnp.concatenate(
        [dq[j * rows : (j + 1) * rows, :HEAD_SIZE] for j in range(SHARE)], axis=1
    )
    for at, out in ((slice(0, half), da_ref), (slice(half, 2 * half), db_ref)):
        turned = mm(stacked, ds_scr[:, at], TN) + mm(grads, p_ref[0, :, at], TN)
        out[...] = turned.T.astype(out.dtype)


def attend_back_call(query, d_out, part_a, part_b, weights):
    heads, rows, wide = query.shape
    half = part_a.shape[0]
    keys = 2 * half
    return pl.pallas_call(
        attend_back_kernel,
        name="attend_back",
        grid=(heads,),
        out_shape=(
            shaped((heads, rows, wide), F32),
            shaped((half, heads * 128), F32),
            shaped((half, heads * 128), BF),
        ),
        in_specs=[
            pl.BlockSpec((1, rows, wide), lambda h: (h, 0, 0)),
            pl.BlockSpec((1, rows, wide), lambda h: (h, 0, 0)),
            pl.BlockSpec((half, 128), lambda h: (0, h)),
            pl.BlockSpec((half, 128), lambda h: (0, h)),
            pl.BlockSpec((1, SHARE * rows, keys), lambda h: (h, 0, 0)),
        ],
        out_specs=(
            pl.BlockSpec((1, rows, wide), lambda h: (h, 0, 0)),
            pl.BlockSpec((half, 128), lambda h: (0, h)),
            pl.BlockSpec((half, 128), lambda h: (0, h)),
        ),
        scratch_shapes=[
            pltpu.VMEM((SHARE * rows, keys), F32),
            pltpu.VMEM((SHARE * rows, keys), BF),
        ],
        compiler_params=params(14 if keys <= 2048 else 60, dimension_semantics=("arbitrary",)),
        cost_estimate=estimate(16 * heads * SHARE * rows * keys * 128, heads * SHARE * rows * keys * 2),
    )(query, d_out, part_a, part_b, weights)


def picks(sel_ref, total_rows):
    capacity = sel_ref.shape[1]
    row = lax.broadcasted_iota(jnp.int32, (total_rows, capacity), 0)
    return row == sel_ref[...]


def live_column(live_ref, rows):
    count = jnp.sum(live_ref[:, :].astype(F32), axis=1, keepdims=True)
    return lax.broadcasted_iota(jnp.int32, (rows, 1), 0).astype(F32) < count


def feed_forward(x, ao_ref, gain_two, wo, wg, wu, wd, ao_out, mid_ref, second_ref, g_ref, u_ref, hid_ref, y_scr):
    rows = x.shape[0]
    mixed = jnp.concatenate([ao_ref[h] for h in range(KEY_VALUE_HEADS)], axis=1)
    ao_out[...] = mixed
    middle = x + mm(mixed, wo[...])
    mid_ref[...] = middle
    normed, _ = normed_rows(middle)
    second_ref[...] = (normed * gain_two).astype(BF)
    y_scr[...] = middle

    def chunk(j, carry):
        at = pl.ds(pl.multiple_of(j * FF_CHUNK, FF_CHUNK), FF_CHUNK)
        second = second_ref[...]
        g = mm(second, wg[:, at])
        u = mm(second, wu[:, at])
        g_ref[:, at] = g
        u_ref[:, at] = u
        hidden = (g / (1.0 + jnp.exp(-g)) * u).astype(BF)
        hid_ref[:, at] = hidden
        y_scr[...] += mm(hidden, wd[:, at], NT)
        return carry

    lax.fori_loop(0, wg.shape[1] // FF_CHUNK, chunk, 0)


def dense_kernel(step, *args):
    args = list(args)
    take = lambda k: [args.pop(0) for _ in range(k)]
    x_ref, ao_ref, gain1_ref, gain2_ref = take(4)
    if step == 0:
        sel_ref, cos_ref, sin_ref = take(3)
    elif step == 1:
        live_ref, cos_ref, sin_ref = take(3)
    else:
        sel_ref, live2_ref, live_ref, h1_ref, h2_ref = take(5)
    wo, wg, wu, wd = take(4)
    if step < 2:
        (wqkv,) = take(1)
    ao_out, mid_ref, second_ref, g_ref, u_ref, hid_ref = take(6)
    if step < 2:
        h_ref, next_ref, first_ref, q_ref, kv_ref = take(5)
    else:
        (out_ref,) = take(1)
    (y_scr,) = take(1)
    rows = x_ref.shape[0]
    x = x_ref[...].astype(F32)
    feed_forward(
        x, ao_ref, gain2_ref[...], wo, wg, wu, wd, ao_out, mid_ref, second_ref,
        g_ref, u_ref, hid_ref, y_scr,
    )
    updated = y_scr[...]
    if step == 0:
        h_ref[...] = updated
        chosen = picks(sel_ref, rows).astype(F32)
        following = mm(chosen, updated, TN, lax.Precision.HIGHEST)
    else:
        updated = jnp.where(live_column(live_ref, rows), updated, x)
    if step == 1:
        h_ref[...] = updated
        following = updated[: next_ref.shape[0]]
    if step < 2:
        next_ref[...] = following
        project(
            following, gain1_ref[...], wqkv, cos_ref[...], sin_ref[...],
            first_ref, q_ref, kv_ref,
        )
    else:
        slots = jnp.concatenate([updated, h2_ref[rows:, :]], axis=0).astype(BF)
        hit = picks(sel_ref, h1_ref.shape[0]) & (live2_ref[...] > 0)
        placed = mm(hit.astype(BF), slots)
        any_hit = jnp.sum(hit.astype(F32), axis=1, keepdims=True) > 0.5
        out_ref[...] = jnp.where(any_hit, placed, h1_ref[...]).astype(BF)


def dense_call(near, step, x, mixed, gain1, gain2, extra, weights, next_rows):
    rows, width = x.shape
    hidden = weights[1].shape[1]
    outs = [
        shaped((rows, width), BF),
        shaped((rows, width), F32),
        shaped((rows, width), BF),
        shaped((rows, hidden), F32),
        shaped((rows, hidden), F32),
        shaped((rows, hidden), BF),
    ]
    if step < 2:
        outs += [
            shaped((rows, width), F32),
            shaped((next_rows, width), F32),
            shaped((next_rows, width), BF),
            shaped((KEY_VALUE_HEADS, next_rows, SHARE * HEAD_SIZE), BF),
            shaped((next_rows, KEY_VALUE_HEADS * 128), BF),
        ]
    else:
        outs += [shaped((next_rows, width), BF)]
    return pl.pallas_call(
        functools.partial(dense_kernel, step),
        name=f"dense_{step}",
        out_shape=tuple(outs),
        in_specs=[vm()] * (4 + len(extra) + len(weights)),
        out_specs=tuple(vm() for _ in outs),
        scratch_shapes=[pltpu.VMEM((rows, width), F32)],
        compiler_params=params(10 if near else 56),
        cost_estimate=estimate(2 * rows * 9.83e6, 2.4e7),
    )(x, mixed, gain1, gain2, *extra, *weights)


def feed_back(d_y, mid_ref, g_ref, u_ref, gain_two, wd, wg, wu, wo, dyb_ref, dg_ref, du_ref, dmid_ref, dz_ref, dao_ref, sum_ref, acc_scr):
    dyb_ref[...] = d_y.astype(BF)
    acc_scr[...] = jnp.zeros_like(acc_scr)

    def chunk(j, carry):
        at = pl.ds(pl.multiple_of(j * FF_CHUNK, FF_CHUNK), FF_CHUNK)
        d_hidden = mm(dyb_ref[...], wd[:, at])
        g, u = g_ref[:, at], u_ref[:, at]
        sigma = 1.0 / (1.0 + jnp.exp(-g))
        d_gate = (d_hidden * u * sigma * (1.0 + g * (1.0 - sigma))).astype(BF)
        d_up = (d_hidden * (g * sigma)).astype(BF)
        dg_ref[:, at] = d_gate
        du_ref[:, at] = d_up
        acc_scr[...] += mm(d_gate, wg[:, at], NT) + mm(d_up, wu[:, at], NT)
        return carry

    lax.fori_loop(0, wg.shape[1] // FF_CHUNK, chunk, 0)
    d_second = acc_scr[...]
    normed, inverse = normed_rows(mid_ref[...])
    sum_ref[...] = jnp.sum(d_second * normed, axis=0, keepdims=True)
    d_mid = norm_back(d_second, normed, inverse, gain_two) + d_y
    dmid_ref[...] = d_mid
    d_low = d_mid.astype(BF)
    dz_ref[...] = d_low
    d_mixed = mm(d_low, wo[...], NT).astype(BF)
    wide = SHARE * HEAD_SIZE
    for h in range(KEY_VALUE_HEADS):
        dao_ref[h] = d_mixed[:, h * wide : (h + 1) * wide]


def project_back(own_ref, others, dq_ref, x, dmid_ref, gain_one, cosine, sine, wqkv, dqkv_ref, sum_ref):
    total = own_ref[...].astype(F32)
    for other in others:
        total = total + other[...].astype(F32)
    d_key = jnp.concatenate(
        [total[:, h * 128 : h * 128 + HEAD_SIZE] for h in range(KEY_VALUE_HEADS)], axis=1
    )
    d_value = jnp.concatenate(
        [total[:, h * 128 + HEAD_SIZE : (h + 1) * 128] for h in range(KEY_VALUE_HEADS)], axis=1
    )
    d_query = jnp.concatenate([dq_ref[h] for h in range(KEY_VALUE_HEADS)], axis=1)
    d_rows = jnp.concatenate(
        [turn(d_query, cosine, sine, True), turn(d_key, cosine, sine, True), d_value], axis=1
    ).astype(BF)
    dqkv_ref[...] = d_rows
    d_first = mm(d_rows, wqkv[...], NT)
    normed, inverse = normed_rows(x)
    sum_ref[...] = jnp.sum(d_first * normed, axis=0, keepdims=True)
    return norm_back(d_first, normed, inverse, gain_one) + dmid_ref[...]


def back_kernel(phase, n_parts, *args):
    args = list(args)
    take = lambda k: [args.pop(0) for _ in range(k)]
    if phase > 0:
        gain1_ref, cos_ref, sin_ref, x_ref, dmid_in, dq_ref = take(6)
        own_ref, *others = take(n_parts)
    if phase < 3:
        gain2_ref, mid_ref, g_ref, u_ref = take(4)
    if phase == 0:
        cot_ref, sel_ref, live3_ref = take(3)
    elif phase == 1:
        slots_ref, live3_ref, live2_ref = take(3)
    elif phase == 2:
        cot_ref, sel_ref, live2_ref = take(3)
    if phase > 0:
        (wqkv,) = take(1)
    if phase < 3:
        mats = take(4)
    if phase > 0:
        dqkv_ref, sum1_ref = take(2)
    if phase < 3:
        dyb_ref, dg_ref, du_ref, dmid_ref, dz_ref, dao_ref, sum2_ref = take(7)
    if phase == 0:
        (slots_out,) = take(1)
    elif phase == 3:
        (grad_ref,) = take(1)
    if phase < 3:
        (acc_scr,) = take(1)
    if phase > 0:
        d_x = project_back(
            own_ref, others, dq_ref, x_ref[...].astype(F32), dmid_in, gain1_ref[...],
            cos_ref[...], sin_ref[...], wqkv, dqkv_ref, sum1_ref,
        )
    if phase == 0:
        chosen = picks(sel_ref, cot_ref.shape[0]).astype(BF)
        slots = mm(chosen, cot_ref[...], TN)
        slots_out[...] = slots
        rows = mid_ref.shape[0]
        d_y = jnp.where(live_column(live3_ref, rows), slots[:rows], 0.0)
    elif phase == 1:
        rows = x_ref.shape[0]
        slots = slots_ref[...]
        head = jnp.where(live_column(live3_ref, rows), d_x, slots[:rows])
        slots = jnp.concatenate([head, slots[rows:]], axis=0)
        d_y = jnp.where(live_column(live2_ref, slots.shape[0]), slots, 0.0)
    elif phase == 2:
        hit = picks(sel_ref, cot_ref.shape[0]) & (live2_ref[...] > 0)
        placed = mm(hit.astype(F32), d_x, NN, lax.Precision.HIGHEST)
        any_hit = jnp.sum(hit.astype(F32), axis=1, keepdims=True) > 0.5
        d_y = jnp.where(any_hit, placed, cot_ref[...].astype(F32))
    else:
        grad_ref[...] = d_x
        return
    feed_back(
        d_y, mid_ref, g_ref, u_ref, gain2_ref[...], *mats,
        dyb_ref, dg_ref, du_ref, dmid_ref, dz_ref, dao_ref, sum2_ref, acc_scr,
    )


def back_call(near, phase, before, parts, into, extra, weights, rows_next):
    ins = list(before) + list(parts) + list(into) + list(extra) + list(weights)
    outs, scratch = [], []
    if phase > 0:
        rows, width = before[3].shape
        outs += [
            shaped((rows, weights[0].shape[1]), BF),
            shaped((1, width), F32),
        ]
    if phase < 3:
        rows, hidden = into[2].shape
        width = into[1].shape[1]
        outs += [
            shaped((rows, width), BF),
            shaped((rows, hidden), BF),
            shaped((rows, hidden), BF),
            shaped((rows, width), F32),
            shaped((rows, width), BF),
            shaped((KEY_VALUE_HEADS, rows, SHARE * HEAD_SIZE), BF),
            shaped((1, width), F32),
        ]
        scratch += [pltpu.VMEM((rows, width), F32)]
    if phase == 0:
        outs += [shaped((rows_next, width), F32)]
    elif phase == 3:
        outs += [shaped((rows, width), F32)]
    return pl.pallas_call(
        functools.partial(back_kernel, phase, len(parts)),
        name=f"back_{phase}",
        out_shape=tuple(outs),
        in_specs=[vm()] * len(ins),
        out_specs=tuple(vm() for _ in outs),
        scratch_shapes=scratch,
        compiler_params=params(10 if near else 56),
        cost_estimate=estimate(2 * rows * 9.83e6, 2.4e7),
    )(*ins)


def stack_rows(refs, scratch):
    at = 0
    for ref in refs:
        scratch[at : at + ref.shape[0], :] = ref[...]
        at += ref.shape[0]


def put_blocks(value, x_of, coords, ref, per_row):
    y, _, x, z = coords
    depth = ref.shape[-2]
    for ya in range(2):
        for xa in range(2) if per_row else (None,):
            for za in range(4):
                row = (ya * (2 if per_row else 1) + (xa or 0)) * 4 + za
                ref[y ^ ya, (x ^ xa) if per_row else x_of, z ^ za] = value[
                    row * depth : (row + 1) * depth
                ].astype(BF)


def grad_cols_kernel(n_steps, coords_ref, *args):
    left, args = args[:n_steps], args[n_steps:]
    right, args = args[:n_steps], args[n_steps:]
    keep_ref, send_ref, l_scr, r_scr = args
    coords = read_coords(coords_ref)
    _, c, x, _ = coords
    stack_rows(left, l_scr)
    stack_rows(right, r_scr)
    block = keep_ref.shape[-1]
    for far, ref in ((1, send_ref), (0, keep_ref)):

        def body(rx, carry, far=far, ref=ref):
            start = pl.multiple_of(((c ^ far) * 2 + (x ^ rx)) * block, 128)
            value = mm(l_scr[...], r_scr[:, pl.ds(start, block)], TN)
            put_blocks(value, rx, coords, ref, False)
            return carry

        lax.fori_loop(0, 2, body, 0)


def grad_rows_kernel(n_steps, coords_ref, *args):
    left, args = args[:n_steps], args[n_steps:]
    right, args = args[:n_steps], args[n_steps:]
    keep_ref, send_ref, l_scr, r_scr = args
    coords = read_coords(coords_ref)
    y, c, x, z = coords
    stack_rows(left, l_scr)
    stack_rows(right, r_scr)
    depth = keep_ref.shape[-2]
    span = 8 * depth
    for far, ref in ((1, send_ref), (0, keep_ref)):

        def body(ry, carry, far=far, ref=ref):
            start = pl.multiple_of(((y ^ ry) * 2 + (c ^ far)) * span, 128)
            value = mm(l_scr[:, pl.ds(start, span)], r_scr[...], TN)
            for xa in range(2):
                for za in range(4):
                    row = (xa * 4 + za) * depth
                    ref[ry, x ^ xa, z ^ za] = value[row : row + depth].astype(BF)
            return carry

        lax.fori_loop(0, 2, body, 0)


def grad_mixed_kernel(n_steps, coords_ref, *args):
    groups = []
    for _ in range(4):
        groups.append(args[:n_steps])
        args = args[n_steps:]
    keep_ref, send_ref, first_scr, mixed_scr, qkv_scr, z_scr, val_scr = args
    coords = read_coords(coords_ref)
    _, c, x, _ = coords
    for refs, scr in zip(groups, (first_scr, mixed_scr, qkv_scr, z_scr), strict=True):
        stack_rows(refs, scr)
    block = keep_ref.shape[-1]
    width = z_scr.shape[1]
    kv_width = (qkv_scr.shape[1] - width) // 2
    for ca in range(2):
        for xa in range(2):
            if ca == 0:
                val_scr[...] = mm(first_scr[...], qkv_scr[:, xa * block : (xa + 1) * block], TN)
            elif xa == 0:
                val_scr[...] = mm(mixed_scr[...], z_scr[:, :block], TN)
            else:
                val_scr[...] = jnp.concatenate(
                    [
                        mm(mixed_scr[...], z_scr[:, block:], TN),
                        mm(first_scr[...], qkv_scr[:, width + kv_width :], TN),
                    ],
                    axis=1,
                )

            @pl.when(c == ca)
            def _(xa=xa):
                put_blocks(val_scr[...], x ^ xa, coords, keep_ref, False)

            @pl.when(c != ca)
            def _(xa=xa):
                put_blocks(val_scr[...], x ^ xa, coords, send_ref, False)


def grad_call(kind, coords, groups):
    n_steps = len(groups[0])
    rows = sum(a.shape[0] for a in groups[0])
    width, cols = groups[0][0].shape[1], groups[1][0].shape[1]
    scratch = [pltpu.VMEM((rows, g[0].shape[1]), BF) for g in groups]
    if kind == "rows":
        kernel, block = grad_rows_kernel, (width // 32, cols)
    elif kind == "cols":
        kernel, block = grad_cols_kernel, (width // 8, cols // 4)
    else:
        total = sum(g[0].shape[1] for g in groups[2:])
        kernel, block = grad_mixed_kernel, (width // 8, total // 4)
        scratch += [pltpu.VMEM((width, block[1]), F32)]
    out = shaped((2, 2, 4) + block, BF)
    ins = [a for g in groups for a in g]
    return pl.pallas_call(
        functools.partial(kernel, n_steps),
        name=f"grad_{kind}",
        out_shape=(out, out),
        in_specs=[sm()] + [vm()] * len(ins),
        out_specs=(vm(), vm()),
        scratch_shapes=scratch,
        compiler_params=params(16),
        cost_estimate=estimate(2 * rows * 16 * 2 * block[0] * block[1], 1e7),
    )(coords, *ins)


def place_cols_kernel(coords_ref, near_ref, far_ref, *outs):
    _, c, x, _ = read_coords(coords_ref)
    block = near_ref.shape[-1]
    target = outs[-1]
    for far, ref in ((0, near_ref), (1, far_ref)):
        for rx in range(2):
            cols = pl.ds(pl.multiple_of(((c ^ far) * 2 + (x ^ rx)) * block, 128), block)
            target[:, cols] = ref[rx, 0].astype(F32)
    if len(outs) > 1:
        at = 0
        for out in outs[:-1]:
            out[...] = target[:, at : at + out.shape[1]]
            at += out.shape[1]


def place_rows_kernel(coords_ref, near_ref, far_ref, out_ref, scr):
    _, _, x, z = read_coords(coords_ref)
    depth = near_ref.shape[-2]

    def put(ref):
        for rx in range(2):
            for rz in range(4):
                row = pl.multiple_of(((x ^ rx) * 4 + (z ^ rz)) * depth, 8)
                scr[pl.ds(row, depth), :] = ref[rx, rz].astype(F32)

    @pl.when(pl.program_id(0) == 0)
    def _():
        put(near_ref)

    @pl.when(pl.program_id(0) == 1)
    def _():
        put(far_ref)

    out_ref[...] = scr[...].T


def place_call(kind, coords, near, far, widths):
    depth, block = near.shape[-2:]
    scratch = []
    if kind == "rows":
        kernel, grid = place_rows_kernel, (2,)
        outs = (shaped((block, 16 * depth), F32),)
        source = pl.BlockSpec((2, 4, depth, block), lambda f, k: (0, 0, 0, 0))
        targets = (pl.BlockSpec((block, 8 * depth), lambda f, k: (0, k[1] ^ f)),)
        scratch = [pltpu.VMEM((8 * depth, block), F32)]
    else:
        kernel, grid = place_cols_kernel, (4,)
        outs = tuple(shaped((4 * depth, w), F32) for w in widths)
        source = pl.BlockSpec((2, 1, depth, block), lambda i, k: (0, i, 0, 0))
        targets = tuple(pl.BlockSpec((depth, w), lambda i, k: (k[3] ^ i, 0)) for w in widths)
        if len(outs) > 1:
            scratch = [pltpu.VMEM((depth, 4 * block), F32)]
    return pl.pallas_call(
        kernel,
        name=f"place_{kind}",
        grid_spec=pltpu.PrefetchScalarGridSpec(
            num_scalar_prefetch=1,
            grid=grid,
            in_specs=[source, source],
            out_specs=targets,
            scratch_shapes=scratch,
        ),
        out_shape=outs,
        compiler_params=params(12),
        cost_estimate=estimate(0, 1e7),
    )(coords, near, far)


def low_sum(left, right):
    return (left.astype(F32) + right.astype(F32)).astype(BF)


def gather_keys(kv, order, near, beside=((), (), ())):
    if not near:
        whole = lax.all_gather(kv, "ctx", axis=0, tiled=True)
        half = whole.shape[0] // 2
        return whole[:half], whole[half:]
    kv = order.take(kv)
    hops = [hop(kv, m) for m in (X_BIT, Y_BIT, Z1_BIT, X_BIT | Y_BIT | Z1_BIT)]
    for start in beside[0]:
        start()
    by_x, by_y, by_z, across = order.take(*hops)
    hops = [hop(by_x, Y_BIT), hop(by_y, Z1_BIT), hop(by_z, X_BIT)]
    for start in beside[1]:
        start()
    hops = order.take(*hops)
    part = stack_call([kv, by_x, by_y, by_z, across, *hops])
    far = hop(part, C_BIT)
    for start in beside[2]:
        start()
    return part, order.take(far)


def scatter_keys(part_a, part_b, order, near, while_one=lambda: None, while_two=lambda: None):
    if not near:
        while_one()
        while_two()
        whole = jnp.concatenate([part_a, part_b.astype(F32)], axis=0)
        return [lax.psum_scatter(whole, "ctx", scatter_dimension=0, tiled=True)]
    part_a, part_b = order.take(part_a, part_b)
    far = hop(part_b, C_BIT)
    while_one()
    own, *others = split_call(part_a, order.take(far))
    others = order.take(*others)
    others = [hop(value, mask) for value, mask in zip(others, NEAR[1:], strict=True)]
    while_two()
    return [own, *order.take(*others)]


def cut_rows(value, index, count):
    size = value.shape[0] // count
    return lax.dynamic_slice_in_dim(value, index * size, size, 0)


def cut_cols(value, index, count):
    size = value.shape[1] // count
    return lax.dynamic_slice_in_dim(value, index * size, size, 1)


def spread(mine):
    return mine, hop(mine, X_BIT), hop(mine, Z1_BIT), hop(mine, X_BIT | Z1_BIT)


BESIDE = ((0, 0), (1, 0), (0, 1), (1, 1))


def pair_sum(keep, send, near):
    if near:
        return low_sum(keep, hop(send, C_BIT))
    return lax.psum(jnp.stack([keep, send]).astype(F32), AXES)


def block_sums(total):
    (got,) = yield [hop(total[1], Y_BIT)]
    total = low_sum(total[0], got)
    (got,) = yield [hop(total[1], X_BIT)]
    total = low_sum(total[0], got)
    along_z = (Z1_BIT, Z2_BIT, Z1_BIT | Z2_BIT)
    got = yield [hop(total[i + 1], mask) for i, mask in enumerate(along_z)]
    mine = total[0].astype(F32)
    for value in got:
        mine = mine + value.astype(F32)
    mine = mine.astype(BF)
    got = yield [hop(mine, mask) for mask in along_z]
    total = jnp.stack([mine, *got])
    (got,) = yield [hop(total, X_BIT)]
    total = jnp.stack([total, got])
    (got,) = yield [hop(total, C_BIT)]
    return total, got


def sums_by_hops(value):
    for mask in (C_BIT, X_BIT, Y_BIT, Z1_BIT, Z2_BIT):
        (got,) = yield [hop(value, mask)]
        value = value + got
    return value


class Course:
    def __init__(self, order, chain, value):
        self.order, self.chain = order, chain(order.take(value))
        self.waiting, self.result = next(self.chain), None

    def step(self):
        got = self.order.take(*self.waiting)
        got = got if isinstance(got, (list, tuple)) else [got]
        try:
            self.waiting = self.chain.send(got)
        except StopIteration as end:
            self.waiting, self.result = None, end.value


def on_device(
    tokens, cotangent, w_query, key_weight, value_weight, w_out, w_gate, w_up, w_down,
    gain_attn, gain_ffn, block_order, sel_mid, live_mid, sel_last, live_last,
):
    ctx_count, ws_count = lax.axis_size("ctx"), lax.axis_size("ws")
    near = ctx_count == 16 and ws_count == 2
    ctx, y = lax.axis_index("ctx"), lax.axis_index("ws")
    tok_local = tokens.shape[1]
    cap_mid, cap_last = sel_mid.shape[1] // ctx_count, sel_last.shape[1] // ctx_count
    if near:
        c, x, z = ctx & 1, (ctx >> 1) & 1, ctx >> 2
        places = (y, c, x, z)
        here = (ctx & 7) | (y << 3)
        turn_order = here ^ jnp.array([ctx_mask(m) for m in NEAR] + [ctx_mask(m) | 1 for m in NEAR], jnp.int32)
        relocate = move
    else:
        zero = jnp.int32(0)
        places = (y, zero, zero, zero)
        here = ctx
        turn_order = jnp.arange(ctx_count, dtype=jnp.int32)
        relocate = lambda v: v
    coords = jnp.stack([jnp.asarray(v, jnp.int32) for v in places])
    block_coords = coords if near else jnp.zeros((4,), jnp.int32)
    width = tokens.shape[2]
    half = w_query.shape[0]
    plan = jnp.concatenate(
        [
            sel_mid.reshape(ctx_count, cap_mid),
            live_mid.reshape(ctx_count, cap_mid),
            live_last.reshape(ctx_count, cap_last),
        ],
        axis=1,
    )
    qkv_width = w_query.shape[1] + 2 * key_weight.shape[1]
    order = Order(coords)
    if near:
        assert tok_local <= 256
        own_qkv, piece = pack_call(
            coords, w_query, key_weight.T, value_weight.T, gain_attn.reshape(1, -1), gain_ffn.reshape(1, -1)
        )
        fetched = hop(piece, Y_BIT)
        marks = jnp.pad(plan.astype(BF), ((0, 0), (0, width - plan.shape[1])))
        tok = move(jnp.concatenate([tokens[0], marks], axis=0))
        quad = x * 2 + (z & 1)
        own_down = w_down.T
        fetched, cut_gate, cut_up, cut_out, cut_down = order.take(
            fetched,
            *(cut_cols(cut_rows(w, c, 2), quad, 4) for w in (w_gate, w_up)),
            cut_rows(w_out, c, 2),
            cut_rows(own_down, c, 2),
        )
        far = hop(fetched, C_BIT)
        gate_mine, up_mine = hop(cut_gate, Y_BIT), hop(cut_up, Y_BIT)
        out_mine, down_mine = hop(cut_out, Y_BIT), hop(cut_down, Y_BIT)
        far, tok = order.take(far, tok)
        plan = tok[tok_local:, : plan.shape[1]].astype(jnp.int32)
        tok = tok[:tok_local]
        depth = half // 2
        beyond = [fetched[depth : depth + 1, i * half : (i + 1) * half] for i in range(2)]
        gains = [
            jnp.where(y == 0, jnp.concatenate([own, other], axis=1), jnp.concatenate([other, own], axis=1))
            for own, other in zip((gain_attn.reshape(1, -1), gain_ffn.reshape(1, -1)), beyond, strict=True)
        ]
        (wqkv,) = join_call(
            coords,
            [own_qkv, fetched, far],
            [(2 * half, qkv_width)],
            [
                [
                    (0, None, 0, half, lambda ky, kc, kx, kz: (ky * half, 0)),
                    (1, None, 0, depth, lambda ky, kc, kx, kz: ((1 - ky) * half + kc * depth, 0)),
                    (2, None, 0, depth, lambda ky, kc, kx, kz: ((1 - ky) * half + (kc ^ 1) * depth, 0)),
                ]
            ],
        )
        state = {}

        def start_gate():
            state["gate"] = spread(order.take(gate_mine))

        def start_up():
            state["up"] = spread(order.take(up_mine))

        def share_gate():
            state["gate"] = stack_call(order.take(*state["gate"]))
            state["gate_far"] = hop(state["gate"], C_BIT)

        beside = ((start_gate,), (start_up,), (share_gate,))

        def fetch_rest():
            up = order.take(*state["up"])
            out, down = order.take(out_mine, down_mine)
            up = stack_call(up)
            fars = [hop(v, C_BIT) for v in (out, up, down)]
            out_far, up_far, down_far, gate_far = order.take(*fars, state["gate_far"])
            hidden_half = own_down.shape[1]
            block = cut_gate.shape[1]
            plans = [[(0, None, 0, half, lambda ky, kc, kx, kz: (ky * half, 0))]]
            for array, far in ((1, 0), (2, 1)):
                plans[0].append(
                    (array, None, 0, depth,
                     lambda ky, kc, kx, kz, far=far: ((1 - ky) * half + (kc ^ far) * depth, 0))
                )
            for first in (3, 6):
                steps = [(first, None, 0, half, lambda ky, kc, kx, kz: (ky * half, 0))]
                for array, far in ((first + 1, 0), (first + 2, 1)):
                    for k, (rx, rz) in enumerate(BESIDE):
                        steps.append(
                            (array, None, k * depth, depth,
                             lambda ky, kc, kx, kz, far=far, rx=rx, rz=rz: (
                                 (1 - ky) * half + (kc ^ far) * depth,
                                 ((kx ^ rx) * 2 + ((kz & 1) ^ rz)) * block,
                             ))
                        )
                plans.append(steps)
            steps = [(9, None, 0, width, lambda ky, kc, kx, kz: (0, ky * hidden_half))]
            for array, far in ((10, 0), (11, 1)):
                steps.append(
                    (array, None, 0, width // 2,
                     lambda ky, kc, kx, kz, far=far: (
                         (kc ^ far) * (width // 2), (1 - ky) * hidden_half
                     ))
                )
            plans.append(steps)
            return join_call(
                coords,
                [w_out, out, out_far, w_gate, state["gate"], gate_far, w_up, up, up_far,
                 own_down, down, down_far],
                [(2 * half, w_out.shape[1]), (2 * half, w_gate.shape[1]), (2 * half, w_up.shape[1]),
                 (width, 2 * hidden_half)],
                plans,
            )
    else:
        tok = tokens[0]
        whole = lambda w: lax.all_gather(w, "ws", axis=0, tiled=True)
        wqkv = whole(jnp.concatenate([w_query, key_weight, value_weight], axis=1))
        gains = [whole(g).reshape(1, -1) for g in (gain_attn, gain_ffn)]
        rest = [whole(w) for w in (w_out, w_gate, w_up)] + [whole(w_down).T]
        beside, fetch_rest = ((), (), ()), lambda: rest
    gain1, gain2 = (g.astype(F32) for g in gains)

    per_device = tok_local // BLK
    blocks = jnp.take(block_order.reshape(ctx_count, per_device), turn_order, axis=0)
    plan_order = jnp.take(plan, turn_order, axis=0)
    sel_all = plan_order[:, :cap_mid]
    live_two = plan_order[:, cap_mid : 2 * cap_mid]
    live_three = plan_order[:, 2 * cap_mid :]
    place_one = (blocks[:, :, None] * BLK + jnp.arange(BLK, dtype=jnp.int32)).reshape(ctx_count, tok_local)
    place_two = sum(
        jnp.where(sel_all // BLK == k, blocks[:, k : k + 1], 0) for k in range(per_device)
    ) * BLK + sel_all % BLK
    place_three = place_two[:, :cap_last]
    if near:
        mine = lambda v: v[0:1]
    else:
        mine = lambda v: lax.dynamic_slice_in_dim(v, here, 1, 0)
    sel_own, live2_own, live3_own = mine(sel_all), mine(live_two), mine(live_three)
    own_places = jnp.concatenate([mine(place_one), mine(place_two)], axis=1).reshape(-1, 1)
    frequency = ROPE_BASE ** (-jnp.arange(HEAD_SIZE // 2, dtype=F32) / (HEAD_SIZE // 2))
    angles = own_places.astype(F32) * frequency[None, :]
    cosine, sine = jnp.cos(angles), jnp.sin(angles)
    cosine = jnp.concatenate([cosine] * 4, axis=1)
    sine = jnp.concatenate([-sine, sine, -sine, sine], axis=1)
    tables = [
        (cosine[:tok_local], sine[:tok_local]),
        (cosine[tok_local:], sine[tok_local:]),
        (cosine[tok_local : tok_local + cap_last], sine[tok_local : tok_local + cap_last]),
    ]
    query_places = [
        own_places[:tok_local],
        own_places[tok_local:],
        own_places[tok_local : tok_local + cap_last],
    ]
    key_places = [v.reshape(1, -1) for v in (place_one, place_two, place_three)]
    key_live = [
        jnp.ones((1, ctx_count * tok_local), jnp.int32),
        live_two.reshape(1, -1),
        live_three.reshape(1, -1),
    ]
    prompt = ctx_count * tok_local // 2

    firsts, mixeds, seconds, hiddens = [], [], [], []
    records = []
    xs = [tok]
    first_in, query, kv = first_call(tok, gain1, *tables[0], wqkv)
    heights = []
    for step in range(3):
        part_a, part_b = gather_keys(kv, order, near, beside if step == 0 else ((), (), ()))
        weights, mixed = attend_call(
            query, part_a, part_b, key_places[step], key_live[step], query_places[step], prompt
        )
        firsts.append(first_in)
        if step == 0:
            extra = (sel_own, *tables[1])
            mixed, cot = order.take(mixed, cotangent[0])
            cot = relocate(cot)
            wo, wg, wu, wd = fetch_rest()
        elif step == 1:
            extra = (live2_own, *tables[2])
        else:
            extra = (sel_own, live2_own, live3_own, heights[0], heights[1])
        result = dense_call(
            near, step, xs[step], mixed, gain1, gain2, extra,
            (wo, wg, wu, wd) + ((wqkv,) if step < 2 else ()),
            (cap_mid, cap_last, tok_local)[step],
        )
        mixed_rows, middle, second, gate, up, hidden = result[:6]
        mixeds.append(mixed_rows)
        seconds.append(second)
        hiddens.append(hidden)
        records.append((query, part_a, part_b, weights, middle, gate, up))
        if step < 2:
            height, following, first_in, query, kv = result[6:]
            heights.append(height)
            xs.append(following)
        else:
            output = relocate(order.take(result[6]))

    d_firsts, d_seconds = [None] * 3, [None] * 3
    sums_one, sums_two = [], []
    slots = None
    parts, d_query, d_middle = (), None, None
    column = lambda rows, i: [r[i] for r in rows]
    courses = {}

    def begin(name, value, chain=block_sums):
        if near:
            courses[name] = Course(order, chain, value)
        else:
            courses[name] = value

    def step_of(*names):
        if near:
            for name in names:
                courses[name].step()

    def grads(kind, groups):
        return pair_sum(*grad_call(kind, block_coords, groups), near)

    for phase in range(4):
        step = 2 - phase
        before, into = (), ()
        if phase > 0:
            before = (gain1, *tables[step + 1], xs[step + 1], d_middle, d_query)
        if phase < 3:
            into = (gain2, *records[step][4:7])
        mats = (wd, wg, wu, wo)
        if phase == 0:
            extra, mats = (cot, sel_own, live3_own), mats
        elif phase == 1:
            extra, mats = (slots, live3_own, live2_own), (wqkv,) + mats
        elif phase == 2:
            extra, mats = (cot, sel_own, live2_own), (wqkv,) + mats
        else:
            extra, mats = (), (wqkv,)
        result = list(back_call(near, phase, before, parts, into, extra, mats, cap_mid))
        if phase > 0:
            d_firsts[step + 1], total = result[:2]
            sums_one.append(total)
            result = result[2:]
        if phase == 3:
            grad_tokens = result[0]
            break
        d_low, d_gate, d_up, d_middle, d_mid_low, d_mixed, total = result[:7]
        d_seconds[step] = (d_low, d_gate, d_up, d_mid_low)
        sums_two.append(total)
        if phase == 0:
            slots = result[7]
        elif phase == 1:
            output = order.take(output)
        else:
            begin("down", grads("rows", [hiddens, column(d_seconds, 0)]))
        d_mixed = order.take(d_mixed)
        query, part_a, part_b, weights = records[step][:4]
        d_query, term_a, term_b = attend_back_call(query, d_mixed, part_a, part_b, weights)
        if phase < 2:
            parts = scatter_keys(term_a, term_b, order, near)
        else:
            ready = {}

            def while_one():
                ready["gate"] = grads("cols", [seconds, order.take(*column(d_seconds, 1))])

            def while_two():
                ready["up"] = grads("cols", [seconds, order.take(*column(d_seconds, 2))])
                step_of("down")
                begin("gate", ready["gate"])

            parts = scatter_keys(term_a, term_b, order, near, while_one, while_two)

    rest = grads("mixed", [firsts, mixeds, d_firsts, column(d_seconds, 3)])
    sums = jnp.concatenate([sum(sums_one), sum(sums_two)], axis=0)
    begin("gains", sums, sums_by_hops)
    grad_tokens = relocate(grad_tokens)
    kv_width = key_weight.shape[1]
    hidden_width = w_gate.shape[1]
    placed = {}

    def place(name, kind, widths):
        got = courses[name]
        if near:
            got = got.result
        else:
            mine = lax.dynamic_index_in_dim(got, y, 1, keepdims=False)
            got = (mine[0], mine[1])
        where = order.token if near else block_coords
        placed[name] = order.take(*place_call(kind, where, *got, widths))

    step_of("down", "gains", "gate")
    begin("up", ready["up"])
    step_of("down", "gains", "gate", "down", "gains", "up")
    begin("rest", rest)
    step_of("gate", "gains", "down")
    grad_tokens = order.take(grad_tokens)
    step_of("up", "gate", "gains", "down")
    place("down", "rows", None)
    step_of("rest", "up", "gate", "rest", "up", "gate")
    place("gate", "cols", (hidden_width,))
    step_of("rest", "up", "rest", "up")
    place("up", "cols", (hidden_width,))
    step_of("rest", "rest")
    place("rest", "cols", (width, kv_width, width, kv_width))
    grad_down, grad_gate, grad_up = placed["down"].T, placed["gate"], placed["up"]
    grad_query, grad_key, grad_out, grad_value = placed["rest"]
    gain_sums = courses["gains"].result if near else lax.psum(sums, AXES)
    gain_sums = lax.dynamic_slice_in_dim(gain_sums, y * half, half, 1)
    return (
        output[None],
        grad_tokens[None],
        grad_query,
        grad_key,
        grad_value,
        grad_out,
        grad_gate,
        grad_up,
        grad_down,
        gain_sums[0],
        gain_sums[1],
    )


def solution(mesh):
    rows = P("ws", "ctx", None)
    flat = P("ws", None)
    in_specs = (rows, rows) + (flat,) * 7 + (P("ws"), P("ws"), P()) + (flat,) * 4
    out_specs = (rows, rows) + (flat,) * 7 + (P("ws"), P("ws"))
    return jax.shard_map(
        on_device, mesh=mesh, in_specs=in_specs, out_specs=out_specs, check_vma=False
    )
```

```python
import functools

import jax
import jax.numpy as jnp
from jax import lax
from jax.experimental import pallas as pl
from jax.experimental.pallas import tpu as pltpu
from jax.sharding import PartitionSpec as P

QUERY_HEADS = 15
KEY_VALUE_HEADS = 5
HEAD_SIZE = 64
SHARE = QUERY_HEADS // KEY_VALUE_HEADS
BLK = 64
CONT_BITS = 10
EPSILON = 1e-05
ROPE_BASE = 10000.0
MASK_FLOOR = -1e30
SCALE = HEAD_SIZE ** (-0.5)

BF = jnp.bfloat16
F32 = jnp.float32
AXES = ("ctx", "ws")
FF_CHUNKS = 4
MIB = 1024 * 1024

Y_BIT, C_BIT, X_BIT, Z1_BIT, Z2_BIT = 1, 2, 4, 8, 16
NEAR = (0, X_BIT, Y_BIT, Z1_BIT, X_BIT | Y_BIT | Z1_BIT, X_BIT | Y_BIT, Y_BIT | Z1_BIT, Z1_BIT | X_BIT)


def hop(value, mask):
    return lax.ppermute(value, AXES, [(i, i ^ mask) for i in range(32)])


def swap_place(i):
    y, z2 = i & 1, (i >> 4) & 1
    return (i & ~(Y_BIT | Z2_BIT)) | (Z2_BIT if y else 0) | (Y_BIT if z2 else 0)


def move(value):
    return lax.ppermute(value, AXES, [(i, swap_place(i)) for i in range(32)])


def ctx_mask(mask):
    return (
        (1 if mask & C_BIT else 0)
        | (2 if mask & X_BIT else 0)
        | (4 if mask & Z1_BIT else 0)
        | (8 if mask & Y_BIT else 0)
    )


NT = (((1,), (1,)), ((), ()))
TN = (((0,), (0,)), ((), ()))
NN = (((1,), (0,)), ((), ()))


def mm(left, right, dims=NN, precision=None):
    return lax.dot_general(left, right, dims, precision=precision, preferred_element_type=F32)


def normed_rows(values):
    inverse = lax.rsqrt(jnp.mean(values * values, axis=-1, keepdims=True) + EPSILON)
    return values * inverse, inverse


def norm_back(grad_in, normed, inverse, gain):
    scaled = grad_in * gain
    return inverse * (scaled - normed * jnp.mean(scaled * normed, axis=-1, keepdims=True))


def turn(values, cosine, sine, back=False):
    rows, width = values.shape
    lane = lax.broadcasted_iota(jnp.int32, (rows, 128), 1)
    first = (lane & (HEAD_SIZE - 1)) < HEAD_SIZE // 2
    if back:
        sine = -sine
    pieces = []
    for start in range(0, width, 128):
        wide = min(128, width - start)
        part = values[:, start : start + wide]
        if wide < 128:
            part = jnp.concatenate([part, jnp.zeros((rows, 128 - wide), F32)], axis=1)
        other = jnp.where(first, pltpu.roll(part, 96, 1), pltpu.roll(part, 32, 1))
        pieces.append((part * cosine + other * sine)[:, :wide])
    return jnp.concatenate(pieces, axis=1)


def vm():
    return pl.BlockSpec(memory_space=pltpu.VMEM)


def sm():
    return pl.BlockSpec(memory_space=pltpu.SMEM)


def hbm():
    return pl.BlockSpec(memory_space=pltpu.HBM)


def shaped(shape, dtype):
    return jax.ShapeDtypeStruct(shape, dtype)


def stored(shape, dtype):
    return pltpu.HBM(shape, dtype)


def apart(arrays):
    return [pltpu.with_memory_space_constraint(a, pltpu.HBM) for a in arrays]


def params(mib, **kw):
    return pltpu.CompilerParams(vmem_limit_bytes=mib * MIB, **kw)


def estimate(micros=1.0):
    return pl.CostEstimate(flops=0, bytes_accessed=int(micros * 3.7e6 / 4), transcendentals=0)


class Order:
    def __init__(self, token):
        self.token = token

    def all(self, *values):
        *values, self.token = lax.optimization_barrier(values + (self.token,))
        return values

    def take(self, *values):
        *values, self.token = lax.optimization_barrier(tuple(values) + (self.token,))
        return values[0] if len(values) == 1 else values


def read_coords(ref):
    return [ref[i] for i in range(4)]


class Weight:
    def __init__(self, shape, arrays, groups):
        self.shape, self.arrays, self.groups = shape, arrays, groups


def at_place(ref, place, rows, cols, coords):
    row, col = place(*coords)
    if rows != ref.shape[0] and not isinstance(row, int):
        row = pl.multiple_of(row, 16)
    if cols != ref.shape[1] and not isinstance(col, int):
        col = pl.multiple_of(col, 128)
    if cols == ref.shape[1]:
        return ref if rows == ref.shape[0] else ref.at[pl.ds(row, rows), :]
    return ref.at[pl.ds(row, rows), pl.ds(col, cols)]


def bring(weights, refs, buffers, sems, coords, turns, ahead=3):
    firsts, at = [], 0
    for weight in weights:
        firsts.append(at)
        at += len(weight.arrays)
    copies, count = {}, 0
    for which, group in turns:
        copies[which, group] = []
        for array, rows, cols, source, target in weights[which].groups[group]:
            copies[which, group].append(
                pltpu.make_async_copy(
                    at_place(refs[firsts[which] + array], source, rows, cols, coords),
                    at_place(buffers[which], target, rows, cols, coords),
                    sems.at[count],
                )
            )
            count += 1
    queue = list(turns)

    def start():
        if queue:
            for copy in copies[queue.pop(0)]:
                copy.start()

    for _ in range(ahead):
        start()

    def wait(which, group=0):
        for copy in copies[which, group]:
            copy.wait()
        start()

    return wait


def arrays_of(weights):
    return [a for w in weights for a in w.arrays]


def weights_in(near, weights):
    arrays = arrays_of(weights)
    if near:
        return [vm()] * len(arrays), arrays, []
    return [hbm()] * len(arrays), apart(arrays), scratch_of(weights)


def weights_here(near, weights, refs, scratch, coords_ref, turns):
    if near:
        return refs, lambda *which: None
    buffers, sems = scratch[: len(weights)], scratch[len(weights)]
    return buffers, bring(weights, refs, buffers, sems, read_coords(coords_ref), turns)


def join_kernel(weights, coords_ref, *args):
    count = len(arrays_of(weights))
    refs, outs, sems = args[:count], args[count:-1], args[-1]
    turns = [(i, g) for i, w in enumerate(weights) for g in range(len(w.groups))]
    wait = bring(weights, refs, outs, sems, read_coords(coords_ref), turns, len(turns))
    for turn in turns:
        wait(*turn)


def join_call(coords, weights):
    arrays = arrays_of(weights)
    joined = pl.pallas_call(
        functools.partial(join_kernel, weights),
        name="join_weights",
        out_shape=tuple(pltpu.VMEM(w.shape, BF) for w in weights),
        in_specs=[sm()] + [hbm()] * len(arrays),
        out_specs=tuple(vm() for _ in weights),
        scratch_shapes=scratch_of(weights)[-1:],
        compiler_params=params(24),
        cost_estimate=estimate(),
    )(coords, *apart(arrays))
    return tuple(one_piece(w) for w in joined)


def scratch_of(weights):
    copies = sum(len(g) for w in weights for g in w.groups)
    return [pltpu.VMEM(w.shape, BF) for w in weights] + [pltpu.SemaphoreType.DMA((copies,))]


def one_piece(array):
    rows, cols = array.shape
    origin = lambda *k: (0, 0)
    return Weight(array.shape, [array], [[(0, rows, cols, origin, origin)]])


def in_columns(array):
    rows, cols = array.shape
    wide = cols // FF_CHUNKS
    place = lambda j: (lambda *k: (0, j * wide))
    return Weight(
        array.shape, [array], [[(0, rows, wide, place(j), place(j))] for j in range(FF_CHUNKS)]
    )


def part_of(j, coords):
    rx, rz = BESIDE[j]
    return (coords[2] ^ rx) * 2 + ((coords[3] & 1) ^ rz)


BESIDE = ((0, 0), (1, 0), (0, 1), (1, 1))


def pack_kernel(coords_ref, q_hbm, k_hbm, v_hbm, own_ref, piece_ref, q_ref, k_ref, v_ref, sems):
    copies = [
        pltpu.make_async_copy(a, b, sems.at[i])
        for i, (a, b) in enumerate(((q_hbm, q_ref), (k_hbm, k_ref), (v_hbm, v_ref)))
    ]
    for copy in copies:
        copy.start()
    half, width = q_ref.shape
    kv_width = k_ref.shape[0]
    end = width + 2 * kv_width
    own_ref[:, end:] = jnp.zeros((half, own_ref.shape[1] - end), BF)
    for copy in copies:
        copy.wait()
    own_ref[:, :width] = q_ref[...]
    own_ref[:, width : width + kv_width] = k_ref[...].T
    own_ref[:, width + kv_width : end] = v_ref[...].T
    depth = half // 2
    start = pl.multiple_of(coords_ref[1] * depth, 16)
    piece_ref[...] = own_ref[pl.ds(start, depth), :]


def pack_call(coords, w_query, key_t, value_t):
    half, width = w_query.shape
    total = -(-(width + 2 * key_t.shape[0]) // 128) * 128
    return pl.pallas_call(
        pack_kernel,
        name="pack",
        out_shape=(stored((half, total), BF), shaped((half // 2, total), BF)),
        in_specs=[sm()] + [hbm()] * 3,
        out_specs=(vm(), vm()),
        scratch_shapes=[pltpu.VMEM(a.shape, BF) for a in (w_query, key_t, value_t)]
        + [pltpu.SemaphoreType.DMA((3,))],
        compiler_params=params(12),
        cost_estimate=estimate(),
    )(coords, *apart([w_query, key_t, value_t]))


def pack_rows_kernel(tokens_ref, plan_ref, out_ref):
    width, rows = tokens_ref.shape
    out_ref[:rows, :] = tokens_ref[...].T
    marks = plan_ref[...].astype(F32).astype(BF)
    out_ref[rows:, : marks.shape[1]] = marks
    out_ref[rows:, marks.shape[1] :] = jnp.zeros((marks.shape[0], width - marks.shape[1]), BF)


def pack_rows_call(tokens_t, plan):
    width, rows = tokens_t.shape
    return pl.pallas_call(
        pack_rows_kernel,
        name="pack_rows",
        out_shape=shaped((rows + plan.shape[0], width), BF),
        in_specs=[vm()] * 2,
        out_specs=vm(),
        compiler_params=params(8),
        cost_estimate=estimate(),
    )(*apart([tokens_t, plan]))


def stack_kernel(*refs):
    out_ref = refs[-1]
    at = 0
    for ref in refs[:-1]:
        out_ref[at : at + ref.shape[0], :] = ref[...]
        at += ref.shape[0]


def stack_call(pieces):
    rows = sum(p.shape[0] for p in pieces)
    return pl.pallas_call(
        stack_kernel,
        name="stack",
        out_shape=shaped((rows, pieces[0].shape[1]), pieces[0].dtype),
        in_specs=[vm()] * len(pieces),
        out_specs=vm(),
        compiler_params=params(8),
        cost_estimate=estimate(),
    )(*pieces)


def split_kernel(total_ref, other_ref, *outs):
    rows = outs[0].shape[0]
    for i, out in enumerate(outs):
        at = slice(i * rows, (i + 1) * rows)
        out[...] = (total_ref[at, :] + other_ref[at, :].astype(F32)).astype(out.dtype)


def split_call(total, other):
    rows, width = total.shape[0] // len(NEAR), total.shape[1]
    outs = [shaped((rows, width), F32)] + [shaped((rows, width), BF)] * (len(NEAR) - 1)
    return pl.pallas_call(
        split_kernel,
        name="split",
        out_shape=tuple(outs),
        in_specs=[vm(), vm()],
        out_specs=tuple(vm() for _ in outs),
        compiler_params=params(10),
        cost_estimate=estimate(),
    )(total, other)


def project(x, gain, wqkv_ref, cosine, sine, first_ref, q_ref, kv_ref):
    normed, _ = normed_rows(x)
    first_in = (normed * gain).astype(BF)
    first_ref[...] = first_in
    rows = mm(first_in, wqkv_ref[...])
    wide = SHARE * HEAD_SIZE
    q_width = KEY_VALUE_HEADS * wide
    kv_width = KEY_VALUE_HEADS * HEAD_SIZE
    key = turn(rows[:, q_width : q_width + kv_width], cosine, sine)
    value = rows[:, q_width + kv_width : q_width + 2 * kv_width]
    for h in range(KEY_VALUE_HEADS):
        at = slice(h * HEAD_SIZE, (h + 1) * HEAD_SIZE)
        kv_ref[:, h * 128 : (h + 1) * 128] = jnp.concatenate(
            [key[:, at], value[:, at]], axis=1
        ).astype(BF)
    query = (turn(rows[:, :q_width], cosine, sine).astype(BF) * SCALE).astype(BF)
    for h in range(KEY_VALUE_HEADS):
        q_ref[h] = query[:, h * wide : (h + 1) * wide]


def first_kernel(near, weights, coords_ref, x_ref, gain_ref, cos_ref, sin_ref, *rest):
    count = len(arrays_of(weights))
    refs, (first_ref, q_ref, kv_ref, *scratch) = rest[:count], rest[count:]
    (wqkv,), wait = weights_here(near, weights, refs, scratch, coords_ref, ((0, 0),))
    wait(0)
    project(
        x_ref[...].astype(F32), gain_ref[...], wqkv, cos_ref[...], sin_ref[...],
        first_ref, q_ref, kv_ref,
    )


def first_call(near, coords, tokens, gain, cosine, sine, weights):
    rows, width = tokens.shape
    specs, arrays, scratch = weights_in(near, weights)
    return pl.pallas_call(
        functools.partial(first_kernel, near, weights),
        name="first_projection",
        out_shape=(
            stored((rows, width), BF),
            shaped((KEY_VALUE_HEADS, rows, SHARE * HEAD_SIZE), BF),
            shaped((rows, KEY_VALUE_HEADS * 128), BF),
        ),
        in_specs=[sm()] + [vm()] * 4 + specs,
        out_specs=(vm(), vm(), vm()),
        scratch_shapes=scratch,
        compiler_params=params(10),
        cost_estimate=estimate(),
    )(coords, tokens, gain, cosine, sine, *arrays)


def padded_heads(wide_rows, left):
    rows = wide_rows.shape[0]
    blank = jnp.zeros((rows, HEAD_SIZE), wide_rows.dtype)
    stacked = []
    for j in range(SHARE):
        part = wide_rows[:, j * HEAD_SIZE : (j + 1) * HEAD_SIZE]
        stacked.append(jnp.concatenate([part, blank] if left else [blank, part], axis=1))
    return jnp.concatenate(stacked, axis=0)


def fill_bias(prompt, kpos_ref, live_ref, qpos_ref, bias_scr, col_scr):
    kpos = kpos_ref[...]
    klive = live_ref[...] > 0
    rows = bias_scr.shape[0]
    square = lambda axis: lax.broadcasted_iota(jnp.int32, (rows, rows), axis)
    own = jnp.where(square(0) == square(1), qpos_ref[...].astype(F32), 0.0)
    col_scr[...] = jnp.sum(own, axis=1, keepdims=True).astype(jnp.int32)
    kseg = jnp.where(kpos < prompt, 0, 1 + ((kpos - prompt) >> CONT_BITS))

    def fill(i, carry):
        at = pl.ds(pl.multiple_of(i * 8, 8), 8)
        qpos = col_scr[at, :]
        qseg = jnp.where(qpos < prompt, 0, 1 + ((qpos - prompt) >> CONT_BITS))
        earlier = kpos <= qpos
        shared = (kseg == 0) | (kseg == qseg)
        seen = earlier & shared & (klive | (kpos == qpos))
        bias_scr[at, :] = jnp.where(seen, 0.0, MASK_FLOOR)
        return carry

    lax.fori_loop(0, bias_scr.shape[0] // 8, fill, 0)


def attend_kernel(prompt, q_ref, a_ref, b_ref, kpos_ref, live_ref, qpos_ref, p_ref, o_ref, bias_scr, col_scr):
    @pl.when(pl.program_id(0) == 0)
    def _():
        fill_bias(prompt, kpos_ref, live_ref, qpos_ref, bias_scr, col_scr)

    o_ref[0] = attend_heads(q_ref, a_ref, b_ref, p_ref, bias_scr)


def attend_heads(q_ref, a_ref, b_ref, p_ref, bias_scr):
    rows = q_ref.shape[1]
    half = a_ref.shape[0]
    together = rows < 128
    if together:
        stacked = padded_heads(q_ref[0], True)
        all_a, all_b = mm(stacked, a_ref[...], NT), mm(stacked, b_ref[...], NT)
    blank = jnp.zeros((rows, HEAD_SIZE), BF)
    outs = []
    for j in range(SHARE):
        at = slice(j * rows, (j + 1) * rows)
        if together:
            s_a, s_b = all_a[at], all_b[at]
        else:
            part = jnp.concatenate([q_ref[0, :, j * HEAD_SIZE : (j + 1) * HEAD_SIZE], blank], axis=1)
            s_a, s_b = mm(part, a_ref[...], NT), mm(part, b_ref[...], NT)
        s_a = s_a + bias_scr[:, :half]
        s_b = s_b + bias_scr[:, half:]
        top = jnp.maximum(
            jnp.max(s_a, axis=-1, keepdims=True), jnp.max(s_b, axis=-1, keepdims=True)
        )
        w_a, w_b = jnp.exp(s_a - top), jnp.exp(s_b - top)
        mass = jnp.sum(w_a, axis=-1, keepdims=True) + jnp.sum(w_b, axis=-1, keepdims=True)
        inverse = 1.0 / mass
        p_a, p_b = (w_a * inverse).astype(BF), (w_b * inverse).astype(BF)
        p_ref[0, at, :half] = p_a
        p_ref[0, at, half:] = p_b
        if not together:
            outs.append((mm(p_a, a_ref[...]) + mm(p_b, b_ref[...]))[:, HEAD_SIZE:])
    if together:
        mixed = mm(p_ref[0, :, :half], a_ref[...]) + mm(p_ref[0, :, half:], b_ref[...])
        outs = [mixed[j * rows : (j + 1) * rows, HEAD_SIZE:] for j in range(SHARE)]
    return jnp.concatenate(outs, axis=1).astype(BF)


def attend_call(query, part_a, part_b, kpos, klive, qpos, prompt):
    heads, rows, wide = query.shape
    half = part_a.shape[0]
    keys = 2 * half
    return pl.pallas_call(
        functools.partial(attend_kernel, prompt),
        name="attend",
        grid=(heads,),
        out_shape=(stored((heads, SHARE * rows, keys), BF), shaped((heads, rows, wide), BF)),
        in_specs=[
            pl.BlockSpec((1, rows, wide), lambda h: (h, 0, 0)),
            pl.BlockSpec((half, 128), lambda h: (0, h)),
            pl.BlockSpec((half, 128), lambda h: (0, h)),
            pl.BlockSpec((1, keys), lambda h: (0, 0)),
            pl.BlockSpec((1, keys), lambda h: (0, 0)),
            pl.BlockSpec((1, rows), lambda h: (0, 0)),
        ],
        out_specs=(
            pl.BlockSpec((1, SHARE * rows, keys), lambda h: (h, 0, 0)),
            pl.BlockSpec((1, rows, wide), lambda h: (h, 0, 0)),
        ),
        scratch_shapes=[pltpu.VMEM((rows, keys), F32), pltpu.VMEM((rows, 1), jnp.int32)],
        compiler_params=params(12 if keys <= 2048 else 56, dimension_semantics=("arbitrary",)),
        cost_estimate=estimate(rows * keys / 17000),
    )(query, part_a, part_b, kpos, klive, qpos)


def attend_back_kernel(q_ref, do_ref, a_ref, b_ref, p_ref, dq_ref, da_ref, db_ref, dp_scr, ds_scr):
    rows = q_ref.shape[1]
    half = a_ref.shape[0]
    stacked = padded_heads(q_ref[0], True)
    grads = padded_heads(do_ref[0], False)
    dp_scr[:, :half] = mm(grads, a_ref[...], NT)
    dp_scr[:, half:] = mm(grads, b_ref[...], NT)

    for j in range(SHARE):
        at = slice(j * rows, (j + 1) * rows)
        weights = p_ref[0, at, :].astype(F32)
        dp = dp_scr[at, :]
        delta = jnp.sum(weights * dp, axis=-1, keepdims=True)
        ds_scr[at, :] = (weights * (dp - delta)).astype(BF)
    dq = (mm(ds_scr[:, :half], a_ref[...]) + mm(ds_scr[:, half:], b_ref[...])) * SCALE
    dq_ref[0] = jnp.concatenate(
        [dq[j * rows : (j + 1) * rows, :HEAD_SIZE] for j in range(SHARE)], axis=1
    )
    for at, out in ((slice(0, half), da_ref), (slice(half, 2 * half), db_ref)):
        turned = mm(stacked, ds_scr[:, at], TN) + mm(grads, p_ref[0, :, at], TN)
        out[...] = turned.T.astype(out.dtype)


def attend_back_call(query, d_out, part_a, part_b, weights):
    heads, rows, wide = query.shape
    half = part_a.shape[0]
    keys = 2 * half
    return pl.pallas_call(
        attend_back_kernel,
        name="attend_back",
        grid=(heads,),
        out_shape=(
            shaped((heads, rows, wide), F32),
            shaped((half, heads * 128), F32),
            shaped((half, heads * 128), BF),
        ),
        in_specs=[
            pl.BlockSpec((1, rows, wide), lambda h: (h, 0, 0)),
            pl.BlockSpec((1, rows, wide), lambda h: (h, 0, 0)),
            pl.BlockSpec((half, 128), lambda h: (0, h)),
            pl.BlockSpec((half, 128), lambda h: (0, h)),
            pl.BlockSpec((1, SHARE * rows, keys), lambda h: (h, 0, 0)),
        ],
        out_specs=(
            pl.BlockSpec((1, rows, wide), lambda h: (h, 0, 0)),
            pl.BlockSpec((half, 128), lambda h: (0, h)),
            pl.BlockSpec((half, 128), lambda h: (0, h)),
        ),
        scratch_shapes=[
            pltpu.VMEM((SHARE * rows, keys), F32),
            pltpu.VMEM((SHARE * rows, keys), BF),
        ],
        compiler_params=params(14 if keys <= 2048 else 60, dimension_semantics=("arbitrary",)),
        cost_estimate=estimate(rows * keys / 22000),
    )(query, d_out, part_a, part_b, *apart([weights]))


def picks(sel_ref, total_rows):
    capacity = sel_ref.shape[1]
    row = lax.broadcasted_iota(jnp.int32, (total_rows, capacity), 0)
    return row == sel_ref[...]


def live_column(live_ref, rows):
    count = jnp.sum(live_ref[:, :].astype(F32), axis=1, keepdims=True)
    return lax.broadcasted_iota(jnp.int32, (rows, 1), 0).astype(F32) < count


def feed_forward(wait, x, mixed, gain_two, wo, wg, wu, wd, ao_out, mid_ref, second_ref, g_ref, u_ref, hid_ref):
    ao_out[...] = mixed
    wait(0)
    middle = x + mm(mixed, wo[...])
    mid_ref[...] = middle
    normed, _ = normed_rows(middle)
    second = (normed * gain_two).astype(BF)
    second_ref[...] = second
    wide = wg.shape[1] // FF_CHUNKS
    for j in range(FF_CHUNKS):
        at = slice(j * wide, (j + 1) * wide)
        wait(1, j)
        g = mm(second, wg[:, at])
        wait(2, j)
        u = mm(second, wu[:, at])
        g_ref[:, at] = g.astype(BF)
        u_ref[:, at] = u.astype(BF)
        hid_ref[:, at] = (g / (1.0 + jnp.exp(-g)) * u).astype(BF)
    wait(3)
    return middle + mm(hid_ref[...], wd[...], NT)


DENSE_TURNS = ((0, 0),) + tuple((w, j) for j in range(FF_CHUNKS) for w in (1, 2)) + ((3, 0),)


def dense_body(near, step, weights, mixed, args):
    args = list(args)
    take = lambda k: [args.pop(0) for _ in range(k)]
    coords_ref, x_ref, gain1_ref, gain2_ref = take(4)
    if step == 0:
        sel_ref, cos_ref, sin_ref = take(3)
    elif step == 1:
        live_ref, cos_ref, sin_ref = take(3)
    else:
        sel_ref, live2_ref, live_ref, h1_ref, h2_ref = take(5)
    refs = take(len(arrays_of(weights)))
    ao_out, mid_ref, second_ref, g_ref, u_ref, hid_ref = take(6)
    if step < 2:
        h_ref, next_ref, first_ref, q_ref, kv_ref = take(5)
    else:
        (out_ref,) = take(1)
    turns = DENSE_TURNS + (((4, 0),) if step < 2 else ())

    def work():
        buffers, wait = weights_here(near, weights, refs, args, coords_ref, turns)
        rows = x_ref.shape[0]
        x = x_ref[...].astype(F32)
        updated = feed_forward(
            wait, x, mixed(), gain2_ref[...], *buffers[:4], ao_out, mid_ref,
            second_ref, g_ref, u_ref, hid_ref,
        )
        if step == 0:
            h_ref[...] = updated
            chosen = picks(sel_ref, rows).astype(F32)
            following = mm(chosen, updated, TN, lax.Precision.HIGHEST)
        else:
            updated = jnp.where(live_column(live_ref, rows), updated, x)
        if step == 1:
            h_ref[...] = updated
            following = updated[: next_ref.shape[0]]
        if step < 2:
            next_ref[...] = following
            wait(4)
            project(
                following, gain1_ref[...], buffers[4], cos_ref[...], sin_ref[...],
                first_ref, q_ref, kv_ref,
            )
        else:
            slots = jnp.concatenate([updated, h2_ref[rows:, :]], axis=0).astype(BF)
            hit = picks(sel_ref, h1_ref.shape[0]) & (live2_ref[...] > 0)
            placed = mm(hit.astype(BF), slots)
            any_hit = jnp.sum(hit.astype(F32), axis=1, keepdims=True) > 0.5
            out_ref[...] = jnp.where(any_hit, placed, h1_ref[...]).T.astype(BF)

    return work


def joined_heads(ao_ref):
    return jnp.concatenate([ao_ref[h] for h in range(KEY_VALUE_HEADS)], axis=1)


def dense_kernel(near, step, weights, ao_ref, *args):
    dense_body(near, step, weights, lambda: joined_heads(ao_ref), args)()


def dense_outs(step, x, weights, next_rows):
    rows, width = x.shape
    hidden = weights[1].shape[1]
    outs = [
        stored((rows, width), BF),
        stored((rows, width), F32),
        stored((rows, width), BF),
        stored((rows, hidden), BF),
        stored((rows, hidden), BF),
        stored((rows, hidden), BF),
    ]
    if step < 2:
        outs += [
            stored((rows, width), F32),
            shaped((next_rows, width), F32),
            stored((next_rows, width), BF),
            shaped((KEY_VALUE_HEADS, next_rows, SHARE * HEAD_SIZE), BF),
            shaped((next_rows, KEY_VALUE_HEADS * 128), BF),
        ]
    else:
        outs += [stored((width, next_rows), BF)]
    return outs


def dense_call(near, step, coords, x, mixed, gain1, gain2, extra, weights, next_rows):
    specs, arrays, scratch = weights_in(near, weights)
    outs = dense_outs(step, x, weights, next_rows)
    return pl.pallas_call(
        functools.partial(dense_kernel, near, step, weights),
        name=f"dense_{step}",
        out_shape=tuple(outs),
        in_specs=[vm(), sm()] + [vm()] * (3 + len(extra)) + specs,
        out_specs=tuple(vm() for _ in outs),
        scratch_shapes=scratch,
        compiler_params=params(12 if near else 50),
        cost_estimate=estimate(6),
    )(mixed, coords, x, gain1, gain2, *extra, *arrays)


def feed_back(wait, first, d_y, mid_ref, g_ref, u_ref, gain_two, wd, wg, wu, wo, dyb_ref, dg_ref, du_ref, dmid_ref, dz_ref, dao_ref, sum_ref):
    d_low = d_y.astype(BF)
    dyb_ref[...] = d_low
    wide = wg.shape[1] // FF_CHUNKS
    d_second = jnp.zeros(d_y.shape, F32)
    wait(first)
    for j in range(FF_CHUNKS):
        at = slice(j * wide, (j + 1) * wide)
        d_hidden = mm(d_low, wd[:, at])
        g, u = g_ref[:, at].astype(F32), u_ref[:, at].astype(F32)
        sigma = 1.0 / (1.0 + jnp.exp(-g))
        d_gate = (d_hidden * u * sigma * (1.0 + g * (1.0 - sigma))).astype(BF)
        d_up = (d_hidden * (g * sigma)).astype(BF)
        dg_ref[:, at] = d_gate
        du_ref[:, at] = d_up
        wait(first + 1, j)
        wait(first + 2, j)
        d_second += mm(d_gate, wg[:, at], NT) + mm(d_up, wu[:, at], NT)
    normed, inverse = normed_rows(mid_ref[...])
    sum_ref[...] = jnp.sum(d_second * normed, axis=0, keepdims=True)
    d_mid = norm_back(d_second, normed, inverse, gain_two) + d_y
    dmid_ref[...] = d_mid
    d_low = d_mid.astype(BF)
    dz_ref[...] = d_low
    wait(first + 3)
    d_mixed = mm(d_low, wo[...], NT).astype(BF)
    wide = SHARE * HEAD_SIZE
    for h in range(KEY_VALUE_HEADS):
        dao_ref[h] = d_mixed[:, h * wide : (h + 1) * wide]


def project_back(own_ref, others, dq_ref, x, dmid_ref, gain_one, cosine, sine, wait, wqkv, dqkv_ref, sum_ref):
    total = own_ref[...].astype(F32)
    for other in others:
        total = total + other[...].astype(F32)
    d_key = jnp.concatenate(
        [total[:, h * 128 : h * 128 + HEAD_SIZE] for h in range(KEY_VALUE_HEADS)], axis=1
    )
    d_value = jnp.concatenate(
        [total[:, h * 128 + HEAD_SIZE : (h + 1) * 128] for h in range(KEY_VALUE_HEADS)], axis=1
    )
    d_query = jnp.concatenate([dq_ref[h] for h in range(KEY_VALUE_HEADS)], axis=1)
    d_rows = jnp.concatenate(
        [turn(d_query, cosine, sine, True), turn(d_key, cosine, sine, True), d_value], axis=1
    ).astype(BF)
    dqkv_ref[...] = d_rows
    wait(0)
    d_first = mm(d_rows, wqkv[:, : d_rows.shape[1]], NT)
    normed, inverse = normed_rows(x)
    sum_ref[...] = jnp.sum(d_first * normed, axis=0, keepdims=True)
    return norm_back(d_first, normed, inverse, gain_one) + dmid_ref[...]


def back_kernel(near, phase, weights, n_parts, *args):
    args = list(args)
    take = lambda k: [args.pop(0) for _ in range(k)]
    (coords_ref,) = take(1)
    if phase > 0:
        gain1_ref, cos_ref, sin_ref, x_ref, dmid_in, dq_ref = take(6)
        own_ref, *others = take(n_parts)
    if phase < 3:
        gain2_ref, mid_ref, g_ref, u_ref = take(4)
    if phase == 0:
        cot_ref, sel_ref, live3_ref = take(3)
    elif phase == 1:
        slots_ref, live3_ref, live2_ref = take(3)
    elif phase == 2:
        cot_ref, sel_ref, live2_ref = take(3)
    refs = take(len(arrays_of(weights)))
    if phase > 0:
        dqkv_ref, sum1_ref = take(2)
    if phase < 3:
        outs = take(7)
    if phase == 0:
        (slots_out,) = take(1)
    elif phase == 3:
        (grad_ref,) = take(1)
    turns = ((0, 0),) if phase > 0 else ()
    first = len(turns)
    if phase < 3:
        turns += ((first, 0),)
        turns += tuple((first + w, j) for j in range(FF_CHUNKS) for w in (1, 2))
        turns += ((first + 3, 0),)
    buffers, wait = weights_here(near, weights, refs, args, coords_ref, turns)
    if phase > 0:
        d_x = project_back(
            own_ref, others, dq_ref, x_ref[...].astype(F32), dmid_in, gain1_ref[...],
            cos_ref[...], sin_ref[...], wait, buffers[0], dqkv_ref, sum1_ref,
        )
    if phase == 0:
        chosen = picks(sel_ref, cot_ref.shape[1]).astype(BF)
        slots = mm(chosen, cot_ref[...].T, TN)
        slots_out[...] = slots
        rows = mid_ref.shape[0]
        d_y = jnp.where(live_column(live3_ref, rows), slots[:rows], 0.0)
    elif phase == 1:
        rows = x_ref.shape[0]
        slots = slots_ref[...]
        head = jnp.where(live_column(live3_ref, rows), d_x, slots[:rows])
        slots = jnp.concatenate([head, slots[rows:]], axis=0)
        d_y = jnp.where(live_column(live2_ref, slots.shape[0]), slots, 0.0)
    elif phase == 2:
        hit = picks(sel_ref, cot_ref.shape[1]) & (live2_ref[...] > 0)
        placed = mm(hit.astype(F32), d_x, NN, lax.Precision.HIGHEST)
        any_hit = jnp.sum(hit.astype(F32), axis=1, keepdims=True) > 0.5
        d_y = jnp.where(any_hit, placed, cot_ref[...].astype(F32).T)
    else:
        grad_ref[...] = d_x.T.astype(BF)
        return
    feed_back(
        wait, first, d_y, mid_ref, g_ref, u_ref, gain2_ref[...],
        *buffers[first : first + 4], *outs,
    )


def back_call(near, phase, coords, before, parts, into, extra, weights, rows_next):
    specs, arrays, scratch = weights_in(near, weights)
    ins = list(before) + list(parts) + list(into) + list(extra)
    outs = []
    if phase > 0:
        rows, width = before[3].shape
        qkv_width = width + 2 * KEY_VALUE_HEADS * HEAD_SIZE
        outs += [stored((rows, qkv_width), BF), stored((1, width), F32)]
    if phase < 3:
        rows, hidden = into[2].shape
        width = into[1].shape[1]
        outs += [
            stored((rows, width), BF),
            stored((rows, hidden), BF),
            stored((rows, hidden), BF),
            stored((rows, width), F32),
            stored((rows, width), BF),
            shaped((KEY_VALUE_HEADS, rows, SHARE * HEAD_SIZE), BF),
            stored((1, width), F32),
        ]
    if phase == 0:
        outs += [stored((rows_next, width), F32)]
    elif phase == 3:
        outs += [stored((width, rows), BF)]
    return pl.pallas_call(
        functools.partial(back_kernel, near, phase, weights, len(parts)),
        name=f"back_{phase}",
        out_shape=tuple(outs),
        in_specs=[sm()] + [vm()] * len(ins) + specs,
        out_specs=tuple(vm() for _ in outs),
        scratch_shapes=scratch,
        compiler_params=params(12 if near else 50),
        cost_estimate=estimate(6),
    )(coords, *before, *parts, *into[:1], *apart(into[1:]), *extra, *arrays)


def stack_rows(refs, scratch):
    at = 0
    for ref in refs:
        scratch[at : at + ref.shape[0], :] = ref[...]
        at += ref.shape[0]


def put_blocks(value, x_of, coords, ref, per_row):
    y, _, x, z = coords
    depth = ref.shape[-2]
    for ya in range(2):
        for xa in range(2) if per_row else (None,):
            for za in range(4):
                row = (ya * (2 if per_row else 1) + (xa or 0)) * 4 + za
                ref[y ^ ya, (x ^ xa) if per_row else x_of, z ^ za] = value[
                    row * depth : (row + 1) * depth
                ].astype(BF)


def grad_cols_kernel(n_steps, coords_ref, *args):
    left, args = args[:n_steps], args[n_steps:]
    right, args = args[:n_steps], args[n_steps:]
    keep_ref, send_ref, l_scr, r_scr = args
    coords = read_coords(coords_ref)
    _, c, x, _ = coords
    stack_rows(left, l_scr)
    stack_rows(right, r_scr)
    block = keep_ref.shape[-1]
    for far, ref in ((1, send_ref), (0, keep_ref)):

        def body(rx, carry, far=far, ref=ref):
            start = pl.multiple_of(((c ^ far) * 2 + (x ^ rx)) * block, 128)
            value = mm(l_scr[...], r_scr[:, pl.ds(start, block)], TN)
            put_blocks(value, rx, coords, ref, False)
            return carry

        lax.fori_loop(0, 2, body, 0)


def grad_rows_kernel(n_steps, coords_ref, *args):
    left, args = args[:n_steps], args[n_steps:]
    right, args = args[:n_steps], args[n_steps:]
    keep_ref, send_ref, l_scr, r_scr = args
    coords = read_coords(coords_ref)
    y, c, x, z = coords
    stack_rows(left, l_scr)
    stack_rows(right, r_scr)
    depth = keep_ref.shape[-2]
    span = 8 * depth
    for far, ref in ((1, send_ref), (0, keep_ref)):

        def body(ry, carry, far=far, ref=ref):
            start = pl.multiple_of(((y ^ ry) * 2 + (c ^ far)) * span, 128)
            value = mm(l_scr[:, pl.ds(start, span)], r_scr[...], TN)
            for xa in range(2):
                for za in range(4):
                    row = (xa * 4 + za) * depth
                    ref[ry, x ^ xa, z ^ za] = value[row : row + depth].astype(BF)
            return carry

        lax.fori_loop(0, 2, body, 0)


def grad_mixed_kernel(n_steps, coords_ref, *args):
    groups = []
    for _ in range(4):
        groups.append(args[:n_steps])
        args = args[n_steps:]
    keep_ref, send_ref, first_scr, mixed_scr, qkv_scr, z_scr, val_scr = args
    coords = read_coords(coords_ref)
    _, c, x, _ = coords
    for refs, scr in zip(groups, (first_scr, mixed_scr, qkv_scr, z_scr), strict=True):
        stack_rows(refs, scr)
    block = keep_ref.shape[-1]
    width = z_scr.shape[1]
    kv_width = (qkv_scr.shape[1] - width) // 2
    for ca in range(2):
        for xa in range(2):
            if ca == 0:
                val_scr[...] = mm(first_scr[...], qkv_scr[:, xa * block : (xa + 1) * block], TN)
            elif xa == 0:
                val_scr[...] = mm(mixed_scr[...], z_scr[:, :block], TN)
            else:
                val_scr[...] = jnp.concatenate(
                    [
                        mm(mixed_scr[...], z_scr[:, block:], TN),
                        mm(first_scr[...], qkv_scr[:, width + kv_width :], TN),
                    ],
                    axis=1,
                )

            @pl.when(c == ca)
            def _(xa=xa):
                put_blocks(val_scr[...], x ^ xa, coords, keep_ref, False)

            @pl.when(c != ca)
            def _(xa=xa):
                put_blocks(val_scr[...], x ^ xa, coords, send_ref, False)


def grad_call(kind, coords, groups):
    n_steps = len(groups[0])
    rows = sum(a.shape[0] for a in groups[0])
    width, cols = groups[0][0].shape[1], groups[1][0].shape[1]
    scratch = [pltpu.VMEM((rows, g[0].shape[1]), BF) for g in groups]
    if kind == "rows":
        kernel, block = grad_rows_kernel, (width // 32, cols)
    elif kind == "cols":
        kernel, block = grad_cols_kernel, (width // 8, cols // 4)
    else:
        total = sum(g[0].shape[1] for g in groups[2:])
        kernel, block = grad_mixed_kernel, (width // 8, total // 4)
        scratch += [pltpu.VMEM((width, block[1]), F32)]
    out = shaped((2, 2, 4) + block, BF)
    ins = [a for g in groups for a in g]
    return pl.pallas_call(
        functools.partial(kernel, n_steps),
        name=f"grad_{kind}",
        out_shape=(out, out),
        in_specs=[sm()] + [vm()] * len(ins),
        out_specs=(vm(), vm()),
        scratch_shapes=scratch,
        compiler_params=params(16),
        cost_estimate=estimate(6),
    )(coords, *apart(ins))


def place_cols_kernel(coords_ref, near_ref, far_ref, *outs):
    _, c, x, _ = read_coords(coords_ref)
    block = near_ref.shape[-1]
    mixed = len(outs) > 1
    target = outs[4] if mixed else outs[0]
    for far, ref in ((0, near_ref), (1, far_ref)):
        for rx in range(2):
            cols = pl.ds(pl.multiple_of(((c ^ far) * 2 + (x ^ rx)) * block, 128), block)
            target[:, cols] = ref[rx, 0].astype(F32)
    if mixed:
        q_ref, k_ref, o_ref, v_ref, _, k_scr, v_scr = outs
        width, kv_width = q_ref.shape[1], k_ref.shape[0]
        depth = q_ref.shape[0]
        rows = pl.ds(pl.multiple_of((coords_ref[3] ^ pl.program_id(0)) * depth, 8), depth)
        q_ref[...] = target[:, :width]
        k_scr[rows, :] = target[:, width : width + kv_width]
        o_ref[...] = target[:, width + kv_width : 2 * width + kv_width]
        v_scr[rows, :] = target[:, 2 * width + kv_width :]

        @pl.when(pl.program_id(0) == 3)
        def _():
            k_ref[...] = k_scr[...].T
            v_ref[...] = v_scr[...].T


def place_rows_kernel(coords_ref, near_ref, far_ref, out_ref, scr):
    _, _, x, z = read_coords(coords_ref)
    depth = near_ref.shape[-2]

    def put(ref):
        for rx in range(2):
            for rz in range(4):
                row = pl.multiple_of(((x ^ rx) * 4 + (z ^ rz)) * depth, 8)
                scr[pl.ds(row, depth), :] = ref[rx, rz].astype(F32)

    @pl.when(pl.program_id(0) == 0)
    def _():
        put(near_ref)

    @pl.when(pl.program_id(0) == 1)
    def _():
        put(far_ref)

    out_ref[...] = scr[...].T


def place_call(kind, coords, near, far, widths):
    depth, block = near.shape[-2:]
    scratch = []
    if kind == "rows":
        kernel, grid = place_rows_kernel, (2,)
        outs = (stored((block, 16 * depth), F32),)
        source = pl.BlockSpec((2, 4, depth, block), lambda f, k: (0, 0, 0, 0))
        targets = (pl.BlockSpec((block, 8 * depth), lambda f, k: (0, k[1] ^ f)),)
        scratch = [pltpu.VMEM((8 * depth, block), F32)]
    else:
        kernel, grid = place_cols_kernel, (4,)
        source = pl.BlockSpec((2, 1, depth, block), lambda i, k: (0, i, 0, 0))
        straight = lambda w: (
            stored((4 * depth, w), F32), pl.BlockSpec((depth, w), lambda i, k: (k[3] ^ i, 0))
        )
        turned = lambda w: (
            stored((w, 4 * depth), F32), pl.BlockSpec((w, 4 * depth), lambda i, k: (0, 0))
        )
        outs, targets = zip(
            *((turned if i % 2 else straight)(w) for i, w in enumerate(widths)), strict=True
        )
        if len(outs) > 1:
            scratch = [pltpu.VMEM((depth, 4 * block), F32)]
            scratch += [pltpu.VMEM((4 * depth, w), F32) for w in widths[1::2]]
    return pl.pallas_call(
        kernel,
        name=f"place_{kind}",
        grid_spec=pltpu.PrefetchScalarGridSpec(
            num_scalar_prefetch=1,
            grid=grid,
            in_specs=[source, source],
            out_specs=targets,
            scratch_shapes=scratch,
        ),
        out_shape=outs,
        compiler_params=params(12),
        cost_estimate=estimate(),
    )(coords, near, far)


def low_sum(left, right):
    return (left.astype(F32) + right.astype(F32)).astype(BF)


def split_list(values, count):
    return values[:count], values[count:]


def gather_keys(kv, order, near, beside=((), ()), meanwhile=([], [])):
    if not near:
        whole = lax.all_gather(kv, "ctx", axis=0, tiled=True)
        half = whole.shape[0] // 2
        return whole[:half], whole[half:]
    kv = order.take(kv)
    hops = [hop(kv, m) for m in (X_BIT, Y_BIT, Z1_BIT, X_BIT | Y_BIT | Z1_BIT)]
    for start in beside[0]:
        start()
    (by_x, by_y, by_z, across), meanwhile[0][:] = split_list(order.all(*hops, *meanwhile[0]), 4)
    hops = [hop(by_x, Y_BIT), hop(by_y, Z1_BIT), hop(by_z, X_BIT)]
    for start in beside[1]:
        start()
    hops, meanwhile[1][:] = split_list(order.all(*hops, *meanwhile[1]), 3)
    part = stack_call([kv, by_x, by_y, by_z, across, *hops])
    return part, order.take(hop(part, C_BIT))


class KeySums:
    def __init__(self, own, others):
        self.own, self.others = own, others

    def sends(self, turn):
        return list(zip(self.others, NEAR[1:], strict=True))

    def got(self, turn, values):
        self.result = [self.own, *values]


class Hop:
    def __init__(self, value, mask):
        self.value, self.mask = value, mask

    def sends(self, turn):
        return [(self.value, self.mask)]

    def got(self, turn, values):
        (self.result,) = values


def scatter_keys(part_a, part_b, order, near):
    if not near:
        whole = jnp.concatenate([part_a, part_b.astype(F32)], axis=0)
        return [lax.psum_scatter(whole, "ctx", scatter_dimension=0, tiled=True)]
    far = Hop(part_b, C_BIT)
    (part_a,) = wave(order, [(far, 0)], lambda a: (a,), (part_a,))
    own, *others = split_call(part_a, far.result)
    sums = KeySums(own, others)
    wave(order, [(sums, 0)])
    return sums.result


def cut_rows(value, index, count):
    size = value.shape[0] // count
    return lax.dynamic_slice_in_dim(value, index * size, size, 0)


def cut_cols(value, index, count):
    size = value.shape[1] // count
    return lax.dynamic_slice_in_dim(value, index * size, size, 1)


def spread(mine):
    return mine, hop(mine, X_BIT), hop(mine, Z1_BIT), hop(mine, X_BIT | Z1_BIT)


def pair_sum(keep, send, near):
    if near:
        return low_sum(keep, hop(send, C_BIT))
    return lax.psum(jnp.stack([keep, send]).astype(F32), AXES)


ALONG_Z = (Z1_BIT, Z2_BIT, Z1_BIT | Z2_BIT)
FAR_FIRST = (2, 1, 0)


class BlockSums:
    rounds = 6

    def __init__(self, total):
        self.total = total

    def sends(self, turn):
        if turn == 0:
            return [(self.total[1, 1], Y_BIT)]
        if turn == 1:
            return [(self.total[1, 0], Y_BIT), (low_sum(self.total[0, 1], self.came), X_BIT)]
        if turn == 2:
            return [(self.total[i + 1], ALONG_Z[i]) for i in FAR_FIRST]
        if turn == 3:
            return [(self.mine, ALONG_Z[i]) for i in FAR_FIRST]
        if turn == 4:
            return [(self.total, X_BIT)]
        return [(self.total, C_BIT)]

    def got(self, turn, values):
        if turn == 0:
            (self.came,) = values
        elif turn == 1:
            total = self.total[0, 0].astype(F32)
            for value in values:
                total = total + value.astype(F32)
            self.total = total.astype(BF)
        elif turn == 2:
            mine = self.total[0].astype(F32)
            for value in values:
                mine = mine + value.astype(F32)
            self.mine = mine.astype(BF)
        elif turn == 3:
            self.total = jnp.stack([self.mine, *values[::-1]])
        elif turn == 4:
            self.total = jnp.stack([self.total, *values])
        else:
            self.result = (self.total, *values)


class RunningSum:
    rounds = 5

    def __init__(self, value):
        self.result = value

    def sends(self, turn):
        return [(self.result, (X_BIT, C_BIT, Y_BIT, Z1_BIT, Z2_BIT)[turn])]

    def got(self, turn, values):
        self.result = self.result + values[0]


class Move:
    rounds = 1

    def __init__(self, value):
        self.value = value

    def sends(self, turn):
        return [(self.value, None)]

    def got(self, turn, values):
        (self.result,) = values


def wave(order, steps, work=None, uses=()):
    plans = [chain.sends(turn) for chain, turn in steps]
    flat = [value for plan in plans for value, _ in plan]
    taken = order.all(*flat, *uses)
    sent, uses = taken[: len(flat)], taken[len(flat) :]
    masks = [mask for plan in plans for _, mask in plan]
    came = [move(v) if mask is None else hop(v, mask) for v, mask in zip(sent, masks, strict=True)]
    made = list(work(*uses)) if work else []
    came = order.all(*came, *made)
    came, made = came[: len(flat)], came[len(flat) :]
    for (chain, turn), plan in zip(steps, plans, strict=True):
        chain.got(turn, came[: len(plan)])
        came = came[len(plan) :]
    return made


def on_device(
    tokens, cotangent, w_query, key_weight, value_weight, w_out, w_gate, w_up, w_down,
    gain_attn, gain_ffn, block_order, sel_mid, live_mid, sel_last, live_last,
):
    ctx_count, ws_count = lax.axis_size("ctx"), lax.axis_size("ws")
    near = ctx_count == 16 and ws_count == 2
    ctx, y = lax.axis_index("ctx"), lax.axis_index("ws")
    tok_local = tokens.shape[1]
    cap_mid, cap_last = sel_mid.shape[1] // ctx_count, sel_last.shape[1] // ctx_count
    if near:
        c, x, z = ctx & 1, (ctx >> 1) & 1, ctx >> 2
        places = (y, c, x, z)
        here = (ctx & 7) | (y << 3)
        turn_order = here ^ jnp.array([ctx_mask(m) for m in NEAR] + [ctx_mask(m) | 1 for m in NEAR], jnp.int32)
        relocate = move
    else:
        zero = jnp.int32(0)
        places = (y, zero, zero, zero)
        here = ctx
        turn_order = jnp.arange(ctx_count, dtype=jnp.int32)
        relocate = lambda v: v
    coords = jnp.stack([jnp.asarray(v, jnp.int32) for v in places])
    block_coords = coords if near else jnp.zeros((4,), jnp.int32)
    width = tokens.shape[2]
    half = w_query.shape[0]
    plan = jnp.concatenate(
        [
            sel_mid.reshape(ctx_count, cap_mid),
            live_mid.reshape(ctx_count, cap_mid),
            live_last.reshape(ctx_count, cap_last),
        ],
        axis=1,
    )
    order = Order(coords)
    if near:
        assert tok_local <= 256
        own_qkv, piece = pack_call(coords, w_query, key_weight.T, value_weight.T)
        fetched = hop(piece, Y_BIT)
        tok = move(pack_rows_call(tokens[0].T, plan))
        gains = jnp.concatenate([gain_attn.reshape(1, -1), gain_ffn.reshape(1, -1)], axis=0)
        beyond = hop(gains, Y_BIT)
        quad = x * 2 + (z & 1)
        own_down = w_down.T
        fetched, cut_gate, cut_up, cut_out, cut_down = order.take(
            fetched,
            *(cut_cols(cut_rows(w, c, 2), quad, 4) for w in (w_gate, w_up)),
            cut_rows(w_out, c, 2),
            cut_rows(own_down, c, 2),
        )
        far = hop(fetched, C_BIT)
        gate_mine, up_mine = hop(cut_gate, Y_BIT), hop(cut_up, Y_BIT)
        out_mine, down_mine = hop(cut_out, Y_BIT), hop(cut_down, Y_BIT)
        far, tok, beyond = order.take(far, tok, beyond)
        plan = tok[tok_local:, : plan.shape[1]].astype(jnp.int32)
        tok = tok[:tok_local]
        depth = half // 2
        gains = jnp.where(
            y == 0,
            jnp.concatenate([gains, beyond], axis=1),
            jnp.concatenate([beyond, gains], axis=1),
        )
        gains = [gains[0:1], gains[1:2]]
        origin = lambda *k: (0, 0)

        def in_rows(own, mine, other):
            wide = own.shape[1]
            return Weight(
                (2 * half, wide),
                [own, mine, other],
                [
                    [
                        (0, half, wide, origin, lambda ky, kc, kx, kz: (ky * half, 0)),
                        (1, depth, wide, origin, lambda ky, kc, kx, kz: ((1 - ky) * half + kc * depth, 0)),
                        (2, depth, wide, origin, lambda ky, kc, kx, kz: ((1 - ky) * half + (1 - kc) * depth, 0)),
                    ]
                ],
            )

        def in_parts(own, mine, other):
            wide = mine.shape[1]
            groups = []
            for j in range(FF_CHUNKS):
                column = lambda *k, j=j: part_of(j, k) * wide
                block = lambda *k, j=j: (j * depth, 0)
                groups.append(
                    [
                        (0, half, wide,
                         lambda *k, column=column: (0, column(*k)),
                         lambda *k, column=column: (k[0] * half, column(*k))),
                        (1, depth, wide, block,
                         lambda *k, column=column: ((1 - k[0]) * half + k[1] * depth, column(*k))),
                        (2, depth, wide, block,
                         lambda *k, column=column: ((1 - k[0]) * half + (1 - k[1]) * depth, column(*k))),
                    ]
                )
            return Weight((2 * half, own.shape[1]), [own, mine, other], groups)

        (weight_qkv,) = join_call(coords, (in_rows(own_qkv, fetched, far),))
        state, marks = {}, {}

        def start_gate():
            state["gate"] = spread(order.take(gate_mine))

        def start_up():
            state["up"] = spread(order.take(up_mine))

        beside = ((start_gate,), (start_up,))

        def fetch_rest():
            gate = stack_call(order.take(*state["gate"]))
            out, down = order.take(out_mine, down_mine)
            fars = [hop(v, C_BIT) for v in (gate, out, down)]
            up = stack_call(order.take(*state["up"]))
            gate_far, out_far, down_far, up_far = order.take(*fars, hop(up, C_BIT))
            wide = own_down.shape[1]
            weight_d = Weight(
                (width, 2 * wide),
                [own_down, down, down_far],
                [
                    [
                        (0, width, wide, origin, lambda ky, kc, kx, kz: (0, ky * wide)),
                        (1, width // 2, wide, origin, lambda ky, kc, kx, kz: (kc * (width // 2), (1 - ky) * wide)),
                        (2, width // 2, wide, origin, lambda ky, kc, kx, kz: ((1 - kc) * (width // 2), (1 - ky) * wide)),
                    ]
                ],
            )
            return join_call(
                coords,
                (
                    in_rows(w_out, out, out_far),
                    in_parts(w_gate, gate, gate_far),
                    in_parts(w_up, up, up_far),
                    weight_d,
                ),
            )
    else:
        tok = tokens[0]
        whole = lambda w: lax.all_gather(w, "ws", axis=0, tiled=True)
        weight_qkv = one_piece(whole(jnp.concatenate([w_query, key_weight, value_weight], axis=1)))
        gains = [whole(g).reshape(1, -1) for g in (gain_attn, gain_ffn)]
        far_weights = (
            one_piece(whole(w_out)), in_columns(whole(w_gate)), in_columns(whole(w_up)),
            one_piece(whole(w_down).T),
        )
        beside, fetch_rest = ((), ()), lambda: far_weights
    gain1, gain2 = (g.astype(F32) for g in gains)

    per_device = tok_local // BLK
    blocks = jnp.take(block_order.reshape(ctx_count, per_device), turn_order, axis=0)
    plan_order = jnp.take(plan, turn_order, axis=0)
    sel_all = plan_order[:, :cap_mid]
    live_two = plan_order[:, cap_mid : 2 * cap_mid]
    live_three = plan_order[:, 2 * cap_mid :]
    place_one = (blocks[:, :, None] * BLK + jnp.arange(BLK, dtype=jnp.int32)).reshape(ctx_count, tok_local)
    place_two = sum(
        jnp.where(sel_all // BLK == k, blocks[:, k : k + 1], 0) for k in range(per_device)
    ) * BLK + sel_all % BLK
    place_three = place_two[:, :cap_last]
    if near:
        mine = lambda v: v[0:1]
    else:
        mine = lambda v: lax.dynamic_slice_in_dim(v, here, 1, 0)
    sel_own, live2_own, live3_own = mine(sel_all), mine(live_two), mine(live_three)
    own_places = jnp.concatenate([mine(place_one), mine(place_two)], axis=1).reshape(-1, 1)
    frequency = ROPE_BASE ** (-jnp.arange(HEAD_SIZE // 2, dtype=F32) / (HEAD_SIZE // 2))
    angles = own_places.astype(F32) * frequency[None, :]
    cosine, sine = jnp.cos(angles), jnp.sin(angles)
    cosine = jnp.concatenate([cosine] * 4, axis=1)
    sine = jnp.concatenate([-sine, sine, -sine, sine], axis=1)
    tables = [
        (cosine[:tok_local], sine[:tok_local]),
        (cosine[tok_local:], sine[tok_local:]),
        (cosine[tok_local : tok_local + cap_last], sine[tok_local : tok_local + cap_last]),
    ]
    query_places = [mine(v) for v in (place_one, place_two, place_three)]
    key_places = [v.reshape(1, -1) for v in (place_one, place_two, place_three)]
    key_live = [
        jnp.ones((1, ctx_count * tok_local), jnp.int32),
        live_two.reshape(1, -1),
        live_three.reshape(1, -1),
    ]
    prompt = ctx_count * tok_local // 2
    if near:
        key_places[0], query_places[0] = order.take(key_places[0], query_places[0])
        marks["places"] = [*query_places[1:], *key_places[1:], *key_live[1:], sel_own, live2_own, live3_own]
        marks["tables"] = [*tables[1], *tables[2]]

    firsts, mixeds, seconds, hiddens = [], [], [], []
    records = []
    xs = [tok]
    first_in, query, kv = first_call(near, coords, tok, gain1, *tables[0], (weight_qkv,))
    heights = []
    for step in range(3):
        if near and step == 0:
            waits = (marks["places"], marks["tables"])
            part_a, part_b = gather_keys(kv, order, near, beside, waits)
        else:
            part_a, part_b = gather_keys(kv, order, near)
        if near and step == 1:
            query_places[1:], key_places[1:], key_live[1:] = (marks["places"][i : i + 2] for i in (0, 2, 4))
        firsts.append(first_in)
        next_rows = (cap_mid, cap_last, tok_local)[step]
        attention = (query, part_a, part_b, key_places[step], key_live[step], query_places[step], prompt)
        weights, mixed = attend_call(*attention)
        if step == 0:
            mixed = order.take(mixed)
            dense_weights = fetch_rest()
            if near:
                sel_own, live2_own, live3_own = marks["places"][6:]
                tables[1:] = [marks["tables"][:2], marks["tables"][2:]]
        if step == 1:
            mixed, cot = order.take(mixed, cotangent[0].T)
            cot = relocate(cot)
        if step == 0:
            extra = (sel_own, *tables[1])
        elif step == 1:
            extra = (live2_own, *tables[2])
        else:
            extra = (sel_own, live2_own, live3_own, heights[0], heights[1])
        mats = dense_weights + ((weight_qkv,) if step < 2 else ())
        result = dense_call(
            near, step, coords, xs[step], mixed, gain1, gain2, extra, mats, next_rows
        )
        mixed_rows, middle, second, gate, up, hidden = result[:6]
        mixeds.append(mixed_rows)
        seconds.append(second)
        hiddens.append(hidden)
        records.append((query, part_a, part_b, weights, middle, gate, up))
        if step < 2:
            height, following, first_in, query, kv = result[6:]
            if step == 1:
                following, cot = order.take(following, cot)
            heights.append(height)
            xs.append(following)
        else:
            output = relocate(order.take(result[6]))

    d_firsts, d_seconds = [None] * 3, [None] * 3
    sums_one, sums_two = [], []
    slots = None
    parts, d_query, d_middle = (), None, None
    column = lambda rows, i: [r[i] for r in rows]

    def grads(kind, groups):
        return grad_call(kind, block_coords, groups)

    for phase in range(4):
        step = 2 - phase
        before, into = (), ()
        if phase > 0:
            before = (gain1, *tables[step + 1], xs[step + 1], d_middle, d_query)
        if phase < 3:
            into = (gain2, *records[step][4:7])
        mats = (dense_weights[3], dense_weights[1], dense_weights[2], dense_weights[0])
        if phase == 0:
            extra, mats = (cot, sel_own, live3_own), mats
        elif phase == 1:
            extra, mats = (slots, live3_own, live2_own), (weight_qkv,) + mats
        elif phase == 2:
            extra, mats = (cot, sel_own, live2_own), (weight_qkv,) + mats
        else:
            extra, mats = (), (weight_qkv,)
        result = list(back_call(near, phase, coords, before, parts, into, extra, mats, cap_mid))
        if phase > 0:
            d_firsts[step + 1], total = result[:2]
            sums_one.append(total)
            result = result[2:]
        if phase == 3:
            grad_tokens = result[0]
            break
        d_low, d_gate, d_up, d_middle, d_mid_low, d_mixed, total = result[:7]
        d_seconds[step] = (d_low, d_gate, d_up, d_mid_low)
        sums_two.append(total)
        if phase == 0:
            slots = result[7]
        query, part_a, part_b, weights = records[step][:4]
        if phase < 2:
            d_mixed = order.take(d_mixed)
            d_query, term_a, term_b = attend_back_call(query, d_mixed, part_a, part_b, weights)
            if phase == 0:
                output, term_b = order.take(output, term_b)
            parts = scatter_keys(term_a, term_b, order, near)

        else:
            attend_last = lambda d: attend_back_call(query, d, part_a, part_b, weights)
            gate_grads = lambda *d: grads("cols", [seconds, list(d)])
            down_grads = grads("rows", [hiddens, column(d_seconds, 0)])
            if not near:
                d_query, term_a, term_b = attend_last(d_mixed)
                parts = scatter_keys(term_a, term_b, order, near)
                sums_of = [
                    pair_sum(*g, near)
                    for g in (down_grads, gate_grads(*column(d_seconds, 1)), gate_grads(*column(d_seconds, 2)))
                ]
                continue
            down = Hop(down_grads[1], C_BIT)
            gate_grads_made = wave(
                order, [(down, 0)], gate_grads, column(d_seconds, 1)
            )
            down = BlockSums(low_sum(down_grads[0], down.result))
            gate = Hop(gate_grads_made[1], C_BIT)
            d_query, term_a, term_b = wave(order, [(down, 0), (gate, 0)], attend_last, (d_mixed,))
            gate = BlockSums(low_sum(gate_grads_made[0], gate.result))
            far = Hop(term_b, C_BIT)
            up_made = wave(order, [(down, 1), (far, 0)], gate_grads, column(d_seconds, 2))
            own, *others = split_call(term_a, far.result)
            keys, up = KeySums(own, others), Hop(up_made[1], C_BIT)
            wave(order, [(keys, 0), (up, 0)])
            up = BlockSums(low_sum(up_made[0], up.result))
            parts = keys.result

    kv_width = key_weight.shape[1]
    hidden_width = w_gate.shape[1]
    mixed_grads = lambda *d: grads("mixed", [firsts, mixeds, list(d), column(d_seconds, 3)])
    sums = jnp.concatenate([sum(sums_one), sum(sums_two)], axis=0)
    placed = {}

    if near:
        def place(kind, widths):
            return lambda near_blocks, far_blocks, at: place_call(kind, at, near_blocks, far_blocks, widths)

        placing = lambda chain: (*chain.result, coords)
        rest_made = wave(order, [(gate, 0), (down, 2)], mixed_grads, d_firsts)
        rest, gains_sum = Hop(rest_made[1], C_BIT), RunningSum(sums)
        wave(order, [(gate, 1), (down, 3), (rest, 0)])
        rest = BlockSums(low_sum(rest_made[0], rest.result))
        wave(order, [(up, 0), (gate, 2), (down, 4)])
        wave(order, [(up, 1), (gate, 3), (down, 5)])
        placed["down"] = wave(
            order, [(rest, 0), (up, 2), (gate, 4)], place("rows", None), placing(down)
        )
        wave(order, [(rest, 1), (up, 3), (gate, 5), (gains_sum, 1)])
        placed["gate"] = wave(
            order, [(rest, 2), (up, 4)], place("cols", (hidden_width,)), placing(gate)
        )
        tokens_back = Move(grad_tokens)
        wave(order, [(rest, 3), (up, 5), (gains_sum, 0)])
        placed["up"] = wave(
            order, [(rest, 4), (gains_sum, 2), (tokens_back, 0)], place("cols", (hidden_width,)), placing(up)
        )
        grad_tokens = tokens_back.result.astype(F32)
        wave(order, [(rest, 5), (gains_sum, 3)])
        wave(order, [(gains_sum, 4)])
        placed["rest"] = order.all(
            *place("cols", (width, kv_width, width, kv_width))(*rest.result, order.token)
        )
        for name in ("down", "gate", "up"):
            (placed[name],) = placed[name]
        gain_sums = gains_sum.result
    else:
        sums_of.append(pair_sum(*mixed_grads(*d_firsts), near))
        for name, kind, widths, total in zip(
            ("down", "gate", "up", "rest"),
            ("rows", "cols", "cols", "cols"),
            (None, (hidden_width,), (hidden_width,), (width, kv_width, width, kv_width)),
            sums_of,
            strict=True,
        ):
            mine = lax.dynamic_index_in_dim(total, y, 1, keepdims=False)
            placed[name] = place_call(kind, block_coords, mine[0], mine[1], widths)
        for name in ("down", "gate", "up"):
            (placed[name],) = placed[name]
        gain_sums = lax.psum(sums, AXES)
        grad_tokens = grad_tokens.astype(F32)
    grad_down, grad_gate, grad_up = placed["down"].T, placed["gate"], placed["up"]
    grad_query, grad_key, grad_out, grad_value = placed["rest"]
    grad_key, grad_value = grad_key.T, grad_value.T
    gain_sums = lax.dynamic_slice_in_dim(gain_sums, y * half, half, 1)
    return (
        output.T[None],
        grad_tokens.T[None],
        grad_query,
        grad_key,
        grad_value,
        grad_out,
        grad_gate,
        grad_up,
        grad_down,
        gain_sums[0],
        gain_sums[1],
    )


def solution(mesh):
    rows = P("ws", "ctx", None)
    flat = P("ws", None)
    in_specs = (rows, rows) + (flat,) * 7 + (P("ws"), P("ws"), P()) + (flat,) * 4
    out_specs = (rows, rows) + (flat,) * 7 + (P("ws"), P("ws"))
    return jax.shard_map(
        on_device, mesh=mesh, in_specs=in_specs, out_specs=out_specs, check_vma=False
    )
```

```python
import functools

import jax
import jax.numpy as jnp
from jax import lax
from jax.experimental import pallas as pl
from jax.experimental.pallas import tpu as pltpu
from jax.sharding import PartitionSpec as P

QUERY_HEADS = 15
KEY_VALUE_HEADS = 5
HEAD_SIZE = 64
SHARE = QUERY_HEADS // KEY_VALUE_HEADS
BLK = 64
CONT_BITS = 10
EPSILON = 1e-05
ROPE_BASE = 10000.0
MASK_FLOOR = -1e30
SCALE = HEAD_SIZE ** (-0.5)

BF = jnp.bfloat16
F32 = jnp.float32
AXES = ("ctx", "ws")
FF_CHUNKS = 4
MIB = 1024 * 1024

Y_BIT, C_BIT, X_BIT, Z1_BIT, Z2_BIT = 1, 2, 4, 8, 16
NEAR = (0, X_BIT, Y_BIT, Z1_BIT, X_BIT | Y_BIT | Z1_BIT, X_BIT | Y_BIT, Y_BIT | Z1_BIT, Z1_BIT | X_BIT)


def hop(value, mask):
    return lax.ppermute(value, AXES, [(i, i ^ mask) for i in range(32)])


def swap_place(i):
    y, z2 = i & 1, (i >> 4) & 1
    return (i & ~(Y_BIT | Z2_BIT)) | (Z2_BIT if y else 0) | (Y_BIT if z2 else 0)


def move(value):
    return lax.ppermute(value, AXES, [(i, swap_place(i)) for i in range(32)])


def ctx_mask(mask):
    return (
        (1 if mask & C_BIT else 0)
        | (2 if mask & X_BIT else 0)
        | (4 if mask & Z1_BIT else 0)
        | (8 if mask & Y_BIT else 0)
    )


NT = (((1,), (1,)), ((), ()))
TN = (((0,), (0,)), ((), ()))
NN = (((1,), (0,)), ((), ()))


def mm(left, right, dims=NN, precision=None):
    return lax.dot_general(left, right, dims, precision=precision, preferred_element_type=F32)


def normed_rows(values):
    inverse = lax.rsqrt(jnp.mean(values * values, axis=-1, keepdims=True) + EPSILON)
    return values * inverse, inverse


def norm_back(grad_in, normed, inverse, gain):
    scaled = grad_in * gain
    return inverse * (scaled - normed * jnp.mean(scaled * normed, axis=-1, keepdims=True))


def turn(values, cosine, sine, back=False):
    rows, width = values.shape
    lane = lax.broadcasted_iota(jnp.int32, (rows, 128), 1)
    first = (lane & (HEAD_SIZE - 1)) < HEAD_SIZE // 2
    if back:
        sine = -sine
    pieces = []
    for start in range(0, width, 128):
        wide = min(128, width - start)
        part = values[:, start : start + wide]
        if wide < 128:
            part = jnp.concatenate([part, jnp.zeros((rows, 128 - wide), F32)], axis=1)
        other = jnp.where(first, pltpu.roll(part, 96, 1), pltpu.roll(part, 32, 1))
        pieces.append((part * cosine + other * sine)[:, :wide])
    return jnp.concatenate(pieces, axis=1)


def vm():
    return pl.BlockSpec(memory_space=pltpu.VMEM)


def sm():
    return pl.BlockSpec(memory_space=pltpu.SMEM)


def hbm():
    return pl.BlockSpec(memory_space=pltpu.HBM)


def shaped(shape, dtype):
    return jax.ShapeDtypeStruct(shape, dtype)


def stored(shape, dtype):
    return pltpu.HBM(shape, dtype)


def apart(arrays):
    return [pltpu.with_memory_space_constraint(a, pltpu.HBM) for a in arrays]


def params(mib, **kw):
    return pltpu.CompilerParams(vmem_limit_bytes=mib * MIB, **kw)


def estimate(micros=1.0):
    return pl.CostEstimate(flops=0, bytes_accessed=int(micros * 3.7e6 / 4), transcendentals=0)


class Order:
    def __init__(self, token):
        self.token = token

    def all(self, *values):
        *values, self.token = lax.optimization_barrier(values + (self.token,))
        return values

    def take(self, *values):
        *values, self.token = lax.optimization_barrier(tuple(values) + (self.token,))
        return values[0] if len(values) == 1 else values


def read_coords(ref):
    return [ref[i] for i in range(4)]


class Weight:
    def __init__(self, shape, arrays, groups):
        self.shape, self.arrays, self.groups = shape, arrays, groups


def at_place(ref, place, rows, cols, coords):
    row, col = place(*coords)
    if rows != ref.shape[0] and not isinstance(row, int):
        row = pl.multiple_of(row, 16)
    if cols != ref.shape[1] and not isinstance(col, int):
        col = pl.multiple_of(col, 128)
    if cols == ref.shape[1]:
        return ref if rows == ref.shape[0] else ref.at[pl.ds(row, rows), :]
    return ref.at[pl.ds(row, rows), pl.ds(col, cols)]


def bring(weights, refs, buffers, sems, coords, turns, ahead=3):
    firsts, at = [], 0
    for weight in weights:
        firsts.append(at)
        at += len(weight.arrays)
    copies, count = {}, 0
    for which, group in turns:
        copies[which, group] = []
        for array, rows, cols, source, target in weights[which].groups[group]:
            copies[which, group].append(
                pltpu.make_async_copy(
                    at_place(refs[firsts[which] + array], source, rows, cols, coords),
                    at_place(buffers[which], target, rows, cols, coords),
                    sems.at[count],
                )
            )
            count += 1
    queue = list(turns)

    def start():
        if queue:
            for copy in copies[queue.pop(0)]:
                copy.start()

    for _ in range(ahead):
        start()

    def wait(which, group=0):
        for copy in copies[which, group]:
            copy.wait()
        start()

    return wait


def arrays_of(weights):
    return [a for w in weights for a in w.arrays]


def weights_in(near, weights):
    arrays = arrays_of(weights)
    if near:
        return [vm()] * len(arrays), arrays, []
    return [hbm()] * len(arrays), apart(arrays), scratch_of(weights)


def weights_here(near, weights, refs, scratch, coords_ref, turns):
    if near:
        return refs, lambda *which: None
    buffers, sems = scratch[: len(weights)], scratch[len(weights)]
    return buffers, bring(weights, refs, buffers, sems, read_coords(coords_ref), turns)


def join_kernel(weights, coords_ref, *args):
    count = len(arrays_of(weights))
    refs, outs, sems = args[:count], args[count:-1], args[-1]
    turns = [(i, g) for i, w in enumerate(weights) for g in range(len(w.groups))]
    wait = bring(weights, refs, outs, sems, read_coords(coords_ref), turns, len(turns))
    for turn in turns:
        wait(*turn)


def join_call(coords, weights):
    arrays = arrays_of(weights)
    joined = pl.pallas_call(
        functools.partial(join_kernel, weights),
        name="join_weights",
        out_shape=tuple(pltpu.VMEM(w.shape, BF) for w in weights),
        in_specs=[sm()] + [hbm()] * len(arrays),
        out_specs=tuple(vm() for _ in weights),
        scratch_shapes=scratch_of(weights)[-1:],
        compiler_params=params(24),
        cost_estimate=estimate(),
    )(coords, *apart(arrays))
    return tuple(one_piece(w) for w in joined)


def scratch_of(weights):
    copies = sum(len(g) for w in weights for g in w.groups)
    return [pltpu.VMEM(w.shape, BF) for w in weights] + [pltpu.SemaphoreType.DMA((copies,))]


def one_piece(array):
    rows, cols = array.shape
    origin = lambda *k: (0, 0)
    return Weight(array.shape, [array], [[(0, rows, cols, origin, origin)]])


def in_columns(array):
    rows, cols = array.shape
    wide = cols // FF_CHUNKS
    place = lambda j: (lambda *k: (0, j * wide))
    return Weight(
        array.shape, [array], [[(0, rows, wide, place(j), place(j))] for j in range(FF_CHUNKS)]
    )


def part_of(j, coords):
    rx, rz = BESIDE[j]
    return (coords[2] ^ rx) * 2 + ((coords[3] & 1) ^ rz)


BESIDE = ((0, 0), (1, 0), (0, 1), (1, 1))


def pack_kernel(coords_ref, q_hbm, k_hbm, v_hbm, own_ref, piece_ref, q_ref, k_ref, v_ref, sems):
    copies = [
        pltpu.make_async_copy(a, b, sems.at[i])
        for i, (a, b) in enumerate(((q_hbm, q_ref), (k_hbm, k_ref), (v_hbm, v_ref)))
    ]
    for copy in copies:
        copy.start()
    half, width = q_ref.shape
    kv_width = k_ref.shape[0]
    end = width + 2 * kv_width
    own_ref[:, end:] = jnp.zeros((half, own_ref.shape[1] - end), BF)
    for copy in copies:
        copy.wait()
    own_ref[:, :width] = q_ref[...]
    own_ref[:, width : width + kv_width] = k_ref[...].T
    own_ref[:, width + kv_width : end] = v_ref[...].T
    depth = half // 2
    start = pl.multiple_of(coords_ref[1] * depth, 16)
    piece_ref[...] = own_ref[pl.ds(start, depth), :]


def pack_call(coords, w_query, key_t, value_t):
    half, width = w_query.shape
    total = -(-(width + 2 * key_t.shape[0]) // 128) * 128
    return pl.pallas_call(
        pack_kernel,
        name="pack",
        out_shape=(stored((half, total), BF), shaped((half // 2, total), BF)),
        in_specs=[sm()] + [hbm()] * 3,
        out_specs=(vm(), vm()),
        scratch_shapes=[pltpu.VMEM(a.shape, BF) for a in (w_query, key_t, value_t)]
        + [pltpu.SemaphoreType.DMA((3,))],
        compiler_params=params(12),
        cost_estimate=estimate(),
    )(coords, *apart([w_query, key_t, value_t]))


def pack_rows_kernel(tokens_ref, plan_ref, out_ref):
    width, rows = tokens_ref.shape
    out_ref[:rows, :] = tokens_ref[...].T
    marks = plan_ref[...].astype(F32).astype(BF)
    out_ref[rows:, : marks.shape[1]] = marks
    out_ref[rows:, marks.shape[1] :] = jnp.zeros((marks.shape[0], width - marks.shape[1]), BF)


def pack_rows_call(tokens_t, plan):
    width, rows = tokens_t.shape
    return pl.pallas_call(
        pack_rows_kernel,
        name="pack_rows",
        out_shape=shaped((rows + plan.shape[0], width), BF),
        in_specs=[vm()] * 2,
        out_specs=vm(),
        compiler_params=params(8),
        cost_estimate=estimate(),
    )(*apart([tokens_t, plan]))


def stack_kernel(*refs):
    out_ref = refs[-1]
    at = 0
    for ref in refs[:-1]:
        out_ref[at : at + ref.shape[0], :] = ref[...]
        at += ref.shape[0]


def stack_call(pieces):
    rows = sum(p.shape[0] for p in pieces)
    return pl.pallas_call(
        stack_kernel,
        name="stack",
        out_shape=shaped((rows, pieces[0].shape[1]), pieces[0].dtype),
        in_specs=[vm()] * len(pieces),
        out_specs=vm(),
        compiler_params=params(8),
        cost_estimate=estimate(),
    )(*pieces)


def split_kernel(total_ref, other_ref, *outs):
    rows = outs[0].shape[0]
    for i, out in enumerate(outs):
        at = slice(i * rows, (i + 1) * rows)
        out[...] = (total_ref[at, :] + other_ref[at, :].astype(F32)).astype(out.dtype)


def split_call(total, other):
    rows, width = total.shape[0] // len(NEAR), total.shape[1]
    outs = [shaped((rows, width), F32)] + [shaped((rows, width), BF)] * (len(NEAR) - 1)
    return pl.pallas_call(
        split_kernel,
        name="split",
        out_shape=tuple(outs),
        in_specs=[vm(), vm()],
        out_specs=tuple(vm() for _ in outs),
        compiler_params=params(10),
        cost_estimate=estimate(),
    )(total, other)


def project(x, gain, wqkv_ref, cosine, sine, first_ref, q_ref, kv_ref):
    normed, _ = normed_rows(x)
    first_in = (normed * gain).astype(BF)
    first_ref[...] = first_in
    rows = mm(first_in, wqkv_ref[...])
    wide = SHARE * HEAD_SIZE
    q_width = KEY_VALUE_HEADS * wide
    kv_width = KEY_VALUE_HEADS * HEAD_SIZE
    key = turn(rows[:, q_width : q_width + kv_width], cosine, sine)
    value = rows[:, q_width + kv_width : q_width + 2 * kv_width]
    for h in range(KEY_VALUE_HEADS):
        at = slice(h * HEAD_SIZE, (h + 1) * HEAD_SIZE)
        kv_ref[:, h * 128 : (h + 1) * 128] = jnp.concatenate(
            [key[:, at], value[:, at]], axis=1
        ).astype(BF)
    query = (turn(rows[:, :q_width], cosine, sine).astype(BF) * SCALE).astype(BF)
    for h in range(KEY_VALUE_HEADS):
        q_ref[h] = query[:, h * wide : (h + 1) * wide]


def first_kernel(near, weights, coords_ref, x_ref, gain_ref, cos_ref, sin_ref, *rest):
    count = len(arrays_of(weights))
    refs, (first_ref, q_ref, kv_ref, *scratch) = rest[:count], rest[count:]
    (wqkv,), wait = weights_here(near, weights, refs, scratch, coords_ref, ((0, 0),))
    wait(0)
    project(
        x_ref[...].astype(F32), gain_ref[...], wqkv, cos_ref[...], sin_ref[...],
        first_ref, q_ref, kv_ref,
    )


def first_call(near, coords, tokens, gain, cosine, sine, weights):
    rows, width = tokens.shape
    specs, arrays, scratch = weights_in(near, weights)
    return pl.pallas_call(
        functools.partial(first_kernel, near, weights),
        name="first_projection",
        out_shape=(
            stored((rows, width), BF),
            shaped((KEY_VALUE_HEADS, rows, SHARE * HEAD_SIZE), BF),
            shaped((rows, KEY_VALUE_HEADS * 128), BF),
        ),
        in_specs=[sm()] + [vm()] * 4 + specs,
        out_specs=(vm(), vm(), vm()),
        scratch_shapes=scratch,
        compiler_params=params(10),
        cost_estimate=estimate(),
    )(coords, tokens, gain, cosine, sine, *arrays)


def padded_heads(wide_rows, left):
    rows = wide_rows.shape[0]
    blank = jnp.zeros((rows, HEAD_SIZE), wide_rows.dtype)
    stacked = []
    for j in range(SHARE):
        part = wide_rows[:, j * HEAD_SIZE : (j + 1) * HEAD_SIZE]
        stacked.append(jnp.concatenate([part, blank] if left else [blank, part], axis=1))
    return jnp.concatenate(stacked, axis=0)


def fill_bias(prompt, kpos_ref, live_ref, qpos_ref, bias_scr, col_scr):
    kpos = kpos_ref[...]
    klive = live_ref[...] > 0
    rows = bias_scr.shape[0]
    square = lambda axis: lax.broadcasted_iota(jnp.int32, (rows, rows), axis)
    own = jnp.where(square(0) == square(1), qpos_ref[...].astype(F32), 0.0)
    col_scr[...] = jnp.sum(own, axis=1, keepdims=True).astype(jnp.int32)
    kseg = jnp.where(kpos < prompt, 0, 1 + ((kpos - prompt) >> CONT_BITS))

    def fill(i, carry):
        at = pl.ds(pl.multiple_of(i * 8, 8), 8)
        qpos = col_scr[at, :]
        qseg = jnp.where(qpos < prompt, 0, 1 + ((qpos - prompt) >> CONT_BITS))
        earlier = kpos <= qpos
        shared = (kseg == 0) | (kseg == qseg)
        seen = earlier & shared & (klive | (kpos == qpos))
        bias_scr[at, :] = jnp.where(seen, 0.0, MASK_FLOOR)
        return carry

    lax.fori_loop(0, bias_scr.shape[0] // 8, fill, 0)


def attend_kernel(prompt, q_ref, a_ref, b_ref, kpos_ref, live_ref, qpos_ref, p_ref, o_ref, bias_scr, col_scr):
    @pl.when(pl.program_id(0) == 0)
    def _():
        fill_bias(prompt, kpos_ref, live_ref, qpos_ref, bias_scr, col_scr)

    o_ref[0] = attend_heads(q_ref, a_ref, b_ref, p_ref, bias_scr)


def attend_heads(q_ref, a_ref, b_ref, p_ref, bias_scr):
    rows = q_ref.shape[1]
    half = a_ref.shape[0]
    together = rows < 128
    if together:
        stacked = padded_heads(q_ref[0], True)
        all_a, all_b = mm(stacked, a_ref[...], NT), mm(stacked, b_ref[...], NT)
    blank = jnp.zeros((rows, HEAD_SIZE), BF)
    outs = []
    for j in range(SHARE):
        at = slice(j * rows, (j + 1) * rows)
        if together:
            s_a, s_b = all_a[at], all_b[at]
        else:
            part = jnp.concatenate([q_ref[0, :, j * HEAD_SIZE : (j + 1) * HEAD_SIZE], blank], axis=1)
            s_a, s_b = mm(part, a_ref[...], NT), mm(part, b_ref[...], NT)
        s_a = s_a + bias_scr[:, :half]
        s_b = s_b + bias_scr[:, half:]
        top = jnp.maximum(
            jnp.max(s_a, axis=-1, keepdims=True), jnp.max(s_b, axis=-1, keepdims=True)
        )
        w_a, w_b = jnp.exp(s_a - top), jnp.exp(s_b - top)
        mass = jnp.sum(w_a, axis=-1, keepdims=True) + jnp.sum(w_b, axis=-1, keepdims=True)
        inverse = 1.0 / mass
        p_a, p_b = (w_a * inverse).astype(BF), (w_b * inverse).astype(BF)
        p_ref[0, at, :half] = p_a
        p_ref[0, at, half:] = p_b
        if not together:
            outs.append((mm(p_a, a_ref[...]) + mm(p_b, b_ref[...]))[:, HEAD_SIZE:])
    if together:
        mixed = mm(p_ref[0, :, :half], a_ref[...]) + mm(p_ref[0, :, half:], b_ref[...])
        outs = [mixed[j * rows : (j + 1) * rows, HEAD_SIZE:] for j in range(SHARE)]
    return jnp.concatenate(outs, axis=1).astype(BF)


def attend_call(query, part_a, part_b, kpos, klive, qpos, prompt):
    heads, rows, wide = query.shape
    half = part_a.shape[0]
    keys = 2 * half
    return pl.pallas_call(
        functools.partial(attend_kernel, prompt),
        name="attend",
        grid=(heads,),
        out_shape=(stored((heads, SHARE * rows, keys), BF), shaped((heads, rows, wide), BF)),
        in_specs=[
            pl.BlockSpec((1, rows, wide), lambda h: (h, 0, 0)),
            pl.BlockSpec((half, 128), lambda h: (0, h)),
            pl.BlockSpec((half, 128), lambda h: (0, h)),
            pl.BlockSpec((1, keys), lambda h: (0, 0)),
            pl.BlockSpec((1, keys), lambda h: (0, 0)),
            pl.BlockSpec((1, rows), lambda h: (0, 0)),
        ],
        out_specs=(
            pl.BlockSpec((1, SHARE * rows, keys), lambda h: (h, 0, 0)),
            pl.BlockSpec((1, rows, wide), lambda h: (h, 0, 0)),
        ),
        scratch_shapes=[pltpu.VMEM((rows, keys), F32), pltpu.VMEM((rows, 1), jnp.int32)],
        compiler_params=params(12 if keys <= 2048 else 56, dimension_semantics=("arbitrary",)),
        cost_estimate=estimate(rows * keys / 17000),
    )(query, part_a, part_b, kpos, klive, qpos)


def attend_back_kernel(q_ref, do_ref, a_ref, b_ref, p_ref, dq_ref, da_ref, db_ref, dp_scr, ds_scr):
    rows = q_ref.shape[1]
    half = a_ref.shape[0]
    stacked = padded_heads(q_ref[0], True)
    grads = padded_heads(do_ref[0], False)
    dp_scr[:, :half] = mm(grads, a_ref[...], NT)
    dp_scr[:, half:] = mm(grads, b_ref[...], NT)

    for j in range(SHARE):
        at = slice(j * rows, (j + 1) * rows)
        weights = p_ref[0, at, :].astype(F32)
        dp = dp_scr[at, :]
        delta = jnp.sum(weights * dp, axis=-1, keepdims=True)
        ds_scr[at, :] = (weights * (dp - delta)).astype(BF)
    dq = (mm(ds_scr[:, :half], a_ref[...]) + mm(ds_scr[:, half:], b_ref[...])) * SCALE
    dq_ref[0] = jnp.concatenate(
        [dq[j * rows : (j + 1) * rows, :HEAD_SIZE] for j in range(SHARE)], axis=1
    )
    for at, out in ((slice(0, half), da_ref), (slice(half, 2 * half), db_ref)):
        turned = mm(stacked, ds_scr[:, at], TN) + mm(grads, p_ref[0, :, at], TN)
        out[...] = turned.T.astype(out.dtype)


def attend_back_call(query, d_out, part_a, part_b, weights):
    heads, rows, wide = query.shape
    half = part_a.shape[0]
    keys = 2 * half
    return pl.pallas_call(
        attend_back_kernel,
        name="attend_back",
        grid=(heads,),
        out_shape=(
            shaped((heads, rows, wide), F32),
            shaped((half, heads * 128), F32),
            shaped((half, heads * 128), BF),
        ),
        in_specs=[
            pl.BlockSpec((1, rows, wide), lambda h: (h, 0, 0)),
            pl.BlockSpec((1, rows, wide), lambda h: (h, 0, 0)),
            pl.BlockSpec((half, 128), lambda h: (0, h)),
            pl.BlockSpec((half, 128), lambda h: (0, h)),
            pl.BlockSpec((1, SHARE * rows, keys), lambda h: (h, 0, 0)),
        ],
        out_specs=(
            pl.BlockSpec((1, rows, wide), lambda h: (h, 0, 0)),
            pl.BlockSpec((half, 128), lambda h: (0, h)),
            pl.BlockSpec((half, 128), lambda h: (0, h)),
        ),
        scratch_shapes=[
            pltpu.VMEM((SHARE * rows, keys), F32),
            pltpu.VMEM((SHARE * rows, keys), BF),
        ],
        compiler_params=params(14 if keys <= 2048 else 60, dimension_semantics=("arbitrary",)),
        cost_estimate=estimate(rows * keys / 22000),
    )(query, d_out, part_a, part_b, *apart([weights]))


def picks(sel_ref, total_rows):
    capacity = sel_ref.shape[1]
    row = lax.broadcasted_iota(jnp.int32, (total_rows, capacity), 0)
    return row == sel_ref[...]


def live_column(live_ref, rows):
    count = jnp.sum(live_ref[:, :].astype(F32), axis=1, keepdims=True)
    return lax.broadcasted_iota(jnp.int32, (rows, 1), 0).astype(F32) < count


def feed_forward(wait, x, mixed, gain_two, wo, wg, wu, wd, ao_out, mid_ref, second_ref, g_ref, u_ref, hid_ref):
    ao_out[...] = mixed
    wait(0)
    middle = x + mm(mixed, wo[...])
    mid_ref[...] = middle
    normed, _ = normed_rows(middle)
    second = (normed * gain_two).astype(BF)
    second_ref[...] = second
    wide = wg.shape[1] // FF_CHUNKS
    for j in range(FF_CHUNKS):
        at = slice(j * wide, (j + 1) * wide)
        wait(1, j)
        g = mm(second, wg[:, at])
        wait(2, j)
        u = mm(second, wu[:, at])
        g_ref[:, at] = g.astype(BF)
        u_ref[:, at] = u.astype(BF)
        hid_ref[:, at] = (g / (1.0 + jnp.exp(-g)) * u).astype(BF)
    wait(3)
    return middle + mm(hid_ref[...], wd[...], NT)


DENSE_TURNS = ((0, 0),) + tuple((w, j) for j in range(FF_CHUNKS) for w in (1, 2)) + ((3, 0),)


def dense_body(near, step, weights, mixed, args):
    args = list(args)
    take = lambda k: [args.pop(0) for _ in range(k)]
    coords_ref, x_ref, gain1_ref, gain2_ref = take(4)
    if step == 0:
        sel_ref, cos_ref, sin_ref = take(3)
    elif step == 1:
        live_ref, cos_ref, sin_ref = take(3)
    else:
        sel_ref, live2_ref, live_ref, h1_ref, h2_ref = take(5)
    refs = take(len(arrays_of(weights)))
    ao_out, mid_ref, second_ref, g_ref, u_ref, hid_ref = take(6)
    if step < 2:
        h_ref, next_ref, first_ref, q_ref, kv_ref = take(5)
    else:
        (out_ref,) = take(1)
    turns = DENSE_TURNS + (((4, 0),) if step < 2 else ())

    def work():
        buffers, wait = weights_here(near, weights, refs, args, coords_ref, turns)
        rows = x_ref.shape[0]
        x = x_ref[...].astype(F32)
        updated = feed_forward(
            wait, x, mixed(), gain2_ref[...], *buffers[:4], ao_out, mid_ref,
            second_ref, g_ref, u_ref, hid_ref,
        )
        if step == 0:
            h_ref[...] = updated
            chosen = picks(sel_ref, rows).astype(F32)
            following = mm(chosen, updated, TN, lax.Precision.HIGHEST)
        else:
            updated = jnp.where(live_column(live_ref, rows), updated, x)
        if step == 1:
            h_ref[...] = updated
            following = updated[: next_ref.shape[0]]
        if step < 2:
            next_ref[...] = following
            wait(4)
            project(
                following, gain1_ref[...], buffers[4], cos_ref[...], sin_ref[...],
                first_ref, q_ref, kv_ref,
            )
        else:
            slots = jnp.concatenate([updated, h2_ref[rows:, :]], axis=0).astype(BF)
            hit = picks(sel_ref, h1_ref.shape[0]) & (live2_ref[...] > 0)
            placed = mm(hit.astype(BF), slots)
            any_hit = jnp.sum(hit.astype(F32), axis=1, keepdims=True) > 0.5
            out_ref[...] = jnp.where(any_hit, placed, h1_ref[...]).T.astype(BF)

    return work


def joined_heads(ao_ref):
    return jnp.concatenate([ao_ref[h] for h in range(KEY_VALUE_HEADS)], axis=1)


def dense_kernel(near, step, weights, ao_ref, *args):
    dense_body(near, step, weights, lambda: joined_heads(ao_ref), args)()


def dense_outs(step, x, weights, next_rows):
    rows, width = x.shape
    hidden = weights[1].shape[1]
    outs = [
        stored((rows, width), BF),
        stored((rows, width), F32),
        stored((rows, width), BF),
        stored((rows, hidden), BF),
        stored((rows, hidden), BF),
        stored((rows, hidden), BF),
    ]
    if step < 2:
        outs += [
            stored((rows, width), F32),
            shaped((next_rows, width), F32),
            stored((next_rows, width), BF),
            shaped((KEY_VALUE_HEADS, next_rows, SHARE * HEAD_SIZE), BF),
            shaped((next_rows, KEY_VALUE_HEADS * 128), BF),
        ]
    else:
        outs += [stored((width, next_rows), BF)]
    return outs


def dense_call(near, step, coords, x, mixed, gain1, gain2, extra, weights, next_rows):
    specs, arrays, scratch = weights_in(near, weights)
    outs = dense_outs(step, x, weights, next_rows)
    return pl.pallas_call(
        functools.partial(dense_kernel, near, step, weights),
        name=f"dense_{step}",
        out_shape=tuple(outs),
        in_specs=[vm(), sm()] + [vm()] * (3 + len(extra)) + specs,
        out_specs=tuple(vm() for _ in outs),
        scratch_shapes=scratch,
        compiler_params=params(12 if near else 50),
        cost_estimate=estimate(6),
    )(mixed, coords, x, gain1, gain2, *extra, *arrays)


def feed_back(wait, first, d_y, mid_ref, g_ref, u_ref, gain_two, wd, wg, wu, wo, dyb_ref, dg_ref, du_ref, dmid_ref, dz_ref, dao_ref, sum_ref):
    d_low = d_y.astype(BF)
    dyb_ref[...] = d_low
    wide = wg.shape[1] // FF_CHUNKS
    d_second = jnp.zeros(d_y.shape, F32)
    wait(first)
    for j in range(FF_CHUNKS):
        at = slice(j * wide, (j + 1) * wide)
        d_hidden = mm(d_low, wd[:, at])
        g, u = g_ref[:, at].astype(F32), u_ref[:, at].astype(F32)
        sigma = 1.0 / (1.0 + jnp.exp(-g))
        d_gate = (d_hidden * u * sigma * (1.0 + g * (1.0 - sigma))).astype(BF)
        d_up = (d_hidden * (g * sigma)).astype(BF)
        dg_ref[:, at] = d_gate
        du_ref[:, at] = d_up
        wait(first + 1, j)
        wait(first + 2, j)
        d_second += mm(d_gate, wg[:, at], NT) + mm(d_up, wu[:, at], NT)
    normed, inverse = normed_rows(mid_ref[...])
    sum_ref[...] = jnp.sum(d_second * normed, axis=0, keepdims=True)
    d_mid = norm_back(d_second, normed, inverse, gain_two) + d_y
    dmid_ref[...] = d_mid
    d_low = d_mid.astype(BF)
    dz_ref[...] = d_low
    wait(first + 3)
    d_mixed = mm(d_low, wo[...], NT).astype(BF)
    wide = SHARE * HEAD_SIZE
    for h in range(KEY_VALUE_HEADS):
        dao_ref[h] = d_mixed[:, h * wide : (h + 1) * wide]


def project_back(own_ref, others, dq_ref, x, dmid_ref, gain_one, cosine, sine, wait, wqkv, dqkv_ref, sum_ref):
    total = own_ref[...].astype(F32)
    for other in others:
        total = total + other[...].astype(F32)
    d_key = jnp.concatenate(
        [total[:, h * 128 : h * 128 + HEAD_SIZE] for h in range(KEY_VALUE_HEADS)], axis=1
    )
    d_value = jnp.concatenate(
        [total[:, h * 128 + HEAD_SIZE : (h + 1) * 128] for h in range(KEY_VALUE_HEADS)], axis=1
    )
    d_query = jnp.concatenate([dq_ref[h] for h in range(KEY_VALUE_HEADS)], axis=1)
    d_rows = jnp.concatenate(
        [turn(d_query, cosine, sine, True), turn(d_key, cosine, sine, True), d_value], axis=1
    ).astype(BF)
    dqkv_ref[...] = d_rows
    wait(0)
    d_first = mm(d_rows, wqkv[:, : d_rows.shape[1]], NT)
    normed, inverse = normed_rows(x)
    sum_ref[...] = jnp.sum(d_first * normed, axis=0, keepdims=True)
    return norm_back(d_first, normed, inverse, gain_one) + dmid_ref[...]


def back_kernel(near, phase, weights, n_parts, *args):
    args = list(args)
    take = lambda k: [args.pop(0) for _ in range(k)]
    (coords_ref,) = take(1)
    if phase > 0:
        gain1_ref, cos_ref, sin_ref, x_ref, dmid_in, dq_ref = take(6)
        own_ref, *others = take(n_parts)
    if phase < 3:
        gain2_ref, mid_ref, g_ref, u_ref = take(4)
    if phase == 0:
        cot_ref, sel_ref, live3_ref = take(3)
    elif phase == 1:
        slots_ref, live3_ref, live2_ref = take(3)
    elif phase == 2:
        cot_ref, sel_ref, live2_ref = take(3)
    refs = take(len(arrays_of(weights)))
    if phase > 0:
        dqkv_ref, sum1_ref = take(2)
    if phase < 3:
        outs = take(7)
    if phase == 0:
        (slots_out,) = take(1)
    elif phase == 3:
        (grad_ref,) = take(1)
    turns = ((0, 0),) if phase > 0 else ()
    first = len(turns)
    if phase < 3:
        turns += ((first, 0),)
        turns += tuple((first + w, j) for j in range(FF_CHUNKS) for w in (1, 2))
        turns += ((first + 3, 0),)
    buffers, wait = weights_here(near, weights, refs, args, coords_ref, turns)
    if phase > 0:
        d_x = project_back(
            own_ref, others, dq_ref, x_ref[...].astype(F32), dmid_in, gain1_ref[...],
            cos_ref[...], sin_ref[...], wait, buffers[0], dqkv_ref, sum1_ref,
        )
    if phase == 0:
        chosen = picks(sel_ref, cot_ref.shape[1]).astype(BF)
        slots = mm(chosen, cot_ref[...].T, TN)
        slots_out[...] = slots
        rows = mid_ref.shape[0]
        d_y = jnp.where(live_column(live3_ref, rows), slots[:rows], 0.0)
    elif phase == 1:
        rows = x_ref.shape[0]
        slots = slots_ref[...]
        head = jnp.where(live_column(live3_ref, rows), d_x, slots[:rows])
        slots = jnp.concatenate([head, slots[rows:]], axis=0)
        d_y = jnp.where(live_column(live2_ref, slots.shape[0]), slots, 0.0)
    elif phase == 2:
        hit = picks(sel_ref, cot_ref.shape[1]) & (live2_ref[...] > 0)
        placed = mm(hit.astype(F32), d_x, NN, lax.Precision.HIGHEST)
        any_hit = jnp.sum(hit.astype(F32), axis=1, keepdims=True) > 0.5
        d_y = jnp.where(any_hit, placed, cot_ref[...].astype(F32).T)
    else:
        grad_ref[...] = d_x.T.astype(BF)
        return
    feed_back(
        wait, first, d_y, mid_ref, g_ref, u_ref, gain2_ref[...],
        *buffers[first : first + 4], *outs,
    )


def back_call(near, phase, coords, before, parts, into, extra, weights, rows_next):
    specs, arrays, scratch = weights_in(near, weights)
    ins = list(before) + list(parts) + list(into) + list(extra)
    outs = []
    if phase > 0:
        rows, width = before[3].shape
        qkv_width = width + 2 * KEY_VALUE_HEADS * HEAD_SIZE
        outs += [stored((rows, qkv_width), BF), stored((1, width), F32)]
    if phase < 3:
        rows, hidden = into[2].shape
        width = into[1].shape[1]
        outs += [
            stored((rows, width), BF),
            stored((rows, hidden), BF),
            stored((rows, hidden), BF),
            stored((rows, width), F32),
            stored((rows, width), BF),
            shaped((KEY_VALUE_HEADS, rows, SHARE * HEAD_SIZE), BF),
            stored((1, width), F32),
        ]
    if phase == 0:
        outs += [stored((rows_next, width), F32)]
    elif phase == 3:
        outs += [stored((width, rows), BF)]
    return pl.pallas_call(
        functools.partial(back_kernel, near, phase, weights, len(parts)),
        name=f"back_{phase}",
        out_shape=tuple(outs),
        in_specs=[sm()] + [vm()] * len(ins) + specs,
        out_specs=tuple(vm() for _ in outs),
        scratch_shapes=scratch,
        compiler_params=params(12 if near else 50),
        cost_estimate=estimate(6),
    )(coords, *before, *parts, *into[:1], *apart(into[1:]), *extra, *arrays)


def stack_rows(refs, scratch):
    at = 0
    for ref in refs:
        scratch[at : at + ref.shape[0], :] = ref[...]
        at += ref.shape[0]


SPARE = 8


def put_blocks(value, x_of, coords, ref, spare=None):
    y, _, _, z = coords
    depth = value.shape[0] // 8
    for ya in range(2):
        for za in range(4):
            row = (ya * 4 + za) * depth
            block = value[row : row + depth].astype(BF)
            if spare is None:
                ref[y ^ ya, x_of, z ^ za] = block
            else:
                ref[y ^ ya, x_of, z ^ za, :depth] = block
                ref[y ^ ya, x_of, z ^ za, depth:] = spare(ya, za).astype(BF)


def grad_cols_kernel(n_steps, coords_ref, *args):
    left, args = args[:n_steps], args[n_steps:]
    right, args = args[:n_steps], args[n_steps:]
    keep_ref, send_ref, l_scr, r_scr = args
    coords = read_coords(coords_ref)
    _, c, x, _ = coords
    stack_rows(left, l_scr)
    stack_rows(right, r_scr)
    block = keep_ref.shape[-1]
    for far, ref in ((1, send_ref), (0, keep_ref)):

        def body(rx, carry, far=far, ref=ref):
            start = pl.multiple_of(((c ^ far) * 2 + (x ^ rx)) * block, 128)
            value = mm(l_scr[...], r_scr[:, pl.ds(start, block)], TN)
            put_blocks(value, rx, coords, ref)
            return carry

        lax.fori_loop(0, 2, body, 0)


def grad_rows_kernel(n_steps, coords_ref, *args):
    left, args = args[:n_steps], args[n_steps:]
    right, args = args[:n_steps], args[n_steps:]
    keep_ref, send_ref, l_scr, r_scr = args
    coords = read_coords(coords_ref)
    y, c, x, z = coords
    stack_rows(left, l_scr)
    stack_rows(right, r_scr)
    depth = keep_ref.shape[-2]
    span = 8 * depth
    for far, ref in ((1, send_ref), (0, keep_ref)):

        def body(ry, carry, far=far, ref=ref):
            start = pl.multiple_of(((y ^ ry) * 2 + (c ^ far)) * span, 128)
            value = mm(l_scr[:, pl.ds(start, span)], r_scr[...], TN)
            for xa in range(2):
                for za in range(4):
                    row = (xa * 4 + za) * depth
                    ref[ry, x ^ xa, z ^ za] = value[row : row + depth].astype(BF)
            return carry

        lax.fori_loop(0, 2, body, 0)


def grad_mixed_kernel(n_steps, coords_ref, sums_ref, *args):
    groups = []
    for _ in range(4):
        groups.append(args[:n_steps])
        args = args[n_steps:]
    keep_ref, send_ref, first_scr, mixed_scr, qkv_scr, z_scr, val_scr = args
    coords = read_coords(coords_ref)
    _, c, x, _ = coords
    for refs, scr in zip(groups, (first_scr, mixed_scr, qkv_scr, z_scr), strict=True):
        stack_rows(refs, scr)
    block = keep_ref.shape[-1]
    width = z_scr.shape[1]
    kv_width = (qkv_scr.shape[1] - width) // 2
    for ca in range(2):
        for xa in range(2):
            if ca == 0:
                val_scr[...] = mm(first_scr[...], qkv_scr[:, xa * block : (xa + 1) * block], TN)
            elif xa == 0:
                val_scr[...] = mm(mixed_scr[...], z_scr[:, :block], TN)
            else:
                val_scr[...] = jnp.concatenate(
                    [
                        mm(mixed_scr[...], z_scr[:, block:], TN),
                        mm(first_scr[...], qkv_scr[:, width + kv_width :], TN),
                    ],
                    axis=1,
                )

            def spare(ya, za, first=ca == 0 and xa == 0):
                if not first or za:
                    return jnp.zeros((SPARE, block), F32)
                half = width // 2
                rows = sums_ref[:, ya * half : (ya + 1) * half]
                rows = jnp.concatenate([rows, jnp.zeros((2, block - half), F32)], axis=1)
                return jnp.concatenate([rows, jnp.zeros((SPARE - 2, block), F32)], axis=0)

            @pl.when(c == ca)
            def _(xa=xa, spare=spare):
                put_blocks(val_scr[...], x ^ xa, coords, keep_ref, spare)

            @pl.when(c != ca)
            def _(xa=xa, spare=spare):
                put_blocks(val_scr[...], x ^ xa, coords, send_ref, spare)


def grad_call(kind, coords, groups, sums=None):
    n_steps = len(groups[0])
    rows = sum(a.shape[0] for a in groups[0])
    width, cols = groups[0][0].shape[1], groups[1][0].shape[1]
    scratch = [pltpu.VMEM((rows, g[0].shape[1]), BF) for g in groups]
    if kind == "rows":
        kernel, block = grad_rows_kernel, (width // 32, cols)
    elif kind == "cols":
        kernel, block = grad_cols_kernel, (width // 8, cols // 4)
    else:
        total = sum(g[0].shape[1] for g in groups[2:])
        kernel, block = grad_mixed_kernel, (width // 8 + SPARE, total // 4)
        scratch += [pltpu.VMEM((width, block[1]), F32)]
    out = shaped((2, 2, 4) + block, BF)
    ins = [a for g in groups for a in g]
    if sums is not None:
        ins = [sums, *ins]
    return pl.pallas_call(
        functools.partial(kernel, n_steps),
        name=f"grad_{kind}",
        out_shape=(out, out),
        in_specs=[sm()] + [vm()] * len(ins),
        out_specs=(vm(), vm()),
        scratch_shapes=scratch,
        compiler_params=params(16),
        cost_estimate=estimate(6),
    )(coords, *apart(ins))


def place_cols_kernel(coords_ref, near_ref, far_ref, *outs):
    _, c, x, z = read_coords(coords_ref)
    block = near_ref.shape[-1]
    mixed = len(outs) > 1
    target = outs[5] if mixed else outs[0]
    depth = target.shape[0]
    for far, ref in ((0, near_ref), (1, far_ref)):
        for rx in range(2):
            cols = pl.ds(pl.multiple_of(((c ^ far) * 2 + (x ^ rx)) * block, 128), block)
            target[:, cols] = ref[rx, 0, :depth].astype(F32)
    if mixed:
        q_ref, k_ref, o_ref, v_ref, gains_ref, _, k_scr, v_scr = outs
        width, kv_width = q_ref.shape[1], k_ref.shape[0]
        rows = pl.ds(pl.multiple_of((z ^ pl.program_id(0)) * depth, 8), depth)
        q_ref[...] = target[:, :width]
        k_scr[rows, :] = target[:, width : width + kv_width]
        o_ref[...] = target[:, width + kv_width : 2 * width + kv_width]
        v_scr[rows, :] = target[:, 2 * width + kv_width :]
        for far, ref in ((0, near_ref), (1, far_ref)):

            @pl.when((z == pl.program_id(0)) & (c == far))
            def _(ref=ref):
                spare = ref[x, 0, depth:].astype(F32)
                gains_ref[...] = spare[:2, : gains_ref.shape[1]]

        @pl.when(pl.program_id(0) == 3)
        def _():
            k_ref[...] = k_scr[...].T
            v_ref[...] = v_scr[...].T


def place_rows_kernel(coords_ref, near_ref, far_ref, out_ref, scr):
    _, _, x, z = read_coords(coords_ref)
    depth = near_ref.shape[-2]

    def put(ref):
        for rx in range(2):
            for rz in range(4):
                row = pl.multiple_of(((x ^ rx) * 4 + (z ^ rz)) * depth, 8)
                scr[pl.ds(row, depth), :] = ref[rx, rz].astype(F32)

    @pl.when(pl.program_id(0) == 0)
    def _():
        put(near_ref)

    @pl.when(pl.program_id(0) == 1)
    def _():
        put(far_ref)

    out_ref[...] = scr[...].T


def place_call(kind, coords, near, far, widths):
    depth, block = near.shape[-2:]
    scratch = []
    if kind == "rows":
        kernel, grid = place_rows_kernel, (2,)
        outs = (stored((block, 16 * depth), F32),)
        source = pl.BlockSpec((2, 4, depth, block), lambda f, k: (0, 0, 0, 0))
        targets = (pl.BlockSpec((block, 8 * depth), lambda f, k: (0, k[1] ^ f)),)
        scratch = [pltpu.VMEM((8 * depth, block), F32)]
    else:
        kernel, grid = place_cols_kernel, (4,)
        source = pl.BlockSpec((2, 1, *near.shape[-2:]), lambda i, k: (0, i, 0, 0))
        if len(widths) > 1:
            depth -= SPARE
        straight = lambda w: (
            stored((4 * depth, w), F32), pl.BlockSpec((depth, w), lambda i, k: (k[3] ^ i, 0))
        )
        turned = lambda w: (
            stored((w, 4 * depth), F32), pl.BlockSpec((w, 4 * depth), lambda i, k: (0, 0))
        )
        outs, targets = zip(
            *((turned if i % 2 else straight)(w) for i, w in enumerate(widths)), strict=True
        )
        if len(outs) > 1:
            outs += (stored((2, 4 * depth), F32),)
            targets += (pl.BlockSpec((2, 4 * depth), lambda i, k: (0, 0)),)
            scratch = [pltpu.VMEM((depth, 4 * block), F32)]
            scratch += [pltpu.VMEM((4 * depth, w), F32) for w in widths[1::2]]
    return pl.pallas_call(
        kernel,
        name=f"place_{kind}",
        grid_spec=pltpu.PrefetchScalarGridSpec(
            num_scalar_prefetch=1,
            grid=grid,
            in_specs=[source, source],
            out_specs=targets,
            scratch_shapes=scratch,
        ),
        out_shape=outs,
        compiler_params=params(12),
        cost_estimate=estimate(),
    )(coords, near, far)


def low_sum(left, right):
    return (left.astype(F32) + right.astype(F32)).astype(BF)


def split_list(values, count):
    return values[:count], values[count:]


def gather_keys(kv, order, near, meanwhile=([], [])):
    if not near:
        whole = lax.all_gather(kv, "ctx", axis=0, tiled=True)
        half = whole.shape[0] // 2
        return whole[:half], whole[half:]
    kv = order.take(kv)
    hops = [hop(kv, m) for m in (X_BIT, Y_BIT, Z1_BIT, X_BIT | Y_BIT | Z1_BIT)]
    (by_x, by_y, by_z, across), meanwhile[0][:] = split_list(order.all(*hops, *meanwhile[0]), 4)
    hops = [hop(by_x, Y_BIT), hop(by_y, Z1_BIT), hop(by_z, X_BIT)]
    hops, meanwhile[1][:] = split_list(order.all(*hops, *meanwhile[1]), 3)
    part = stack_call([kv, by_x, by_y, by_z, across, *hops])
    return part, order.take(hop(part, C_BIT))


class KeySums:
    def __init__(self, own, others):
        self.own, self.others = own, others

    def sends(self, turn):
        return list(zip(self.others, NEAR[1:], strict=True))

    def got(self, turn, values):
        self.result = [self.own, *values]


class Hop:
    def __init__(self, value, mask):
        self.value, self.mask = value, mask

    def sends(self, turn):
        return [(self.value, self.mask)]

    def got(self, turn, values):
        (self.result,) = values


def scatter_keys(part_a, part_b, order, near):
    if not near:
        whole = jnp.concatenate([part_a, part_b.astype(F32)], axis=0)
        return [lax.psum_scatter(whole, "ctx", scatter_dimension=0, tiled=True)]
    far = Hop(part_b, C_BIT)
    (part_a,) = wave(order, [(far, 0)], lambda a: (a,), (part_a,))
    own, *others = split_call(part_a, far.result)
    sums = KeySums(own, others)
    wave(order, [(sums, 0)])
    return sums.result


def cut_rows(value, index, count):
    size = value.shape[0] // count
    return lax.dynamic_slice_in_dim(value, index * size, size, 0)


def cut_cols(value, index, count):
    size = value.shape[1] // count
    return lax.dynamic_slice_in_dim(value, index * size, size, 1)


class Share:
    def __init__(self, mine):
        self.mine = mine

    def sends(self, turn):
        return [(self.mine, mask) for mask in (X_BIT | Z1_BIT, X_BIT, Z1_BIT)]

    def got(self, turn, values):
        across, by_x, by_z = values
        self.result = [self.mine, by_x, by_z, across]


def pair_sum(keep, send, near):
    if near:
        return low_sum(keep, hop(send, C_BIT))
    return lax.psum(jnp.stack([keep, send]).astype(F32), AXES)


ALONG_Z = (Z1_BIT, Z2_BIT, Z1_BIT | Z2_BIT)
FAR_FIRST = (2, 1, 0)


class BlockSums:
    rounds = 6

    def __init__(self, total):
        self.total = total

    def sends(self, turn):
        if turn == 0:
            return [(self.total[1, 1], Y_BIT)]
        if turn == 1:
            return [(self.total[1, 0], Y_BIT), (low_sum(self.total[0, 1], self.came), X_BIT)]
        if turn == 2:
            return [(self.total[i + 1], ALONG_Z[i]) for i in FAR_FIRST]
        if turn == 3:
            return [(self.mine, ALONG_Z[i]) for i in FAR_FIRST]
        if turn == 4:
            return [(self.total, X_BIT)]
        return [(self.total, C_BIT)]

    def got(self, turn, values):
        if turn == 0:
            (self.came,) = values
        elif turn == 1:
            total = self.total[0, 0].astype(F32)
            for value in values:
                total = total + value.astype(F32)
            self.total = total.astype(BF)
        elif turn == 2:
            mine = self.total[0].astype(F32)
            for value in values:
                mine = mine + value.astype(F32)
            self.mine = mine.astype(BF)
        elif turn == 3:
            self.total = jnp.stack([self.mine, *values[::-1]])
        elif turn == 4:
            self.total = jnp.stack([self.total, *values])
        else:
            self.result = (self.total, *values)


class BothWays(BlockSums):
    def sends(self, turn):
        if turn == 0:
            return [(self.total[1, :, :2], Y_BIT), (self.total[:, 1, 2:], X_BIT)]
        if turn == 1:
            return [(self.first[1], X_BIT), (self.second[1], Y_BIT)]
        return super().sends(turn)

    def got(self, turn, values):
        if turn == 0:
            self.first = low_sum(self.total[0, :, :2], values[0])
            self.second = low_sum(self.total[:, 0, 2:], values[1])
        elif turn == 1:
            self.total = jnp.concatenate(
                [low_sum(self.first[0], values[0]), low_sum(self.second[0], values[1])]
            )
        else:
            super().got(turn, values)


class Move:
    rounds = 1

    def __init__(self, value):
        self.value = value

    def sends(self, turn):
        return [(self.value, None)]

    def got(self, turn, values):
        (self.result,) = values


def wave(order, steps, work=None, uses=()):
    plans = [chain.sends(turn) for chain, turn in steps]
    flat = [value for plan in plans for value, _ in plan]
    taken = order.all(*flat, *uses)
    sent, uses = taken[: len(flat)], taken[len(flat) :]
    masks = [mask for plan in plans for _, mask in plan]
    came = [move(v) if mask is None else hop(v, mask) for v, mask in zip(sent, masks, strict=True)]
    made = list(work(*uses)) if work else []
    came = order.all(*came, *made)
    came, made = came[: len(flat)], came[len(flat) :]
    for (chain, turn), plan in zip(steps, plans, strict=True):
        chain.got(turn, came[: len(plan)])
        came = came[len(plan) :]
    return made


def on_device(
    tokens, cotangent, w_query, key_weight, value_weight, w_out, w_gate, w_up, w_down,
    gain_attn, gain_ffn, block_order, sel_mid, live_mid, sel_last, live_last,
):
    ctx_count, ws_count = lax.axis_size("ctx"), lax.axis_size("ws")
    near = ctx_count == 16 and ws_count == 2
    ctx, y = lax.axis_index("ctx"), lax.axis_index("ws")
    tok_local = tokens.shape[1]
    cap_mid, cap_last = sel_mid.shape[1] // ctx_count, sel_last.shape[1] // ctx_count
    if near:
        c, x, z = ctx & 1, (ctx >> 1) & 1, ctx >> 2
        places = (y, c, x, z)
        here = (ctx & 7) | (y << 3)
        turn_order = here ^ jnp.array([ctx_mask(m) for m in NEAR] + [ctx_mask(m) | 1 for m in NEAR], jnp.int32)
        relocate = move
    else:
        zero = jnp.int32(0)
        places = (y, zero, zero, zero)
        here = ctx
        turn_order = jnp.arange(ctx_count, dtype=jnp.int32)
        relocate = lambda v: v
    coords = jnp.stack([jnp.asarray(v, jnp.int32) for v in places])
    block_coords = coords if near else jnp.zeros((4,), jnp.int32)
    width = tokens.shape[2]
    half = w_query.shape[0]
    plan = jnp.concatenate(
        [
            sel_mid.reshape(ctx_count, cap_mid),
            live_mid.reshape(ctx_count, cap_mid),
            live_last.reshape(ctx_count, cap_last),
        ],
        axis=1,
    )
    order = Order(coords)
    if near:
        assert tok_local <= 256
        own_qkv, piece = pack_call(coords, w_query, key_weight.T, value_weight.T)
        fetched = hop(piece, Y_BIT)
        tok = move(pack_rows_call(tokens[0].T, plan))
        gains = jnp.concatenate([gain_attn.reshape(1, -1), gain_ffn.reshape(1, -1)], axis=0)
        beyond = hop(gains, Y_BIT)
        quad = x * 2 + (z & 1)
        own_down = w_down.T
        fetched, cut_pair, cut_out, cut_down = order.take(
            fetched,
            jnp.concatenate([cut_cols(cut_rows(w, c, 2), quad, 4) for w in (w_gate, w_up)], axis=0),
            cut_rows(w_out, c, 2),
            cut_rows(own_down, c, 2),
        )
        far = hop(fetched, C_BIT)
        pair_mine, out_mine = hop(cut_pair, Y_BIT), hop(cut_out, Y_BIT)
        far, tok, beyond = order.take(far, tok, beyond)
        plan = tok[tok_local:, : plan.shape[1]].astype(jnp.int32)
        tok = tok[:tok_local]
        depth = half // 2
        gains = jnp.where(
            y == 0,
            jnp.concatenate([gains, beyond], axis=1),
            jnp.concatenate([beyond, gains], axis=1),
        )
        gains = [gains[0:1], gains[1:2]]
        origin = lambda *k: (0, 0)

        def in_rows(own, mine, other):
            wide = own.shape[1]
            return Weight(
                (2 * half, wide),
                [own, mine, other],
                [
                    [
                        (0, half, wide, origin, lambda ky, kc, kx, kz: (ky * half, 0)),
                        (1, depth, wide, origin, lambda ky, kc, kx, kz: ((1 - ky) * half + kc * depth, 0)),
                        (2, depth, wide, origin, lambda ky, kc, kx, kz: ((1 - ky) * half + (1 - kc) * depth, 0)),
                    ]
                ],
            )

        def in_parts(own, mine, other, which):
            wide = mine.shape[1]
            groups = []
            for j in range(FF_CHUNKS):
                column = lambda *k, j=j: part_of(j, k) * wide
                block = lambda *k, j=j: ((2 * j + which) * depth, 0)
                groups.append(
                    [
                        (0, half, wide,
                         lambda *k, column=column: (0, column(*k)),
                         lambda *k, column=column: (k[0] * half, column(*k))),
                        (1, depth, wide, block,
                         lambda *k, column=column: ((1 - k[0]) * half + k[1] * depth, column(*k))),
                        (2, depth, wide, block,
                         lambda *k, column=column: ((1 - k[0]) * half + (1 - k[1]) * depth, column(*k))),
                    ]
                )
            return Weight((2 * half, own.shape[1]), [own, mine, other], groups)

        (weight_qkv,) = join_call(coords, (in_rows(own_qkv, fetched, far),))
        marks = {}

        def fetch_rest(pair, out, down):
            pair = stack_call(pair)
            shared = [Hop(v, C_BIT) for v in (pair, out, down)]
            wave(order, [(s, 0) for s in shared])
            pair_far, out_far, down_far = (s.result for s in shared)
            wide = own_down.shape[1]
            weight_d = Weight(
                (width, 2 * wide),
                [own_down, down, down_far],
                [
                    [
                        (0, width, wide, origin, lambda ky, kc, kx, kz: (0, ky * wide)),
                        (1, width // 2, wide, origin, lambda ky, kc, kx, kz: (kc * (width // 2), (1 - ky) * wide)),
                        (2, width // 2, wide, origin, lambda ky, kc, kx, kz: ((1 - kc) * (width // 2), (1 - ky) * wide)),
                    ]
                ],
            )
            return join_call(
                coords,
                (
                    in_rows(w_out, out, out_far),
                    in_parts(w_gate, pair, pair_far, 0),
                    in_parts(w_up, pair, pair_far, 1),
                    weight_d,
                ),
            )
    else:
        tok = tokens[0]
        whole = lambda w: lax.all_gather(w, "ws", axis=0, tiled=True)
        weight_qkv = one_piece(whole(jnp.concatenate([w_query, key_weight, value_weight], axis=1)))
        gains = [whole(g).reshape(1, -1) for g in (gain_attn, gain_ffn)]
        far_weights = (
            one_piece(whole(w_out)), in_columns(whole(w_gate)), in_columns(whole(w_up)),
            one_piece(whole(w_down).T),
        )
        fetch_rest = lambda: far_weights
    gain1, gain2 = (g.astype(F32) for g in gains)

    per_device = tok_local // BLK
    blocks = jnp.take(block_order.reshape(ctx_count, per_device), turn_order, axis=0)
    plan_order = jnp.take(plan, turn_order, axis=0)
    sel_all = plan_order[:, :cap_mid]
    live_two = plan_order[:, cap_mid : 2 * cap_mid]
    live_three = plan_order[:, 2 * cap_mid :]
    place_one = (blocks[:, :, None] * BLK + jnp.arange(BLK, dtype=jnp.int32)).reshape(ctx_count, tok_local)
    place_two = sum(
        jnp.where(sel_all // BLK == k, blocks[:, k : k + 1], 0) for k in range(per_device)
    ) * BLK + sel_all % BLK
    place_three = place_two[:, :cap_last]
    if near:
        mine = lambda v: v[0:1]
    else:
        mine = lambda v: lax.dynamic_slice_in_dim(v, here, 1, 0)
    sel_own, live2_own, live3_own = mine(sel_all), mine(live_two), mine(live_three)
    own_places = jnp.concatenate([mine(place_one), mine(place_two)], axis=1).reshape(-1, 1)
    frequency = ROPE_BASE ** (-jnp.arange(HEAD_SIZE // 2, dtype=F32) / (HEAD_SIZE // 2))
    angles = own_places.astype(F32) * frequency[None, :]
    cosine, sine = jnp.cos(angles), jnp.sin(angles)
    cosine = jnp.concatenate([cosine] * 4, axis=1)
    sine = jnp.concatenate([-sine, sine, -sine, sine], axis=1)
    tables = [
        (cosine[:tok_local], sine[:tok_local]),
        (cosine[tok_local:], sine[tok_local:]),
        (cosine[tok_local : tok_local + cap_last], sine[tok_local : tok_local + cap_last]),
    ]
    query_places = [mine(v) for v in (place_one, place_two, place_three)]
    key_places = [v.reshape(1, -1) for v in (place_one, place_two, place_three)]
    key_live = [
        jnp.ones((1, ctx_count * tok_local), jnp.int32),
        live_two.reshape(1, -1),
        live_three.reshape(1, -1),
    ]
    prompt = ctx_count * tok_local // 2
    if near:
        key_places[0], query_places[0] = order.take(key_places[0], query_places[0])
        marks["places"] = [*query_places[1:], *key_places[1:], *key_live[1:], sel_own, live2_own, live3_own]
        marks["tables"] = [*tables[1], *tables[2]]

    firsts, mixeds, seconds, hiddens = [], [], [], []
    records = []
    xs = [tok]
    first_in, query, kv = first_call(near, coords, tok, gain1, *tables[0], (weight_qkv,))
    heights = []
    for step in range(3):
        if near and step == 0:
            waits = ([*marks["places"], pair_mine], [*marks["tables"], out_mine])
            part_a, part_b = gather_keys(kv, order, near, waits)
            *marks["places"], pair_mine = waits[0]
            *marks["tables"], out_mine = waits[1]
        else:
            part_a, part_b = gather_keys(kv, order, near)
        if near and step == 1:
            query_places[1:], key_places[1:], key_live[1:] = (marks["places"][i : i + 2] for i in (0, 2, 4))
        firsts.append(first_in)
        next_rows = (cap_mid, cap_last, tok_local)[step]
        attention = (query, part_a, part_b, key_places[step], key_live[step], query_places[step], prompt)
        if near and step == 0:
            pair, down_mine = Share(pair_mine), Hop(cut_down, Y_BIT)
            weights, mixed = wave(
                order, [(down_mine, 0), (pair, 0)], lambda *a: attend_call(*a, prompt), attention[:-1]
            )
            dense_weights = fetch_rest(pair.result, out_mine, down_mine.result)
            sel_own, live2_own, live3_own = marks["places"][6:]
            tables[1:] = [marks["tables"][:2], marks["tables"][2:]]
        elif step == 0:
            weights, mixed = attend_call(*attention)
            dense_weights = fetch_rest()
        if step == 0:
            extra = (sel_own, *tables[1])
        elif step == 1:
            extra = (live2_own, *tables[2])
        else:
            extra = (sel_own, live2_own, live3_own, heights[0], heights[1])
        mats = dense_weights + ((weight_qkv,) if step < 2 else ())

        def dense(mixed, step=step, extra=extra, mats=mats, next_rows=next_rows):
            return dense_call(
                near, step, coords, xs[step], mixed, gain1, gain2, extra, mats, next_rows
            )

        def both(*a):
            made = attend_call(*a, prompt)
            return *made, *dense(made[1])

        if step == 0:
            result = dense(mixed)
        elif step == 1 and near:
            there = Move(cotangent[0].T)
            weights, mixed, *result = wave(order, [(there, 0)], both, attention[:-1])
            cot = there.result
        else:
            weights, mixed, *result = both(*attention[:-1])
            if step == 1:
                cot = cotangent[0].T
        mixed_rows, middle, second, gate, up, hidden = result[:6]
        mixeds.append(mixed_rows)
        seconds.append(second)
        hiddens.append(hidden)
        records.append((query, part_a, part_b, weights, middle, gate, up))
        if step < 2:
            height, following, first_in, query, kv = result[6:]
            heights.append(height)
            xs.append(following)
        else:
            output = relocate(order.take(result[6]))

    d_firsts, d_seconds = [None] * 3, [None] * 3
    sums_one, sums_two = [], []
    slots = None
    parts, d_query, d_middle = (), None, None
    column = lambda rows, i: [r[i] for r in rows]

    def grads(kind, groups):
        return grad_call(kind, block_coords, groups)

    for phase in range(4):
        step = 2 - phase
        before, into = (), ()
        if phase > 0:
            before = (gain1, *tables[step + 1], xs[step + 1], d_middle, d_query)
        if phase < 3:
            into = (gain2, *records[step][4:7])
        mats = (dense_weights[3], dense_weights[1], dense_weights[2], dense_weights[0])
        if phase == 0:
            extra, mats = (cot, sel_own, live3_own), mats
        elif phase == 1:
            extra, mats = (slots, live3_own, live2_own), (weight_qkv,) + mats
        elif phase == 2:
            extra, mats = (cot, sel_own, live2_own), (weight_qkv,) + mats
        else:
            extra, mats = (), (weight_qkv,)
        last = lambda *parts: back_call(near, phase, coords, before, parts, into, extra, mats, cap_mid)
        if near and phase == 3:
            break
        result = list(last(*parts))
        if phase > 0:
            d_firsts[step + 1], total = result[:2]
            sums_one.append(total)
            result = result[2:]
        if phase == 3:
            grad_tokens = result[0]
            break
        d_low, d_gate, d_up, d_middle, d_mid_low, d_mixed, total = result[:7]
        d_seconds[step] = (d_low, d_gate, d_up, d_mid_low)
        sums_two.append(total)
        if phase == 0:
            slots = result[7]
        query, part_a, part_b, weights = records[step][:4]
        if phase < 2:
            d_mixed = order.take(d_mixed)
            d_query, term_a, term_b = attend_back_call(query, d_mixed, part_a, part_b, weights)
            if phase == 0:
                output, term_b = order.take(output, term_b)
            parts = scatter_keys(term_a, term_b, order, near)

        else:
            attend_last = lambda d: attend_back_call(query, d, part_a, part_b, weights)
            gate_grads = lambda *d: grads("cols", [seconds, list(d)])
            down_grads = grads("rows", [hiddens, column(d_seconds, 0)])
            if not near:
                d_query, term_a, term_b = attend_last(d_mixed)
                parts = scatter_keys(term_a, term_b, order, near)
                sums_of = [
                    pair_sum(*g, near)
                    for g in (down_grads, gate_grads(*column(d_seconds, 1)), gate_grads(*column(d_seconds, 2)))
                ]
                continue
            down = Hop(down_grads[1], C_BIT)
            gate_grads_made = wave(
                order, [(down, 0)], gate_grads, column(d_seconds, 1)
            )
            down = BothWays(low_sum(down_grads[0], down.result))
            gate = Hop(gate_grads_made[1], C_BIT)
            d_query, term_a, term_b = wave(order, [(down, 0), (gate, 0)], attend_last, (d_mixed,))
            gate = BlockSums(low_sum(gate_grads_made[0], gate.result))
            far = Hop(term_b, C_BIT)
            up_made = wave(order, [(down, 1), (far, 0)], gate_grads, column(d_seconds, 2))
            own, *others = split_call(term_a, far.result)
            keys, up = KeySums(own, others), Hop(up_made[1], C_BIT)
            wave(order, [(keys, 0), (up, 0)])
            up = BlockSums(low_sum(up_made[0], up.result))
            parts = keys.result

    kv_width = key_weight.shape[1]
    hidden_width = w_gate.shape[1]

    def mixed_grads(*d):
        sums = jnp.concatenate([sum(sums_one), sum(sums_two)], axis=0)
        return grad_call("mixed", block_coords, [firsts, mixeds, list(d), column(d_seconds, 3)], sums)

    def last_grads(*parts):
        d_firsts[0], total, grad_tokens = last(*parts)
        sums_one.append(total)
        return *mixed_grads(*d_firsts), grad_tokens

    placed = {}

    if near:
        def place(kind, widths):
            return lambda near_blocks, far_blocks, at: place_call(kind, at, near_blocks, far_blocks, widths)

        placing = lambda chain: (*chain.result, coords)
        *rest_made, grad_tokens = wave(order, [(gate, 0), (down, 2)], last_grads, parts)
        rest = Hop(rest_made[1], C_BIT)
        wave(order, [(gate, 1), (down, 3), (rest, 0)])
        rest = BlockSums(low_sum(rest_made[0], rest.result))
        wave(order, [(up, 0), (gate, 2), (down, 4)])
        wave(order, [(up, 1), (gate, 3)])
        wave(order, [(rest, 0), (up, 2), (gate, 4)])
        wave(order, [(rest, 1), (up, 3)])
        wave(order, [(rest, 2), (up, 4), (down, 5)])
        placed["down"] = wave(
            order, [(rest, 3), (up, 5), (gate, 5)], place("rows", None), placing(down)
        )
        tokens_back = Move(grad_tokens)

        def place_two(*arrays):
            cols = place("cols", (hidden_width,))
            return *cols(*arrays[:3]), *cols(*arrays[3:])

        placed["gate"], placed["up"] = wave(
            order, [(rest, 4), (tokens_back, 0)], place_two, (*placing(gate), *placing(up))
        )
        grad_tokens = tokens_back.result.astype(F32)
        wave(order, [(rest, 5)])
        placed["rest"] = order.all(
            *place("cols", (width, kv_width, width, kv_width))(*rest.result, order.token)
        )
        (placed["down"],) = placed["down"]
    else:
        sums_of.append(pair_sum(*mixed_grads(*d_firsts), near))
        for name, kind, widths, total in zip(
            ("down", "gate", "up", "rest"),
            ("rows", "cols", "cols", "cols"),
            (None, (hidden_width,), (hidden_width,), (width, kv_width, width, kv_width)),
            sums_of,
            strict=True,
        ):
            mine = lax.dynamic_index_in_dim(total, y, 1, keepdims=False)
            placed[name] = place_call(kind, block_coords, mine[0], mine[1], widths)
        for name in ("down", "gate", "up"):
            (placed[name],) = placed[name]
        grad_tokens = grad_tokens.astype(F32)
    grad_down, grad_gate, grad_up = placed["down"].T, placed["gate"], placed["up"]
    grad_query, grad_key, grad_out, grad_value, gain_sums = placed["rest"]
    grad_key, grad_value = grad_key.T, grad_value.T
    return (
        output.T[None],
        grad_tokens.T[None],
        grad_query,
        grad_key,
        grad_value,
        grad_out,
        grad_gate,
        grad_up,
        grad_down,
        gain_sums[0],
        gain_sums[1],
    )


def solution(mesh):
    rows = P("ws", "ctx", None)
    flat = P("ws", None)
    in_specs = (rows, rows) + (flat,) * 7 + (P("ws"), P("ws"), P()) + (flat,) * 4
    out_specs = (rows, rows) + (flat,) * 7 + (P("ws"), P("ws"))
    return jax.shard_map(
        on_device, mesh=mesh, in_specs=in_specs, out_specs=out_specs, check_vma=False
    )
```

```python
import functools

import jax
import jax.numpy as jnp
from jax import lax
from jax.experimental import pallas as pl
from jax.experimental.pallas import tpu as pltpu
from jax.sharding import PartitionSpec as P

QUERY_HEADS = 15
KEY_VALUE_HEADS = 5
HEAD_SIZE = 64
SHARE = QUERY_HEADS // KEY_VALUE_HEADS
BLK = 64
CONT_BITS = 10
EPSILON = 1e-05
ROPE_BASE = 10000.0
MASK_FLOOR = -1e30
SCALE = HEAD_SIZE ** (-0.5)

BF = jnp.bfloat16
F32 = jnp.float32
AXES = ("ctx", "ws")
FF_CHUNKS = 4
MIB = 1024 * 1024

Y_BIT, C_BIT, X_BIT, Z1_BIT, Z2_BIT = 1, 2, 4, 8, 16
NEAR = (0, X_BIT, Y_BIT, Z1_BIT, X_BIT | Y_BIT | Z1_BIT, X_BIT | Y_BIT, Y_BIT | Z1_BIT, Z1_BIT | X_BIT)


def hop(value, mask):
    return lax.ppermute(value, AXES, [(i, i ^ mask) for i in range(32)])


def swap_place(i):
    y, z2 = i & 1, (i >> 4) & 1
    return (i & ~(Y_BIT | Z2_BIT)) | (Z2_BIT if y else 0) | (Y_BIT if z2 else 0)


def move(value):
    return lax.ppermute(value, AXES, [(i, swap_place(i)) for i in range(32)])


def ctx_mask(mask):
    return (
        (1 if mask & C_BIT else 0)
        | (2 if mask & X_BIT else 0)
        | (4 if mask & Z1_BIT else 0)
        | (8 if mask & Y_BIT else 0)
    )


NT = (((1,), (1,)), ((), ()))
TN = (((0,), (0,)), ((), ()))
NN = (((1,), (0,)), ((), ()))


def mm(left, right, dims=NN, precision=None):
    return lax.dot_general(left, right, dims, precision=precision, preferred_element_type=F32)


def normed_rows(values):
    inverse = lax.rsqrt(jnp.mean(values * values, axis=-1, keepdims=True) + EPSILON)
    return values * inverse, inverse


def norm_back(grad_in, normed, inverse, gain):
    scaled = grad_in * gain
    return inverse * (scaled - normed * jnp.mean(scaled * normed, axis=-1, keepdims=True))


def turn(values, cosine, sine, back=False):
    rows, width = values.shape
    lane = lax.broadcasted_iota(jnp.int32, (rows, 128), 1)
    first = (lane & (HEAD_SIZE - 1)) < HEAD_SIZE // 2
    if back:
        sine = -sine
    pieces = []
    for start in range(0, width, 128):
        wide = min(128, width - start)
        part = values[:, start : start + wide]
        if wide < 128:
            part = jnp.concatenate([part, jnp.zeros((rows, 128 - wide), F32)], axis=1)
        other = jnp.where(first, pltpu.roll(part, 96, 1), pltpu.roll(part, 32, 1))
        pieces.append((part * cosine + other * sine)[:, :wide])
    return jnp.concatenate(pieces, axis=1)


def vm():
    return pl.BlockSpec(memory_space=pltpu.VMEM)


def sm():
    return pl.BlockSpec(memory_space=pltpu.SMEM)


def hbm():
    return pl.BlockSpec(memory_space=pltpu.HBM)


def shaped(shape, dtype):
    return jax.ShapeDtypeStruct(shape, dtype)


def stored(shape, dtype):
    return pltpu.HBM(shape, dtype)


def apart(arrays):
    return [pltpu.with_memory_space_constraint(a, pltpu.HBM) for a in arrays]


def params(mib, **kw):
    return pltpu.CompilerParams(vmem_limit_bytes=mib * MIB, **kw)


def estimate(micros=1.0):
    return pl.CostEstimate(flops=0, bytes_accessed=int(micros * 3.7e6 / 4), transcendentals=0)


class Order:
    def __init__(self, token):
        self.token = token

    def all(self, *values):
        *values, self.token = lax.optimization_barrier(values + (self.token,))
        return values

    def take(self, *values):
        *values, self.token = lax.optimization_barrier(tuple(values) + (self.token,))
        return values[0] if len(values) == 1 else values


def read_coords(ref):
    return [ref[i] for i in range(4)]


class Weight:
    def __init__(self, shape, arrays, groups):
        self.shape, self.arrays, self.groups = shape, arrays, groups


def at_place(ref, place, rows, cols, coords):
    row, col = place(*coords)
    if rows != ref.shape[0] and not isinstance(row, int):
        row = pl.multiple_of(row, 16)
    if cols != ref.shape[1] and not isinstance(col, int):
        col = pl.multiple_of(col, 128)
    if cols == ref.shape[1]:
        return ref if rows == ref.shape[0] else ref.at[pl.ds(row, rows), :]
    return ref.at[pl.ds(row, rows), pl.ds(col, cols)]


def bring(weights, refs, buffers, sems, coords, turns, ahead=3):
    firsts, at = [], 0
    for weight in weights:
        firsts.append(at)
        at += len(weight.arrays)
    copies, count = {}, 0
    for which, group in turns:
        copies[which, group] = []
        for array, rows, cols, source, target in weights[which].groups[group]:
            copies[which, group].append(
                pltpu.make_async_copy(
                    at_place(refs[firsts[which] + array], source, rows, cols, coords),
                    at_place(buffers[which], target, rows, cols, coords),
                    sems.at[count],
                )
            )
            count += 1
    queue = list(turns)

    def start():
        if queue:
            for copy in copies[queue.pop(0)]:
                copy.start()

    for _ in range(ahead):
        start()

    def wait(which, group=0):
        for copy in copies[which, group]:
            copy.wait()
        start()

    return wait


def arrays_of(weights):
    return [a for w in weights for a in w.arrays]


def weights_in(near, weights):
    arrays = arrays_of(weights)
    if near:
        return [vm()] * len(arrays), arrays, []
    return [hbm()] * len(arrays), apart(arrays), scratch_of(weights)


def weights_here(near, weights, refs, scratch, coords_ref, turns):
    if near:
        return refs, lambda *which: None
    buffers, sems = scratch[: len(weights)], scratch[len(weights)]
    return buffers, bring(weights, refs, buffers, sems, read_coords(coords_ref), turns)


def join_kernel(weights, n_bases, coords_ref, *args):
    count = len(arrays_of(weights))
    args = args[n_bases:]
    refs, outs, sems = args[:count], args[count:-1], args[-1]
    turns = [(i, g) for i, w in enumerate(weights) for g in range(len(w.groups))]
    wait = bring(weights, refs, outs, sems, read_coords(coords_ref), turns, len(turns))
    for turn in turns:
        wait(*turn)


def join_call(coords, weights, bases=()):
    arrays = arrays_of(weights)
    return pl.pallas_call(
        functools.partial(join_kernel, weights, len(bases)),
        name="join_weights",
        out_shape=tuple(pltpu.VMEM(w.shape, BF) for w in weights),
        in_specs=[sm()] + [vm()] * len(bases) + [hbm()] * len(arrays),
        out_specs=tuple(vm() for _ in weights),
        scratch_shapes=scratch_of(weights)[-1:],
        input_output_aliases={1 + i: i for i in range(len(bases))},
        compiler_params=params(24),
        cost_estimate=estimate(),
    )(coords, *bases, *apart(arrays))


def part_of_weight(weight, own):
    shift = 0 if own else 1
    groups = [
        [(copy[0] - shift, *copy[1:]) for copy in group if (copy[0] == 0) == own]
        for group in weight.groups
    ]
    return Weight(weight.shape, weight.arrays[:1] if own else weight.arrays[1:], groups)


def scratch_of(weights):
    copies = sum(len(g) for w in weights for g in w.groups)
    return [pltpu.VMEM(w.shape, BF) for w in weights] + [pltpu.SemaphoreType.DMA((copies,))]


def one_piece(array):
    rows, cols = array.shape
    origin = lambda *k: (0, 0)
    return Weight(array.shape, [array], [[(0, rows, cols, origin, origin)]])


def in_columns(array):
    rows, cols = array.shape
    wide = cols // FF_CHUNKS
    place = lambda j: (lambda *k: (0, j * wide))
    return Weight(
        array.shape, [array], [[(0, rows, wide, place(j), place(j))] for j in range(FF_CHUNKS)]
    )


def part_of(j, coords):
    rx, rz = BESIDE[j]
    return (coords[2] ^ rx) * 2 + ((coords[3] & 1) ^ rz)


BESIDE = ((0, 0), (1, 0), (0, 1), (1, 1))


def pack_kernel(coords_ref, q_hbm, k_hbm, v_hbm, own_ref, piece_ref, q_ref, k_ref, v_ref, sems):
    copies = [
        pltpu.make_async_copy(a, b, sems.at[i])
        for i, (a, b) in enumerate(((q_hbm, q_ref), (k_hbm, k_ref), (v_hbm, v_ref)))
    ]
    for copy in copies:
        copy.start()
    half, width = q_ref.shape
    kv_width = k_ref.shape[0]
    end = width + 2 * kv_width
    own_ref[:, end:] = jnp.zeros((half, own_ref.shape[1] - end), BF)
    for copy in copies:
        copy.wait()
    own_ref[:, :width] = q_ref[...]
    own_ref[:, width : width + kv_width] = k_ref[...].T
    own_ref[:, width + kv_width : end] = v_ref[...].T
    depth = half // 2
    start = pl.multiple_of(coords_ref[1] * depth, 16)
    piece_ref[...] = own_ref[pl.ds(start, depth), :]


def pack_call(coords, w_query, key_t, value_t):
    half, width = w_query.shape
    total = -(-(width + 2 * key_t.shape[0]) // 128) * 128
    return pl.pallas_call(
        pack_kernel,
        name="pack",
        out_shape=(stored((half, total), BF), shaped((half // 2, total), BF)),
        in_specs=[sm()] + [hbm()] * 3,
        out_specs=(vm(), vm()),
        scratch_shapes=[pltpu.VMEM(a.shape, BF) for a in (w_query, key_t, value_t)]
        + [pltpu.SemaphoreType.DMA((3,))],
        compiler_params=params(12),
        cost_estimate=estimate(),
    )(coords, *apart([w_query, key_t, value_t]))


def pack_rows_kernel(tokens_ref, plan_ref, out_ref):
    width, rows = tokens_ref.shape
    out_ref[:rows, :] = tokens_ref[...].T
    marks = plan_ref[...].astype(F32).astype(BF)
    out_ref[rows:, : marks.shape[1]] = marks
    out_ref[rows:, marks.shape[1] :] = jnp.zeros((marks.shape[0], width - marks.shape[1]), BF)


def pack_rows_call(tokens_t, plan):
    width, rows = tokens_t.shape
    return pl.pallas_call(
        pack_rows_kernel,
        name="pack_rows",
        out_shape=shaped((rows + plan.shape[0], width), BF),
        in_specs=[vm()] * 2,
        out_specs=vm(),
        compiler_params=params(8),
        cost_estimate=estimate(),
    )(*apart([tokens_t, plan]))


def stack_kernel(*refs):
    out_ref = refs[-1]
    at = 0
    for ref in refs[:-1]:
        out_ref[at : at + ref.shape[0], :] = ref[...]
        at += ref.shape[0]


def stack_call(pieces):
    rows = sum(p.shape[0] for p in pieces)
    return pl.pallas_call(
        stack_kernel,
        name="stack",
        out_shape=shaped((rows, pieces[0].shape[1]), pieces[0].dtype),
        in_specs=[vm()] * len(pieces),
        out_specs=vm(),
        compiler_params=params(8),
        cost_estimate=estimate(),
    )(*pieces)


def split_kernel(total_ref, other_ref, *outs):
    rows = outs[0].shape[0]
    for i, out in enumerate(outs):
        at = slice(i * rows, (i + 1) * rows)
        out[...] = (total_ref[at, :] + other_ref[at, :].astype(F32)).astype(out.dtype)


def split_call(total, other):
    rows, width = total.shape[0] // len(NEAR), total.shape[1]
    outs = [shaped((rows, width), F32)] + [shaped((rows, width), BF)] * (len(NEAR) - 1)
    return pl.pallas_call(
        split_kernel,
        name="split",
        out_shape=tuple(outs),
        in_specs=[vm(), vm()],
        out_specs=tuple(vm() for _ in outs),
        compiler_params=params(10),
        cost_estimate=estimate(),
    )(total, other)


def project(x, gain, wqkv_ref, cosine, sine, first_ref, q_ref, kv_ref):
    normed, _ = normed_rows(x)
    first_in = (normed * gain).astype(BF)
    first_ref[...] = first_in
    rows = mm(first_in, wqkv_ref[...])
    wide = SHARE * HEAD_SIZE
    q_width = KEY_VALUE_HEADS * wide
    kv_width = KEY_VALUE_HEADS * HEAD_SIZE
    key = turn(rows[:, q_width : q_width + kv_width], cosine, sine)
    value = rows[:, q_width + kv_width : q_width + 2 * kv_width]
    for h in range(KEY_VALUE_HEADS):
        at = slice(h * HEAD_SIZE, (h + 1) * HEAD_SIZE)
        kv_ref[:, h * 128 : (h + 1) * 128] = jnp.concatenate(
            [key[:, at], value[:, at]], axis=1
        ).astype(BF)
    query = (turn(rows[:, :q_width], cosine, sine).astype(BF) * SCALE).astype(BF)
    for h in range(KEY_VALUE_HEADS):
        q_ref[h] = query[:, h * wide : (h + 1) * wide]


def first_kernel(near, weights, coords_ref, x_ref, gain_ref, cos_ref, sin_ref, *rest):
    count = len(arrays_of(weights))
    refs, (first_ref, q_ref, kv_ref, *scratch) = rest[:count], rest[count:]
    (wqkv,), wait = weights_here(near, weights, refs, scratch, coords_ref, ((0, 0),))
    wait(0)
    project(
        x_ref[...].astype(F32), gain_ref[...], wqkv, cos_ref[...], sin_ref[...],
        first_ref, q_ref, kv_ref,
    )


def first_call(near, coords, tokens, gain, cosine, sine, weights):
    rows, width = tokens.shape
    specs, arrays, scratch = weights_in(near, weights)
    return pl.pallas_call(
        functools.partial(first_kernel, near, weights),
        name="first_projection",
        out_shape=(
            stored((rows, width), BF),
            shaped((KEY_VALUE_HEADS, rows, SHARE * HEAD_SIZE), BF),
            shaped((rows, KEY_VALUE_HEADS * 128), BF),
        ),
        in_specs=[sm()] + [vm()] * 4 + specs,
        out_specs=(vm(), vm(), vm()),
        scratch_shapes=scratch,
        compiler_params=params(10),
        cost_estimate=estimate(),
    )(coords, tokens, gain, cosine, sine, *arrays)


def padded_heads(wide_rows, left):
    rows = wide_rows.shape[0]
    blank = jnp.zeros((rows, HEAD_SIZE), wide_rows.dtype)
    stacked = []
    for j in range(SHARE):
        part = wide_rows[:, j * HEAD_SIZE : (j + 1) * HEAD_SIZE]
        stacked.append(jnp.concatenate([part, blank] if left else [blank, part], axis=1))
    return jnp.concatenate(stacked, axis=0)


def fill_bias(prompt, kpos_ref, live_ref, qpos_ref, bias_scr, col_scr):
    kpos = kpos_ref[...]
    klive = live_ref[...] > 0
    rows = bias_scr.shape[0]
    square = lambda axis: lax.broadcasted_iota(jnp.int32, (rows, rows), axis)
    own = jnp.where(square(0) == square(1), qpos_ref[...].astype(F32), 0.0)
    col_scr[...] = jnp.sum(own, axis=1, keepdims=True).astype(jnp.int32)
    kseg = jnp.where(kpos < prompt, 0, 1 + ((kpos - prompt) >> CONT_BITS))

    def fill(i, carry):
        at = pl.ds(pl.multiple_of(i * 8, 8), 8)
        qpos = col_scr[at, :]
        qseg = jnp.where(qpos < prompt, 0, 1 + ((qpos - prompt) >> CONT_BITS))
        earlier = kpos <= qpos
        shared = (kseg == 0) | (kseg == qseg)
        seen = earlier & shared & (klive | (kpos == qpos))
        bias_scr[at, :] = jnp.where(seen, 0.0, MASK_FLOOR)
        return carry

    lax.fori_loop(0, bias_scr.shape[0] // 8, fill, 0)


def attend_kernel(prompt, q_ref, a_ref, b_ref, kpos_ref, live_ref, qpos_ref, p_ref, o_ref, bias_scr, col_scr):
    @pl.when(pl.program_id(0) == 0)
    def _():
        fill_bias(prompt, kpos_ref, live_ref, qpos_ref, bias_scr, col_scr)

    o_ref[0] = attend_heads(q_ref, a_ref, b_ref, p_ref, bias_scr)


def attend_heads(q_ref, a_ref, b_ref, p_ref, bias_scr):
    rows = q_ref.shape[1]
    half = a_ref.shape[0]
    together = rows < 128
    if together:
        stacked = padded_heads(q_ref[0], True)
        all_a, all_b = mm(stacked, a_ref[...], NT), mm(stacked, b_ref[...], NT)
    blank = jnp.zeros((rows, HEAD_SIZE), BF)
    outs = []
    for j in range(SHARE):
        at = slice(j * rows, (j + 1) * rows)
        if together:
            s_a, s_b = all_a[at], all_b[at]
        else:
            part = jnp.concatenate([q_ref[0, :, j * HEAD_SIZE : (j + 1) * HEAD_SIZE], blank], axis=1)
            s_a, s_b = mm(part, a_ref[...], NT), mm(part, b_ref[...], NT)
        s_a = s_a + bias_scr[:, :half]
        s_b = s_b + bias_scr[:, half:]
        top = jnp.maximum(
            jnp.max(s_a, axis=-1, keepdims=True), jnp.max(s_b, axis=-1, keepdims=True)
        )
        w_a, w_b = jnp.exp(s_a - top), jnp.exp(s_b - top)
        mass = jnp.sum(w_a, axis=-1, keepdims=True) + jnp.sum(w_b, axis=-1, keepdims=True)
        inverse = 1.0 / mass
        p_a, p_b = (w_a * inverse).astype(BF), (w_b * inverse).astype(BF)
        p_ref[0, at, :half] = p_a
        p_ref[0, at, half:] = p_b
        if not together:
            outs.append((mm(p_a, a_ref[...]) + mm(p_b, b_ref[...]))[:, HEAD_SIZE:])
    if together:
        mixed = mm(p_ref[0, :, :half], a_ref[...]) + mm(p_ref[0, :, half:], b_ref[...])
        outs = [mixed[j * rows : (j + 1) * rows, HEAD_SIZE:] for j in range(SHARE)]
    return jnp.concatenate(outs, axis=1).astype(BF)


def attend_call(query, part_a, part_b, kpos, klive, qpos, prompt):
    heads, rows, wide = query.shape
    half = part_a.shape[0]
    keys = 2 * half
    return pl.pallas_call(
        functools.partial(attend_kernel, prompt),
        name="attend",
        grid=(heads,),
        out_shape=(stored((heads, SHARE * rows, keys), BF), shaped((heads, rows, wide), BF)),
        in_specs=[
            pl.BlockSpec((1, rows, wide), lambda h: (h, 0, 0)),
            pl.BlockSpec((half, 128), lambda h: (0, h)),
            pl.BlockSpec((half, 128), lambda h: (0, h)),
            pl.BlockSpec((1, keys), lambda h: (0, 0)),
            pl.BlockSpec((1, keys), lambda h: (0, 0)),
            pl.BlockSpec((1, rows), lambda h: (0, 0)),
        ],
        out_specs=(
            pl.BlockSpec((1, SHARE * rows, keys), lambda h: (h, 0, 0)),
            pl.BlockSpec((1, rows, wide), lambda h: (h, 0, 0)),
        ),
        scratch_shapes=[pltpu.VMEM((rows, keys), F32), pltpu.VMEM((rows, 1), jnp.int32)],
        compiler_params=params(12 if keys <= 2048 else 56, dimension_semantics=("arbitrary",)),
        cost_estimate=estimate(rows * keys / 17000),
    )(query, part_a, part_b, kpos, klive, qpos)


def attend_back_kernel(q_ref, do_ref, a_ref, b_ref, p_ref, dq_ref, da_ref, db_ref, dp_scr, ds_scr):
    rows = q_ref.shape[1]
    half = a_ref.shape[0]
    stacked = padded_heads(q_ref[0], True)
    grads = padded_heads(do_ref[0], False)
    dp_scr[:, :half] = mm(grads, a_ref[...], NT)
    dp_scr[:, half:] = mm(grads, b_ref[...], NT)

    for j in range(SHARE):
        at = slice(j * rows, (j + 1) * rows)
        weights = p_ref[0, at, :].astype(F32)
        dp = dp_scr[at, :]
        delta = jnp.sum(weights * dp, axis=-1, keepdims=True)
        ds_scr[at, :] = (weights * (dp - delta)).astype(BF)
    dq = (mm(ds_scr[:, :half], a_ref[...]) + mm(ds_scr[:, half:], b_ref[...])) * SCALE
    dq_ref[0] = jnp.concatenate(
        [dq[j * rows : (j + 1) * rows, :HEAD_SIZE] for j in range(SHARE)], axis=1
    )
    for at, out in ((slice(0, half), da_ref), (slice(half, 2 * half), db_ref)):
        turned = mm(stacked, ds_scr[:, at], TN) + mm(grads, p_ref[0, :, at], TN)
        out[...] = turned.T.astype(out.dtype)


def attend_back_call(query, d_out, part_a, part_b, weights):
    heads, rows, wide = query.shape
    half = part_a.shape[0]
    keys = 2 * half
    return pl.pallas_call(
        attend_back_kernel,
        name="attend_back",
        grid=(heads,),
        out_shape=(
            shaped((heads, rows, wide), F32),
            shaped((half, heads * 128), F32),
            shaped((half, heads * 128), BF),
        ),
        in_specs=[
            pl.BlockSpec((1, rows, wide), lambda h: (h, 0, 0)),
            pl.BlockSpec((1, rows, wide), lambda h: (h, 0, 0)),
            pl.BlockSpec((half, 128), lambda h: (0, h)),
            pl.BlockSpec((half, 128), lambda h: (0, h)),
            pl.BlockSpec((1, SHARE * rows, keys), lambda h: (h, 0, 0)),
        ],
        out_specs=(
            pl.BlockSpec((1, rows, wide), lambda h: (h, 0, 0)),
            pl.BlockSpec((half, 128), lambda h: (0, h)),
            pl.BlockSpec((half, 128), lambda h: (0, h)),
        ),
        scratch_shapes=[
            pltpu.VMEM((SHARE * rows, keys), F32),
            pltpu.VMEM((SHARE * rows, keys), BF),
        ],
        compiler_params=params(14 if keys <= 2048 else 60, dimension_semantics=("arbitrary",)),
        cost_estimate=estimate(rows * keys / 22000),
    )(query, d_out, part_a, part_b, *apart([weights]))


def picks(sel_ref, total_rows):
    capacity = sel_ref.shape[1]
    row = lax.broadcasted_iota(jnp.int32, (total_rows, capacity), 0)
    return row == sel_ref[...]


def live_column(live_ref, rows):
    count = jnp.sum(live_ref[:, :].astype(F32), axis=1, keepdims=True)
    return lax.broadcasted_iota(jnp.int32, (rows, 1), 0).astype(F32) < count


def feed_forward(wait, x, mixed, gain_two, wo, wg, wu, wd, ao_out, mid_ref, second_ref, g_ref, u_ref, hid_ref):
    ao_out[...] = mixed
    wait(0)
    middle = x + mm(mixed, wo[...])
    mid_ref[...] = middle
    normed, _ = normed_rows(middle)
    second = (normed * gain_two).astype(BF)
    second_ref[...] = second
    wide = wg.shape[1] // FF_CHUNKS
    for j in range(FF_CHUNKS):
        at = slice(j * wide, (j + 1) * wide)
        wait(1, j)
        g = mm(second, wg[:, at])
        wait(2, j)
        u = mm(second, wu[:, at])
        g_ref[:, at] = g.astype(BF)
        u_ref[:, at] = u.astype(BF)
        hid_ref[:, at] = (g / (1.0 + jnp.exp(-g)) * u).astype(BF)
    wait(3)
    return middle + mm(hid_ref[...], wd[...], NT)


DENSE_TURNS = ((0, 0),) + tuple((w, j) for j in range(FF_CHUNKS) for w in (1, 2)) + ((3, 0),)


def dense_body(near, step, weights, mixed, args):
    args = list(args)
    take = lambda k: [args.pop(0) for _ in range(k)]
    coords_ref, x_ref, gain1_ref, gain2_ref = take(4)
    if step == 0:
        sel_ref, cos_ref, sin_ref = take(3)
    elif step == 1:
        live_ref, cos_ref, sin_ref = take(3)
    else:
        sel_ref, live2_ref, live_ref, h1_ref, h2_ref = take(5)
    refs = take(len(arrays_of(weights)))
    ao_out, mid_ref, second_ref, g_ref, u_ref, hid_ref = take(6)
    if step < 2:
        h_ref, next_ref, first_ref, q_ref, kv_ref = take(5)
    else:
        (out_ref,) = take(1)
    turns = DENSE_TURNS + (((4, 0),) if step < 2 else ())

    def work():
        buffers, wait = weights_here(near, weights, refs, args, coords_ref, turns)
        rows = x_ref.shape[0]
        x = x_ref[...].astype(F32)
        updated = feed_forward(
            wait, x, mixed(), gain2_ref[...], *buffers[:4], ao_out, mid_ref,
            second_ref, g_ref, u_ref, hid_ref,
        )
        if step == 0:
            h_ref[...] = updated
            chosen = picks(sel_ref, rows).astype(F32)
            following = mm(chosen, updated, TN, lax.Precision.HIGHEST)
        else:
            updated = jnp.where(live_column(live_ref, rows), updated, x)
        if step == 1:
            h_ref[...] = updated
            following = updated[: next_ref.shape[0]]
        if step < 2:
            next_ref[...] = following
            wait(4)
            project(
                following, gain1_ref[...], buffers[4], cos_ref[...], sin_ref[...],
                first_ref, q_ref, kv_ref,
            )
        else:
            slots = jnp.concatenate([updated, h2_ref[rows:, :]], axis=0).astype(BF)
            hit = picks(sel_ref, h1_ref.shape[0]) & (live2_ref[...] > 0)
            placed = mm(hit.astype(BF), slots)
            any_hit = jnp.sum(hit.astype(F32), axis=1, keepdims=True) > 0.5
            out_ref[...] = jnp.where(any_hit, placed, h1_ref[...]).T.astype(BF)

    return work


def joined_heads(ao_ref):
    return jnp.concatenate([ao_ref[h] for h in range(KEY_VALUE_HEADS)], axis=1)


def dense_kernel(near, step, weights, ao_ref, *args):
    dense_body(near, step, weights, lambda: joined_heads(ao_ref), args)()


def dense_outs(step, x, weights, next_rows):
    rows, width = x.shape
    hidden = weights[1].shape[1]
    outs = [
        stored((rows, width), BF),
        stored((rows, width), F32),
        stored((rows, width), BF),
        stored((rows, hidden), BF),
        stored((rows, hidden), BF),
        stored((rows, hidden), BF),
    ]
    if step < 2:
        outs += [
            stored((rows, width), F32),
            shaped((next_rows, width), F32),
            stored((next_rows, width), BF),
            shaped((KEY_VALUE_HEADS, next_rows, SHARE * HEAD_SIZE), BF),
            shaped((next_rows, KEY_VALUE_HEADS * 128), BF),
        ]
    else:
        outs += [stored((width, next_rows), BF)]
    return outs


def dense_call(near, step, coords, x, mixed, gain1, gain2, extra, weights, next_rows):
    specs, arrays, scratch = weights_in(near, weights)
    outs = dense_outs(step, x, weights, next_rows)
    return pl.pallas_call(
        functools.partial(dense_kernel, near, step, weights),
        name=f"dense_{step}",
        out_shape=tuple(outs),
        in_specs=[vm(), sm()] + [vm()] * (3 + len(extra)) + specs,
        out_specs=tuple(vm() for _ in outs),
        scratch_shapes=scratch,
        compiler_params=params(12 if near else 50),
        cost_estimate=estimate(6),
    )(mixed, coords, x, gain1, gain2, *extra, *arrays)


def feed_back(wait, first, d_y, mid_ref, g_ref, u_ref, gain_two, wd, wg, wu, wo, dyb_ref, dg_ref, du_ref, dmid_ref, dz_ref, dao_ref, sum_ref):
    d_low = d_y.astype(BF)
    dyb_ref[...] = d_low
    wide = wg.shape[1] // FF_CHUNKS
    d_second = jnp.zeros(d_y.shape, F32)
    wait(first)
    for j in range(FF_CHUNKS):
        at = slice(j * wide, (j + 1) * wide)
        d_hidden = mm(d_low, wd[:, at])
        g, u = g_ref[:, at].astype(F32), u_ref[:, at].astype(F32)
        sigma = 1.0 / (1.0 + jnp.exp(-g))
        d_gate = (d_hidden * u * sigma * (1.0 + g * (1.0 - sigma))).astype(BF)
        d_up = (d_hidden * (g * sigma)).astype(BF)
        dg_ref[:, at] = d_gate
        du_ref[:, at] = d_up
        wait(first + 1, j)
        wait(first + 2, j)
        d_second += mm(d_gate, wg[:, at], NT) + mm(d_up, wu[:, at], NT)
    normed, inverse = normed_rows(mid_ref[...])
    sum_ref[...] = jnp.sum(d_second * normed, axis=0, keepdims=True)
    d_mid = norm_back(d_second, normed, inverse, gain_two) + d_y
    dmid_ref[...] = d_mid
    d_low = d_mid.astype(BF)
    dz_ref[...] = d_low
    wait(first + 3)
    d_mixed = mm(d_low, wo[...], NT).astype(BF)
    wide = SHARE * HEAD_SIZE
    for h in range(KEY_VALUE_HEADS):
        dao_ref[h] = d_mixed[:, h * wide : (h + 1) * wide]


def project_back(own_ref, others, dq_ref, x, dmid_ref, gain_one, cosine, sine, wait, wqkv, dqkv_ref, sum_ref):
    total = own_ref[...].astype(F32)
    for other in others:
        total = total + other[...].astype(F32)
    d_key = jnp.concatenate(
        [total[:, h * 128 : h * 128 + HEAD_SIZE] for h in range(KEY_VALUE_HEADS)], axis=1
    )
    d_value = jnp.concatenate(
        [total[:, h * 128 + HEAD_SIZE : (h + 1) * 128] for h in range(KEY_VALUE_HEADS)], axis=1
    )
    d_query = jnp.concatenate([dq_ref[h] for h in range(KEY_VALUE_HEADS)], axis=1)
    d_rows = jnp.concatenate(
        [turn(d_query, cosine, sine, True), turn(d_key, cosine, sine, True), d_value], axis=1
    ).astype(BF)
    dqkv_ref[...] = d_rows
    wait(0)
    d_first = mm(d_rows, wqkv[:, : d_rows.shape[1]], NT)
    normed, inverse = normed_rows(x)
    sum_ref[...] = jnp.sum(d_first * normed, axis=0, keepdims=True)
    return norm_back(d_first, normed, inverse, gain_one) + dmid_ref[...]


def back_kernel(near, phase, weights, n_parts, *args):
    args = list(args)
    take = lambda k: [args.pop(0) for _ in range(k)]
    (coords_ref,) = take(1)
    if phase > 0:
        gain1_ref, cos_ref, sin_ref, x_ref, dmid_in, dq_ref = take(6)
        own_ref, *others = take(n_parts)
    if phase < 3:
        gain2_ref, mid_ref, g_ref, u_ref = take(4)
    if phase == 0:
        cot_ref, sel_ref, live3_ref = take(3)
    elif phase == 1:
        slots_ref, live3_ref, live2_ref = take(3)
    elif phase == 2:
        cot_ref, sel_ref, live2_ref = take(3)
    refs = take(len(arrays_of(weights)))
    if phase > 0:
        dqkv_ref, sum1_ref = take(2)
    if phase < 3:
        outs = take(7)
    if phase == 0:
        (slots_out,) = take(1)
    elif phase == 3:
        (grad_ref,) = take(1)
    turns = ((0, 0),) if phase > 0 else ()
    first = len(turns)
    if phase < 3:
        turns += ((first, 0),)
        turns += tuple((first + w, j) for j in range(FF_CHUNKS) for w in (1, 2))
        turns += ((first + 3, 0),)
    buffers, wait = weights_here(near, weights, refs, args, coords_ref, turns)
    if phase > 0:
        d_x = project_back(
            own_ref, others, dq_ref, x_ref[...].astype(F32), dmid_in, gain1_ref[...],
            cos_ref[...], sin_ref[...], wait, buffers[0], dqkv_ref, sum1_ref,
        )
    if phase == 0:
        chosen = picks(sel_ref, cot_ref.shape[1]).astype(BF)
        slots = mm(chosen, cot_ref[...].T, TN)
        slots_out[...] = slots
        rows = mid_ref.shape[0]
        d_y = jnp.where(live_column(live3_ref, rows), slots[:rows], 0.0)
    elif phase == 1:
        rows = x_ref.shape[0]
        slots = slots_ref[...]
        head = jnp.where(live_column(live3_ref, rows), d_x, slots[:rows])
        slots = jnp.concatenate([head, slots[rows:]], axis=0)
        d_y = jnp.where(live_column(live2_ref, slots.shape[0]), slots, 0.0)
    elif phase == 2:
        hit = picks(sel_ref, cot_ref.shape[1]) & (live2_ref[...] > 0)
        placed = mm(hit.astype(F32), d_x, NN, lax.Precision.HIGHEST)
        any_hit = jnp.sum(hit.astype(F32), axis=1, keepdims=True) > 0.5
        d_y = jnp.where(any_hit, placed, cot_ref[...].astype(F32).T)
    else:
        grad_ref[...] = d_x.T.astype(BF)
        return
    feed_back(
        wait, first, d_y, mid_ref, g_ref, u_ref, gain2_ref[...],
        *buffers[first : first + 4], *outs,
    )


def back_call(near, phase, coords, before, parts, into, extra, weights, rows_next):
    specs, arrays, scratch = weights_in(near, weights)
    ins = list(before) + list(parts) + list(into) + list(extra)
    outs = []
    if phase > 0:
        rows, width = before[3].shape
        qkv_width = width + 2 * KEY_VALUE_HEADS * HEAD_SIZE
        outs += [stored((rows, qkv_width), BF), stored((1, width), F32)]
    if phase < 3:
        rows, hidden = into[2].shape
        width = into[1].shape[1]
        outs += [
            stored((rows, width), BF),
            stored((rows, hidden), BF),
            stored((rows, hidden), BF),
            stored((rows, width), F32),
            stored((rows, width), BF),
            shaped((KEY_VALUE_HEADS, rows, SHARE * HEAD_SIZE), BF),
            stored((1, width), F32),
        ]
    if phase == 0:
        outs += [stored((rows_next, width), F32)]
    elif phase == 3:
        outs += [stored((width, rows), BF)]
    return pl.pallas_call(
        functools.partial(back_kernel, near, phase, weights, len(parts)),
        name=f"back_{phase}",
        out_shape=tuple(outs),
        in_specs=[sm()] + [vm()] * len(ins) + specs,
        out_specs=tuple(vm() for _ in outs),
        scratch_shapes=scratch,
        compiler_params=params(12 if near else 50),
        cost_estimate=estimate(6),
    )(coords, *before, *parts, *into[:1], *apart(into[1:]), *extra, *arrays)


def stack_rows(refs, scratch):
    at = 0
    for ref in refs:
        scratch[at : at + ref.shape[0], :] = ref[...]
        at += ref.shape[0]


SPARE = 8


def put_blocks(value, x_of, coords, ref, spare=None):
    y, _, _, z = coords
    depth = value.shape[0] // 8
    for ya in range(2):
        for za in range(4):
            row = (ya * 4 + za) * depth
            block = value[row : row + depth].astype(BF)
            if spare is None:
                ref[y ^ ya, x_of, z ^ za] = block
            else:
                ref[y ^ ya, x_of, z ^ za, :depth] = block
                ref[y ^ ya, x_of, z ^ za, depth:] = spare(ya, za).astype(BF)


def grad_cols_kernel(n_steps, coords_ref, *args):
    left, args = args[:n_steps], args[n_steps:]
    right, args = args[:n_steps], args[n_steps:]
    keep_ref, send_ref, l_scr, r_scr = args
    coords = read_coords(coords_ref)
    _, c, x, _ = coords
    stack_rows(left, l_scr)
    stack_rows(right, r_scr)
    block = keep_ref.shape[-1]
    for far, ref in ((1, send_ref), (0, keep_ref)):

        def body(rx, carry, far=far, ref=ref):
            start = pl.multiple_of(((c ^ far) * 2 + (x ^ rx)) * block, 128)
            value = mm(l_scr[...], r_scr[:, pl.ds(start, block)], TN)
            put_blocks(value, rx, coords, ref)
            return carry

        lax.fori_loop(0, 2, body, 0)


def grad_rows_kernel(n_steps, coords_ref, *args):
    left, args = args[:n_steps], args[n_steps:]
    right, args = args[:n_steps], args[n_steps:]
    keep_ref, send_ref, l_scr, r_scr = args
    coords = read_coords(coords_ref)
    y, c, x, z = coords
    stack_rows(left, l_scr)
    stack_rows(right, r_scr)
    depth = keep_ref.shape[-2]
    span = 8 * depth
    for far, ref in ((1, send_ref), (0, keep_ref)):

        def body(ry, carry, far=far, ref=ref):
            start = pl.multiple_of(((y ^ ry) * 2 + (c ^ far)) * span, 128)
            value = mm(l_scr[:, pl.ds(start, span)], r_scr[...], TN)
            for xa in range(2):
                for za in range(4):
                    row = (xa * 4 + za) * depth
                    ref[ry, x ^ xa, z ^ za] = value[row : row + depth].astype(BF)
            return carry

        lax.fori_loop(0, 2, body, 0)


def grad_mixed_kernel(n_steps, coords_ref, sums_ref, *args):
    groups = []
    for _ in range(4):
        groups.append(args[:n_steps])
        args = args[n_steps:]
    keep_ref, send_ref, first_scr, mixed_scr, qkv_scr, z_scr, val_scr = args
    coords = read_coords(coords_ref)
    _, c, x, _ = coords
    for refs, scr in zip(groups, (first_scr, mixed_scr, qkv_scr, z_scr), strict=True):
        stack_rows(refs, scr)
    block = keep_ref.shape[-1]
    width = z_scr.shape[1]
    kv_width = (qkv_scr.shape[1] - width) // 2
    for ca in range(2):
        for xa in range(2):
            if ca == 0:
                val_scr[...] = mm(first_scr[...], qkv_scr[:, xa * block : (xa + 1) * block], TN)
            elif xa == 0:
                val_scr[...] = mm(mixed_scr[...], z_scr[:, :block], TN)
            else:
                val_scr[...] = jnp.concatenate(
                    [
                        mm(mixed_scr[...], z_scr[:, block:], TN),
                        mm(first_scr[...], qkv_scr[:, width + kv_width :], TN),
                    ],
                    axis=1,
                )

            def spare(ya, za, first=ca == 0 and xa == 0):
                if not first or za:
                    return jnp.zeros((SPARE, block), F32)
                half = width // 2
                rows = sums_ref[:, ya * half : (ya + 1) * half]
                rows = jnp.concatenate([rows, jnp.zeros((2, block - half), F32)], axis=1)
                return jnp.concatenate([rows, jnp.zeros((SPARE - 2, block), F32)], axis=0)

            @pl.when(c == ca)
            def _(xa=xa, spare=spare):
                put_blocks(val_scr[...], x ^ xa, coords, keep_ref, spare)

            @pl.when(c != ca)
            def _(xa=xa, spare=spare):
                put_blocks(val_scr[...], x ^ xa, coords, send_ref, spare)


def grad_call(kind, coords, groups, sums=None):
    n_steps = len(groups[0])
    rows = sum(a.shape[0] for a in groups[0])
    width, cols = groups[0][0].shape[1], groups[1][0].shape[1]
    scratch = [pltpu.VMEM((rows, g[0].shape[1]), BF) for g in groups]
    if kind == "rows":
        kernel, block = grad_rows_kernel, (width // 32, cols)
    elif kind == "cols":
        kernel, block = grad_cols_kernel, (width // 8, cols // 4)
    else:
        total = sum(g[0].shape[1] for g in groups[2:])
        kernel, block = grad_mixed_kernel, (width // 8 + SPARE, total // 4)
        scratch += [pltpu.VMEM((width, block[1]), F32)]
    out = shaped((2, 2, 4) + block, BF)
    ins = [a for g in groups for a in g]
    if sums is not None:
        ins = [sums, *ins]
    return pl.pallas_call(
        functools.partial(kernel, n_steps),
        name=f"grad_{kind}",
        out_shape=(out, out),
        in_specs=[sm()] + [vm()] * len(ins),
        out_specs=(vm(), vm()),
        scratch_shapes=scratch,
        compiler_params=params(16),
        cost_estimate=estimate(6),
    )(coords, *apart(ins))


def place_cols_kernel(coords_ref, near_ref, far_ref, *outs):
    _, c, x, z = read_coords(coords_ref)
    block = near_ref.shape[-1]
    mixed = len(outs) > 1
    target = outs[5] if mixed else outs[0]
    depth = target.shape[0]
    for far, ref in ((0, near_ref), (1, far_ref)):
        for rx in range(2):
            cols = pl.ds(pl.multiple_of(((c ^ far) * 2 + (x ^ rx)) * block, 128), block)
            target[:, cols] = ref[rx, 0, :depth].astype(F32)
    if mixed:
        q_ref, k_ref, o_ref, v_ref, gains_ref, _, k_scr, v_scr = outs
        width, kv_width = q_ref.shape[1], k_ref.shape[0]
        rows = pl.ds(pl.multiple_of((z ^ pl.program_id(0)) * depth, 8), depth)
        q_ref[...] = target[:, :width]
        k_scr[rows, :] = target[:, width : width + kv_width]
        o_ref[...] = target[:, width + kv_width : 2 * width + kv_width]
        v_scr[rows, :] = target[:, 2 * width + kv_width :]
        for far, ref in ((0, near_ref), (1, far_ref)):

            @pl.when((z == pl.program_id(0)) & (c == far))
            def _(ref=ref):
                spare = ref[x, 0, depth:].astype(F32)
                gains_ref[...] = spare[:2, : gains_ref.shape[1]]

        @pl.when(pl.program_id(0) == 3)
        def _():
            k_ref[...] = k_scr[...].T
            v_ref[...] = v_scr[...].T


def place_rows_kernel(coords_ref, near_ref, far_ref, out_ref, scr):
    _, _, x, z = read_coords(coords_ref)
    depth = near_ref.shape[-2]

    def put(ref):
        for rx in range(2):
            for rz in range(4):
                row = pl.multiple_of(((x ^ rx) * 4 + (z ^ rz)) * depth, 8)
                scr[pl.ds(row, depth), :] = ref[rx, rz].astype(F32)

    @pl.when(pl.program_id(0) == 0)
    def _():
        put(near_ref)

    @pl.when(pl.program_id(0) == 1)
    def _():
        put(far_ref)

    out_ref[...] = scr[...].T


def place_call(kind, coords, near, far, widths):
    depth, block = near.shape[-2:]
    scratch = []
    if kind == "rows":
        kernel, grid = place_rows_kernel, (2,)
        outs = (stored((block, 16 * depth), F32),)
        source = pl.BlockSpec((2, 4, depth, block), lambda f, k: (0, 0, 0, 0))
        targets = (pl.BlockSpec((block, 8 * depth), lambda f, k: (0, k[1] ^ f)),)
        scratch = [pltpu.VMEM((8 * depth, block), F32)]
    else:
        kernel, grid = place_cols_kernel, (4,)
        source = pl.BlockSpec((2, 1, *near.shape[-2:]), lambda i, k: (0, i, 0, 0))
        if len(widths) > 1:
            depth -= SPARE
        straight = lambda w: (
            stored((4 * depth, w), F32), pl.BlockSpec((depth, w), lambda i, k: (k[3] ^ i, 0))
        )
        turned = lambda w: (
            stored((w, 4 * depth), F32), pl.BlockSpec((w, 4 * depth), lambda i, k: (0, 0))
        )
        outs, targets = zip(
            *((turned if i % 2 else straight)(w) for i, w in enumerate(widths)), strict=True
        )
        if len(outs) > 1:
            outs += (stored((2, 4 * depth), F32),)
            targets += (pl.BlockSpec((2, 4 * depth), lambda i, k: (0, 0)),)
            scratch = [pltpu.VMEM((depth, 4 * block), F32)]
            scratch += [pltpu.VMEM((4 * depth, w), F32) for w in widths[1::2]]
    return pl.pallas_call(
        kernel,
        name=f"place_{kind}",
        grid_spec=pltpu.PrefetchScalarGridSpec(
            num_scalar_prefetch=1,
            grid=grid,
            in_specs=[source, source],
            out_specs=targets,
            scratch_shapes=scratch,
        ),
        out_shape=outs,
        compiler_params=params(12),
        cost_estimate=estimate(),
    )(coords, near, far)


def low_sum(left, right):
    return (left.astype(F32) + right.astype(F32)).astype(BF)


def split_list(values, count):
    return values[:count], values[count:]


def gather_keys(kv, order, near, meanwhile=([], [])):
    if not near:
        whole = lax.all_gather(kv, "ctx", axis=0, tiled=True)
        half = whole.shape[0] // 2
        return whole[:half], whole[half:]
    kv = order.take(kv)
    hops = [hop(kv, m) for m in (X_BIT, Y_BIT, Z1_BIT, X_BIT | Y_BIT | Z1_BIT)]
    (by_x, by_y, by_z, across), meanwhile[0][:] = split_list(order.all(*hops, *meanwhile[0]), 4)
    hops = [hop(by_x, Y_BIT), hop(by_y, Z1_BIT), hop(by_z, X_BIT)]
    hops, meanwhile[1][:] = split_list(order.all(*hops, *meanwhile[1]), 3)
    part = stack_call([kv, by_x, by_y, by_z, across, *hops])
    return part, order.take(hop(part, C_BIT))


class KeySums:
    def __init__(self, own, others):
        self.own = own
        self.near, self.across, self.beyond = others[:3], others[3], others[4:]

    def sends(self, turn):
        if turn == 0:
            return list(zip(self.beyond, (Y_BIT, Z1_BIT, X_BIT), strict=True))
        return [
            (self.across, X_BIT | Y_BIT | Z1_BIT),
            *zip(self.near, (X_BIT, Y_BIT, Z1_BIT), strict=True),
        ]

    def got(self, turn, values):
        if turn == 0:
            self.near = [low_sum(a, b) for a, b in zip(self.near, values, strict=True)]
        else:
            self.result = [self.own, *values]


class Hop:
    def __init__(self, value, mask):
        self.value, self.mask = value, mask

    def sends(self, turn):
        return [(self.value, self.mask)]

    def got(self, turn, values):
        (self.result,) = values


def scatter_keys(part_a, part_b, order, near):
    if not near:
        whole = jnp.concatenate([part_a, part_b.astype(F32)], axis=0)
        return [lax.psum_scatter(whole, "ctx", scatter_dimension=0, tiled=True)]
    far = Hop(part_b, C_BIT)
    (part_a,) = wave(order, [(far, 0)], lambda a: (a,), (part_a,))
    own, *others = split_call(part_a, far.result)
    sums = KeySums(own, others)
    wave(order, [(sums, 0)])
    wave(order, [(sums, 1)])
    return sums.result


def cut_rows(value, index, count):
    size = value.shape[0] // count
    return lax.dynamic_slice_in_dim(value, index * size, size, 0)


def cut_cols(value, index, count):
    size = value.shape[1] // count
    return lax.dynamic_slice_in_dim(value, index * size, size, 1)


class Share:
    def __init__(self, mine):
        self.mine = mine

    def sends(self, turn):
        return [(self.mine, mask) for mask in (X_BIT | Z1_BIT, X_BIT, Z1_BIT)]

    def got(self, turn, values):
        across, by_x, by_z = values
        self.result = [self.mine, by_x, by_z, across]


def pair_sum(keep, send, near):
    if near:
        return low_sum(keep, hop(send, C_BIT))
    return lax.psum(jnp.stack([keep, send]).astype(F32), AXES)


ALONG_Z = (Z1_BIT, Z2_BIT, Z1_BIT | Z2_BIT)
FAR_FIRST = (2, 1, 0)


class BlockSums:
    rounds = 6

    def __init__(self, total):
        self.total = total

    def sends(self, turn):
        if turn == 0:
            return [(self.total[1, 1], Y_BIT)]
        if turn == 1:
            return [(self.total[1, 0], Y_BIT), (low_sum(self.total[0, 1], self.came), X_BIT)]
        if turn == 2:
            return [(self.total[i + 1], ALONG_Z[i]) for i in FAR_FIRST]
        if turn == 3:
            return [(self.mine, ALONG_Z[i]) for i in FAR_FIRST]
        if turn == 4:
            return [(self.total, X_BIT)]
        return [(self.total, C_BIT)]

    def got(self, turn, values):
        if turn == 0:
            (self.came,) = values
        elif turn == 1:
            total = self.total[0, 0].astype(F32)
            for value in values:
                total = total + value.astype(F32)
            self.total = total.astype(BF)
        elif turn == 2:
            mine = self.total[0].astype(F32)
            for value in values:
                mine = mine + value.astype(F32)
            self.mine = mine.astype(BF)
        elif turn == 3:
            self.total = jnp.stack([self.mine, *values[::-1]])
        elif turn == 4:
            self.total = jnp.stack([self.total, *values])
        else:
            self.result = (self.total, *values)


class BothWays(BlockSums):
    def sends(self, turn):
        if turn == 0:
            return [(self.total[1, :, :2], Y_BIT), (self.total[:, 1, 2:], X_BIT)]
        if turn == 1:
            return [(self.first[1], X_BIT), (self.second[1], Y_BIT)]
        return super().sends(turn)

    def got(self, turn, values):
        if turn == 0:
            self.first = low_sum(self.total[0, :, :2], values[0])
            self.second = low_sum(self.total[:, 0, 2:], values[1])
        elif turn == 1:
            self.total = jnp.concatenate(
                [low_sum(self.first[0], values[0]), low_sum(self.second[0], values[1])]
            )
        else:
            super().got(turn, values)


class Move:
    rounds = 1

    def __init__(self, value):
        self.value = value

    def sends(self, turn):
        return [(self.value, None)]

    def got(self, turn, values):
        (self.result,) = values


def wave(order, steps, work=None, uses=()):
    plans = [chain.sends(turn) for chain, turn in steps]
    flat = [value for plan in plans for value, _ in plan]
    taken = order.all(*flat, *uses)
    sent, uses = taken[: len(flat)], taken[len(flat) :]
    masks = [mask for plan in plans for _, mask in plan]
    came = [move(v) if mask is None else hop(v, mask) for v, mask in zip(sent, masks, strict=True)]
    made = list(work(*uses)) if work else []
    came = order.all(*came, *made)
    came, made = came[: len(flat)], came[len(flat) :]
    for (chain, turn), plan in zip(steps, plans, strict=True):
        chain.got(turn, came[: len(plan)])
        came = came[len(plan) :]
    return made


def on_device(
    tokens, cotangent, w_query, key_weight, value_weight, w_out, w_gate, w_up, w_down,
    gain_attn, gain_ffn, block_order, sel_mid, live_mid, sel_last, live_last,
):
    ctx_count, ws_count = lax.axis_size("ctx"), lax.axis_size("ws")
    near = ctx_count == 16 and ws_count == 2
    ctx, y = lax.axis_index("ctx"), lax.axis_index("ws")
    tok_local = tokens.shape[1]
    cap_mid, cap_last = sel_mid.shape[1] // ctx_count, sel_last.shape[1] // ctx_count
    if near:
        c, x, z = ctx & 1, (ctx >> 1) & 1, ctx >> 2
        places = (y, c, x, z)
        here = (ctx & 7) | (y << 3)
        turn_order = here ^ jnp.array([ctx_mask(m) for m in NEAR] + [ctx_mask(m) | 1 for m in NEAR], jnp.int32)
        relocate = move
    else:
        zero = jnp.int32(0)
        places = (y, zero, zero, zero)
        here = ctx
        turn_order = jnp.arange(ctx_count, dtype=jnp.int32)
        relocate = lambda v: v
    coords = jnp.stack([jnp.asarray(v, jnp.int32) for v in places])
    block_coords = coords if near else jnp.zeros((4,), jnp.int32)
    width = tokens.shape[2]
    half = w_query.shape[0]
    plan = jnp.concatenate(
        [
            sel_mid.reshape(ctx_count, cap_mid),
            live_mid.reshape(ctx_count, cap_mid),
            live_last.reshape(ctx_count, cap_last),
        ],
        axis=1,
    )
    order = Order(coords)
    if near:
        assert tok_local <= 256
        own_qkv, piece = pack_call(coords, w_query, key_weight.T, value_weight.T)
        fetched = hop(piece, Y_BIT)
        tok = move(pack_rows_call(tokens[0].T, plan))
        gains = jnp.concatenate([gain_attn.reshape(1, -1), gain_ffn.reshape(1, -1)], axis=0)
        beyond = hop(gains, Y_BIT)
        quad = x * 2 + (z & 1)
        own_down = w_down.T
        fetched, cut_pair, cut_out, cut_down = order.take(
            fetched,
            jnp.concatenate([cut_cols(cut_rows(w, c, 2), quad, 4) for w in (w_gate, w_up)], axis=0),
            cut_rows(w_out, c, 2),
            cut_rows(own_down, c, 2),
        )
        far = hop(fetched, C_BIT)
        pair_mine, out_mine = hop(cut_pair, Y_BIT), hop(cut_out, Y_BIT)
        far, tok, beyond = order.take(far, tok, beyond)
        plan = tok[tok_local:, : plan.shape[1]].astype(jnp.int32)
        tok = tok[:tok_local]
        depth = half // 2
        gains = jnp.where(
            y == 0,
            jnp.concatenate([gains, beyond], axis=1),
            jnp.concatenate([beyond, gains], axis=1),
        )
        gains = [gains[0:1], gains[1:2]]
        origin = lambda *k: (0, 0)

        def in_rows(own, mine, other):
            wide = own.shape[1]
            return Weight(
                (2 * half, wide),
                [own, mine, other],
                [
                    [
                        (0, half, wide, origin, lambda ky, kc, kx, kz: (ky * half, 0)),
                        (1, depth, wide, origin, lambda ky, kc, kx, kz: ((1 - ky) * half + kc * depth, 0)),
                        (2, depth, wide, origin, lambda ky, kc, kx, kz: ((1 - ky) * half + (1 - kc) * depth, 0)),
                    ]
                ],
            )

        def in_parts(own, mine, other, which):
            wide = mine.shape[1]
            groups = []
            for j in range(FF_CHUNKS):
                column = lambda *k, j=j: part_of(j, k) * wide
                block = lambda *k, j=j: ((2 * j + which) * depth, 0)
                groups.append(
                    [
                        (0, half, wide,
                         lambda *k, column=column: (0, column(*k)),
                         lambda *k, column=column: (k[0] * half, column(*k))),
                        (1, depth, wide, block,
                         lambda *k, column=column: ((1 - k[0]) * half + k[1] * depth, column(*k))),
                        (2, depth, wide, block,
                         lambda *k, column=column: ((1 - k[0]) * half + (1 - k[1]) * depth, column(*k))),
                    ]
                )
            return Weight((2 * half, own.shape[1]), [own, mine, other], groups)

        weight_qkv = one_piece(join_call(coords, (in_rows(own_qkv, fetched, far),))[0])
        marks = {}

        def fetch_rest(pair, out, down):
            pair = stack_call(pair)
            shared = [Hop(v, C_BIT) for v in (pair, out, down)]
            wide = own_down.shape[1]

            def whole_weights(pair_far, out_far, down_far):
                weight_d = Weight(
                    (width, 2 * wide),
                    [own_down, down, down_far],
                    [
                        [
                            (0, width, wide, origin, lambda ky, kc, kx, kz: (0, ky * wide)),
                            (1, width // 2, wide, origin, lambda ky, kc, kx, kz: (kc * (width // 2), (1 - ky) * wide)),
                            (2, width // 2, wide, origin, lambda ky, kc, kx, kz: ((1 - kc) * (width // 2), (1 - ky) * wide)),
                        ]
                    ],
                )
                return (
                    in_rows(w_out, out, out_far),
                    in_parts(w_gate, pair, pair_far, 0),
                    in_parts(w_up, pair, pair_far, 1),
                    weight_d,
                )

            begun = [part_of_weight(w, True) for w in whole_weights(pair, out, down)]
            bases = wave(order, [(s, 0) for s in shared], lambda k: join_call(k, begun), (coords,))
            rest = whole_weights(*(s.result for s in shared))
            joined = join_call(coords, [part_of_weight(w, False) for w in rest], bases)
            return tuple(one_piece(w) for w in joined)
    else:
        tok = tokens[0]
        whole = lambda w: lax.all_gather(w, "ws", axis=0, tiled=True)
        weight_qkv = one_piece(whole(jnp.concatenate([w_query, key_weight, value_weight], axis=1)))
        gains = [whole(g).reshape(1, -1) for g in (gain_attn, gain_ffn)]
        far_weights = (
            one_piece(whole(w_out)), in_columns(whole(w_gate)), in_columns(whole(w_up)),
            one_piece(whole(w_down).T),
        )
        fetch_rest = lambda: far_weights
    gain1, gain2 = (g.astype(F32) for g in gains)

    per_device = tok_local // BLK
    blocks = jnp.take(block_order.reshape(ctx_count, per_device), turn_order, axis=0)
    plan_order = jnp.take(plan, turn_order, axis=0)
    sel_all = plan_order[:, :cap_mid]
    live_two = plan_order[:, cap_mid : 2 * cap_mid]
    live_three = plan_order[:, 2 * cap_mid :]
    place_one = (blocks[:, :, None] * BLK + jnp.arange(BLK, dtype=jnp.int32)).reshape(ctx_count, tok_local)
    place_two = sum(
        jnp.where(sel_all // BLK == k, blocks[:, k : k + 1], 0) for k in range(per_device)
    ) * BLK + sel_all % BLK
    place_three = place_two[:, :cap_last]
    if near:
        mine = lambda v: v[0:1]
    else:
        mine = lambda v: lax.dynamic_slice_in_dim(v, here, 1, 0)
    sel_own, live2_own, live3_own = mine(sel_all), mine(live_two), mine(live_three)
    own_places = jnp.concatenate([mine(place_one), mine(place_two)], axis=1).reshape(-1, 1)
    frequency = ROPE_BASE ** (-jnp.arange(HEAD_SIZE // 2, dtype=F32) / (HEAD_SIZE // 2))
    angles = own_places.astype(F32) * frequency[None, :]
    cosine, sine = jnp.cos(angles), jnp.sin(angles)
    cosine = jnp.concatenate([cosine] * 4, axis=1)
    sine = jnp.concatenate([-sine, sine, -sine, sine], axis=1)
    tables = [
        (cosine[:tok_local], sine[:tok_local]),
        (cosine[tok_local:], sine[tok_local:]),
        (cosine[tok_local : tok_local + cap_last], sine[tok_local : tok_local + cap_last]),
    ]
    query_places = [mine(v) for v in (place_one, place_two, place_three)]
    key_places = [v.reshape(1, -1) for v in (place_one, place_two, place_three)]
    key_live = [
        jnp.ones((1, ctx_count * tok_local), jnp.int32),
        live_two.reshape(1, -1),
        live_three.reshape(1, -1),
    ]
    prompt = ctx_count * tok_local // 2
    if near:
        key_places[0], query_places[0] = order.take(key_places[0], query_places[0])
        marks["places"] = [*query_places[1:], *key_places[1:], *key_live[1:], sel_own, live2_own, live3_own]
        marks["tables"] = [*tables[1], *tables[2]]

    firsts, mixeds, seconds, hiddens = [], [], [], []
    records = []
    xs = [tok]
    first_in, query, kv = first_call(near, coords, tok, gain1, *tables[0], (weight_qkv,))
    heights = []
    for step in range(3):
        if near and step == 0:
            waits = ([*marks["places"], pair_mine], [*marks["tables"], out_mine])
            part_a, part_b = gather_keys(kv, order, near, waits)
            *marks["places"], pair_mine = waits[0]
            *marks["tables"], out_mine = waits[1]
        else:
            part_a, part_b = gather_keys(kv, order, near)
        if near and step == 1:
            query_places[1:], key_places[1:], key_live[1:] = (marks["places"][i : i + 2] for i in (0, 2, 4))
        firsts.append(first_in)
        next_rows = (cap_mid, cap_last, tok_local)[step]
        attention = (query, part_a, part_b, key_places[step], key_live[step], query_places[step], prompt)
        if near and step == 0:
            pair, down_mine = Share(pair_mine), Hop(cut_down, Y_BIT)
            weights, mixed = wave(
                order, [(down_mine, 0), (pair, 0)], lambda *a: attend_call(*a, prompt), attention[:-1]
            )
            dense_weights = fetch_rest(pair.result, out_mine, down_mine.result)
            sel_own, live2_own, live3_own = marks["places"][6:]
            tables[1:] = [marks["tables"][:2], marks["tables"][2:]]
        elif step == 0:
            weights, mixed = attend_call(*attention)
            dense_weights = fetch_rest()
        if step == 0:
            extra = (sel_own, *tables[1])
        elif step == 1:
            extra = (live2_own, *tables[2])
        else:
            extra = (sel_own, live2_own, live3_own, heights[0], heights[1])
        mats = dense_weights + ((weight_qkv,) if step < 2 else ())

        def dense(mixed, step=step, extra=extra, mats=mats, next_rows=next_rows):
            return dense_call(
                near, step, coords, xs[step], mixed, gain1, gain2, extra, mats, next_rows
            )

        def both(*a):
            made = attend_call(*a, prompt)
            return *made, *dense(made[1])

        if step == 0:
            result = dense(mixed)
        elif step == 1 and near:
            there = Move(cotangent[0].T)
            weights, mixed, *result = wave(order, [(there, 0)], both, attention[:-1])
            cot = there.result
        else:
            weights, mixed, *result = both(*attention[:-1])
            if step == 1:
                cot = cotangent[0].T
        mixed_rows, middle, second, gate, up, hidden = result[:6]
        mixeds.append(mixed_rows)
        seconds.append(second)
        hiddens.append(hidden)
        records.append((query, part_a, part_b, weights, middle, gate, up))
        if step < 2:
            height, following, first_in, query, kv = result[6:]
            heights.append(height)
            xs.append(following)
        else:
            output = relocate(order.take(result[6]))

    d_firsts, d_seconds = [None] * 3, [None] * 3
    sums_one, sums_two = [], []
    slots = None
    parts, d_query, d_middle = (), None, None
    column = lambda rows, i: [r[i] for r in rows]

    def grads(kind, groups):
        return grad_call(kind, block_coords, groups)

    for phase in range(4):
        step = 2 - phase
        before, into = (), ()
        if phase > 0:
            before = (gain1, *tables[step + 1], xs[step + 1], d_middle, d_query)
        if phase < 3:
            into = (gain2, *records[step][4:7])
        mats = (dense_weights[3], dense_weights[1], dense_weights[2], dense_weights[0])
        if phase == 0:
            extra, mats = (cot, sel_own, live3_own), mats
        elif phase == 1:
            extra, mats = (slots, live3_own, live2_own), (weight_qkv,) + mats
        elif phase == 2:
            extra, mats = (cot, sel_own, live2_own), (weight_qkv,) + mats
        else:
            extra, mats = (), (weight_qkv,)
        last = lambda *parts: back_call(near, phase, coords, before, parts, into, extra, mats, cap_mid)
        if near and phase == 3:
            break
        result = list(last(*parts))
        if phase > 0:
            d_firsts[step + 1], total = result[:2]
            sums_one.append(total)
            result = result[2:]
        if phase == 3:
            grad_tokens = result[0]
            break
        d_low, d_gate, d_up, d_middle, d_mid_low, d_mixed, total = result[:7]
        d_seconds[step] = (d_low, d_gate, d_up, d_mid_low)
        sums_two.append(total)
        if phase == 0:
            slots = result[7]
        query, part_a, part_b, weights = records[step][:4]
        if phase < 2:
            d_mixed = order.take(d_mixed)
            d_query, term_a, term_b = attend_back_call(query, d_mixed, part_a, part_b, weights)
            if phase == 0:
                output, term_b = order.take(output, term_b)
            parts = scatter_keys(term_a, term_b, order, near)

        else:
            attend_last = lambda d: attend_back_call(query, d, part_a, part_b, weights)
            gate_grads = lambda *d: grads("cols", [seconds, list(d)])
            down_grads = grads("rows", [hiddens, column(d_seconds, 0)])
            if not near:
                d_query, term_a, term_b = attend_last(d_mixed)
                parts = scatter_keys(term_a, term_b, order, near)
                sums_of = [
                    pair_sum(*g, near)
                    for g in (down_grads, gate_grads(*column(d_seconds, 1)), gate_grads(*column(d_seconds, 2)))
                ]
                continue
            down = Hop(down_grads[1], C_BIT)
            gate_grads_made = wave(
                order, [(down, 0)], gate_grads, column(d_seconds, 1)
            )
            down = BothWays(low_sum(down_grads[0], down.result))
            gate = Hop(gate_grads_made[1], C_BIT)
            d_query, term_a, term_b = wave(order, [(down, 0), (gate, 0)], attend_last, (d_mixed,))
            gate = BlockSums(low_sum(gate_grads_made[0], gate.result))
            far = Hop(term_b, C_BIT)
            up_made = wave(order, [(down, 1), (far, 0)], gate_grads, column(d_seconds, 2))
            own, *others = split_call(term_a, far.result)
            keys, up = KeySums(own, others), Hop(up_made[1], C_BIT)
            wave(order, [(keys, 0), (up, 0)])
            wave(order, [(keys, 1)])
            up = BlockSums(low_sum(up_made[0], up.result))
            parts = keys.result

    kv_width = key_weight.shape[1]
    hidden_width = w_gate.shape[1]

    def mixed_grads(*d):
        sums = jnp.concatenate([sum(sums_one), sum(sums_two)], axis=0)
        return grad_call("mixed", block_coords, [firsts, mixeds, list(d), column(d_seconds, 3)], sums)

    def last_grads(*parts):
        d_firsts[0], total, grad_tokens = last(*parts)
        sums_one.append(total)
        return *mixed_grads(*d_firsts), grad_tokens

    placed = {}

    if near:
        def place(kind, widths):
            return lambda near_blocks, far_blocks, at: place_call(kind, at, near_blocks, far_blocks, widths)

        placing = lambda chain: (*chain.result, coords)
        *rest_made, grad_tokens = wave(order, [(gate, 0), (down, 2)], last_grads, parts)
        rest = Hop(rest_made[1], C_BIT)
        wave(order, [(gate, 1), (down, 3), (rest, 0)])
        rest = BlockSums(low_sum(rest_made[0], rest.result))
        wave(order, [(up, 0), (gate, 2), (down, 4)])
        wave(order, [(up, 1), (gate, 3)])
        wave(order, [(rest, 0), (up, 2), (gate, 4)])
        wave(order, [(rest, 1), (up, 3)])
        wave(order, [(rest, 2), (up, 4), (down, 5)])
        placed["down"] = wave(
            order, [(rest, 3), (up, 5), (gate, 5)], place("rows", None), placing(down)
        )
        tokens_back = Move(grad_tokens)

        def place_two(*arrays):
            cols = place("cols", (hidden_width,))
            return *cols(*arrays[:3]), *cols(*arrays[3:])

        placed["gate"], placed["up"] = wave(
            order, [(rest, 4), (tokens_back, 0)], place_two, (*placing(gate), *placing(up))
        )
        grad_tokens = tokens_back.result.astype(F32)
        wave(order, [(rest, 5)])
        placed["rest"] = order.all(
            *place("cols", (width, kv_width, width, kv_width))(*rest.result, order.token)
        )
        (placed["down"],) = placed["down"]
    else:
        sums_of.append(pair_sum(*mixed_grads(*d_firsts), near))
        for name, kind, widths, total in zip(
            ("down", "gate", "up", "rest"),
            ("rows", "cols", "cols", "cols"),
            (None, (hidden_width,), (hidden_width,), (width, kv_width, width, kv_width)),
            sums_of,
            strict=True,
        ):
            mine = lax.dynamic_index_in_dim(total, y, 1, keepdims=False)
            placed[name] = place_call(kind, block_coords, mine[0], mine[1], widths)
        for name in ("down", "gate", "up"):
            (placed[name],) = placed[name]
        grad_tokens = grad_tokens.astype(F32)
    grad_down, grad_gate, grad_up = placed["down"].T, placed["gate"], placed["up"]
    grad_query, grad_key, grad_out, grad_value, gain_sums = placed["rest"]
    grad_key, grad_value = grad_key.T, grad_value.T
    return (
        output.T[None],
        grad_tokens.T[None],
        grad_query,
        grad_key,
        grad_value,
        grad_out,
        grad_gate,
        grad_up,
        grad_down,
        gain_sums[0],
        gain_sums[1],
    )


def solution(mesh):
    rows = P("ws", "ctx", None)
    flat = P("ws", None)
    in_specs = (rows, rows) + (flat,) * 7 + (P("ws"), P("ws"), P()) + (flat,) * 4
    out_specs = (rows, rows) + (flat,) * 7 + (P("ws"), P("ws"))
    return jax.shard_map(
        on_device, mesh=mesh, in_specs=in_specs, out_specs=out_specs, check_vma=False
    )
```

```python
import functools

import jax
import jax.numpy as jnp
from jax import lax
from jax.experimental import pallas as pl
from jax.experimental.pallas import tpu as pltpu
from jax.sharding import PartitionSpec as P

QUERY_HEADS = 15
KEY_VALUE_HEADS = 5
HEAD_SIZE = 64
SHARE = QUERY_HEADS // KEY_VALUE_HEADS
BLK = 64
CONT_BITS = 10
EPSILON = 1e-05
ROPE_BASE = 10000.0
MASK_FLOOR = -1e30
SCALE = HEAD_SIZE ** (-0.5)

BF = jnp.bfloat16
F32 = jnp.float32
AXES = ("ctx", "ws")
FF_CHUNKS = 4
MIB = 1024 * 1024

Y_BIT, C_BIT, X_BIT, Z1_BIT, Z2_BIT = 1, 2, 4, 8, 16
NEAR = (0, X_BIT, Y_BIT, Z1_BIT, X_BIT | Y_BIT | Z1_BIT, X_BIT | Y_BIT, Y_BIT | Z1_BIT, Z1_BIT | X_BIT)


def hop(value, mask):
    return lax.ppermute(value, AXES, [(i, i ^ mask) for i in range(32)])


def swap_place(i):
    y, z2 = i & 1, (i >> 4) & 1
    return (i & ~(Y_BIT | Z2_BIT)) | (Z2_BIT if y else 0) | (Y_BIT if z2 else 0)


def move(value):
    return lax.ppermute(value, AXES, [(i, swap_place(i)) for i in range(32)])


def ctx_mask(mask):
    return (
        (1 if mask & C_BIT else 0)
        | (2 if mask & X_BIT else 0)
        | (4 if mask & Z1_BIT else 0)
        | (8 if mask & Y_BIT else 0)
    )


NT = (((1,), (1,)), ((), ()))
TN = (((0,), (0,)), ((), ()))
NN = (((1,), (0,)), ((), ()))


def mm(left, right, dims=NN, precision=None):
    return lax.dot_general(left, right, dims, precision=precision, preferred_element_type=F32)


def normed_rows(values):
    inverse = lax.rsqrt(jnp.mean(values * values, axis=-1, keepdims=True) + EPSILON)
    return values * inverse, inverse


def norm_back(grad_in, normed, inverse, gain):
    scaled = grad_in * gain
    return inverse * (scaled - normed * jnp.mean(scaled * normed, axis=-1, keepdims=True))


def turn(values, cosine, sine, back=False):
    rows, width = values.shape
    lane = lax.broadcasted_iota(jnp.int32, (rows, 128), 1)
    first = (lane & (HEAD_SIZE - 1)) < HEAD_SIZE // 2
    if back:
        sine = -sine
    pieces = []
    for start in range(0, width, 128):
        wide = min(128, width - start)
        part = values[:, start : start + wide]
        if wide < 128:
            part = jnp.concatenate([part, jnp.zeros((rows, 128 - wide), F32)], axis=1)
        other = jnp.where(first, pltpu.roll(part, 96, 1), pltpu.roll(part, 32, 1))
        pieces.append((part * cosine + other * sine)[:, :wide])
    return jnp.concatenate(pieces, axis=1)


def vm():
    return pl.BlockSpec(memory_space=pltpu.VMEM)


def sm():
    return pl.BlockSpec(memory_space=pltpu.SMEM)


def hbm():
    return pl.BlockSpec(memory_space=pltpu.HBM)


def shaped(shape, dtype):
    return jax.ShapeDtypeStruct(shape, dtype)


def stored(shape, dtype):
    return pltpu.HBM(shape, dtype)


def apart(arrays):
    return [pltpu.with_memory_space_constraint(a, pltpu.HBM) for a in arrays]


def params(mib, **kw):
    return pltpu.CompilerParams(vmem_limit_bytes=mib * MIB, **kw)


def estimate(micros=1.0):
    return pl.CostEstimate(flops=0, bytes_accessed=int(micros * 3.7e6 / 4), transcendentals=0)


class Order:
    def __init__(self, token):
        self.token = token

    def all(self, *values):
        *values, self.token = lax.optimization_barrier(values + (self.token,))
        return values

    def take(self, *values):
        *values, self.token = lax.optimization_barrier(tuple(values) + (self.token,))
        return values[0] if len(values) == 1 else values


def read_coords(ref):
    return [ref[i] for i in range(4)]


class Weight:
    def __init__(self, shape, arrays, groups):
        self.shape, self.arrays, self.groups = shape, arrays, groups


def at_place(ref, place, rows, cols, coords):
    row, col = place(*coords)
    if rows != ref.shape[0] and not isinstance(row, int):
        row = pl.multiple_of(row, 16)
    if cols != ref.shape[1] and not isinstance(col, int):
        col = pl.multiple_of(col, 128)
    if cols == ref.shape[1]:
        return ref if rows == ref.shape[0] else ref.at[pl.ds(row, rows), :]
    return ref.at[pl.ds(row, rows), pl.ds(col, cols)]


def bring(weights, refs, buffers, sems, coords, turns, ahead=3):
    firsts, at = [], 0
    for weight in weights:
        firsts.append(at)
        at += len(weight.arrays)
    copies, count = {}, 0
    for which, group in turns:
        copies[which, group] = []
        for array, rows, cols, source, target in weights[which].groups[group]:
            copies[which, group].append(
                pltpu.make_async_copy(
                    at_place(refs[firsts[which] + array], source, rows, cols, coords),
                    at_place(buffers[which], target, rows, cols, coords),
                    sems.at[count],
                )
            )
            count += 1
    queue = list(turns)

    def start():
        if queue:
            for copy in copies[queue.pop(0)]:
                copy.start()

    for _ in range(ahead):
        start()

    def wait(which, group=0):
        for copy in copies[which, group]:
            copy.wait()
        start()

    return wait


def arrays_of(weights):
    return [a for w in weights for a in w.arrays]


def weights_in(near, weights):
    arrays = arrays_of(weights)
    if near:
        return [vm()] * len(arrays), arrays, []
    return [hbm()] * len(arrays), apart(arrays), scratch_of(weights)


def weights_here(near, weights, refs, scratch, coords_ref, turns):
    if near:
        return refs, lambda *which: None
    buffers, sems = scratch[: len(weights)], scratch[len(weights)]
    return buffers, bring(weights, refs, buffers, sems, read_coords(coords_ref), turns)


def join_kernel(weights, n_bases, coords_ref, *args):
    count = len(arrays_of(weights))
    args = args[n_bases:]
    refs, outs, sems = args[:count], args[count:-1], args[-1]
    turns = [(i, g) for i, w in enumerate(weights) for g in range(len(w.groups))]
    wait = bring(weights, refs, outs, sems, read_coords(coords_ref), turns, len(turns))
    for turn in turns:
        wait(*turn)


def join_call(coords, weights, bases=()):
    arrays, place = arrays_of(weights), pl.BlockSpec(memory_space=pl.ANY)
    if not bases:
        arrays, place = apart(arrays), hbm()
    return pl.pallas_call(
        functools.partial(join_kernel, weights, len(bases)),
        name="join_weights",
        out_shape=tuple(pltpu.VMEM(w.shape, BF) for w in weights),
        in_specs=[sm()] + [vm()] * len(bases) + [place] * len(arrays),
        out_specs=tuple(vm() for _ in weights),
        scratch_shapes=scratch_of(weights)[-1:],
        input_output_aliases={1 + i: i for i in range(len(bases))},
        compiler_params=params(24),
        cost_estimate=estimate(),
    )(coords, *bases, *arrays)


def part_of_weight(weight, own):
    shift = 0 if own else 1
    groups = [
        [(copy[0] - shift, *copy[1:]) for copy in group if (copy[0] == 0) == own]
        for group in weight.groups
    ]
    return Weight(weight.shape, weight.arrays[:1] if own else weight.arrays[1:], groups)


def scratch_of(weights):
    copies = sum(len(g) for w in weights for g in w.groups)
    return [pltpu.VMEM(w.shape, BF) for w in weights] + [pltpu.SemaphoreType.DMA((copies,))]


def one_piece(array):
    rows, cols = array.shape
    origin = lambda *k: (0, 0)
    return Weight(array.shape, [array], [[(0, rows, cols, origin, origin)]])


def in_columns(array):
    rows, cols = array.shape
    wide = cols // FF_CHUNKS
    place = lambda j: (lambda *k: (0, j * wide))
    return Weight(
        array.shape, [array], [[(0, rows, wide, place(j), place(j))] for j in range(FF_CHUNKS)]
    )


def part_of(j, coords):
    rx, rz = BESIDE[j]
    return (coords[2] ^ rx) * 2 + ((coords[3] & 1) ^ rz)


BESIDE = ((0, 0), (1, 0), (0, 1), (1, 1))


def pack_kernel(coords_ref, q_hbm, k_hbm, v_hbm, own_ref, piece_ref, q_ref, k_ref, v_ref, sems):
    copies = [
        pltpu.make_async_copy(a, b, sems.at[i])
        for i, (a, b) in enumerate(((q_hbm, q_ref), (k_hbm, k_ref), (v_hbm, v_ref)))
    ]
    for copy in copies:
        copy.start()
    half, width = q_ref.shape
    kv_width = k_ref.shape[0]
    end = width + 2 * kv_width
    own_ref[:, end:] = jnp.zeros((half, own_ref.shape[1] - end), BF)
    for copy in copies:
        copy.wait()
    own_ref[:, :width] = q_ref[...]
    own_ref[:, width : width + kv_width] = k_ref[...].T
    own_ref[:, width + kv_width : end] = v_ref[...].T
    depth = half // 2
    start = pl.multiple_of(coords_ref[1] * depth, 16)
    piece_ref[...] = own_ref[pl.ds(start, depth), :]


def pack_call(coords, w_query, key_t, value_t):
    half, width = w_query.shape
    total = -(-(width + 2 * key_t.shape[0]) // 128) * 128
    return pl.pallas_call(
        pack_kernel,
        name="pack",
        out_shape=(stored((half, total), BF), shaped((half // 2, total), BF)),
        in_specs=[sm()] + [hbm()] * 3,
        out_specs=(vm(), vm()),
        scratch_shapes=[pltpu.VMEM(a.shape, BF) for a in (w_query, key_t, value_t)]
        + [pltpu.SemaphoreType.DMA((3,))],
        compiler_params=params(12),
        cost_estimate=estimate(),
    )(coords, *apart([w_query, key_t, value_t]))


def pack_rows_kernel(tokens_ref, plan_ref, out_ref):
    width, rows = tokens_ref.shape
    out_ref[:rows, :] = tokens_ref[...].T
    marks = plan_ref[...].astype(F32).astype(BF)
    out_ref[rows:, : marks.shape[1]] = marks
    out_ref[rows:, marks.shape[1] :] = jnp.zeros((marks.shape[0], width - marks.shape[1]), BF)


def pack_rows_call(tokens_t, plan):
    width, rows = tokens_t.shape
    return pl.pallas_call(
        pack_rows_kernel,
        name="pack_rows",
        out_shape=shaped((rows + plan.shape[0], width), BF),
        in_specs=[vm()] * 2,
        out_specs=vm(),
        compiler_params=params(8),
        cost_estimate=estimate(),
    )(*apart([tokens_t, plan]))


def stack_kernel(*refs):
    out_ref = refs[-1]
    at = 0
    for ref in refs[:-1]:
        out_ref[at : at + ref.shape[0], :] = ref[...]
        at += ref.shape[0]


def stack_call(pieces):
    rows = sum(p.shape[0] for p in pieces)
    return pl.pallas_call(
        stack_kernel,
        name="stack",
        out_shape=shaped((rows, pieces[0].shape[1]), pieces[0].dtype),
        in_specs=[vm()] * len(pieces),
        out_specs=vm(),
        compiler_params=params(8),
        cost_estimate=estimate(),
    )(*pieces)


def split_kernel(total_ref, other_ref, *outs):
    rows = outs[0].shape[0]
    for i, out in enumerate(outs):
        at = slice(i * rows, (i + 1) * rows)
        out[...] = (total_ref[at, :] + other_ref[at, :].astype(F32)).astype(out.dtype)


def split_call(total, other):
    rows, width = total.shape[0] // len(NEAR), total.shape[1]
    outs = [shaped((rows, width), F32)] + [shaped((rows, width), BF)] * (len(NEAR) - 1)
    return pl.pallas_call(
        split_kernel,
        name="split",
        out_shape=tuple(outs),
        in_specs=[vm(), vm()],
        out_specs=tuple(vm() for _ in outs),
        compiler_params=params(10),
        cost_estimate=estimate(),
    )(total, other)


def project(x, gain, wqkv_ref, cosine, sine, first_ref, q_ref, kv_ref):
    normed, _ = normed_rows(x)
    first_in = (normed * gain).astype(BF)
    first_ref[...] = first_in
    rows = mm(first_in, wqkv_ref[...])
    wide = SHARE * HEAD_SIZE
    q_width = KEY_VALUE_HEADS * wide
    kv_width = KEY_VALUE_HEADS * HEAD_SIZE
    key = turn(rows[:, q_width : q_width + kv_width], cosine, sine)
    value = rows[:, q_width + kv_width : q_width + 2 * kv_width]
    for h in range(KEY_VALUE_HEADS):
        at = slice(h * HEAD_SIZE, (h + 1) * HEAD_SIZE)
        kv_ref[:, h * 128 : (h + 1) * 128] = jnp.concatenate(
            [key[:, at], value[:, at]], axis=1
        ).astype(BF)
    query = (turn(rows[:, :q_width], cosine, sine).astype(BF) * SCALE).astype(BF)
    for h in range(KEY_VALUE_HEADS):
        q_ref[h] = query[:, h * wide : (h + 1) * wide]


def first_kernel(near, weights, coords_ref, x_ref, gain_ref, cos_ref, sin_ref, *rest):
    count = len(arrays_of(weights))
    refs, (first_ref, q_ref, kv_ref, *scratch) = rest[:count], rest[count:]
    (wqkv,), wait = weights_here(near, weights, refs, scratch, coords_ref, ((0, 0),))
    wait(0)
    project(
        x_ref[...].astype(F32), gain_ref[...], wqkv, cos_ref[...], sin_ref[...],
        first_ref, q_ref, kv_ref,
    )


def first_call(near, coords, tokens, gain, cosine, sine, weights):
    rows, width = tokens.shape
    specs, arrays, scratch = weights_in(near, weights)
    return pl.pallas_call(
        functools.partial(first_kernel, near, weights),
        name="first_projection",
        out_shape=(
            stored((rows, width), BF),
            shaped((KEY_VALUE_HEADS, rows, SHARE * HEAD_SIZE), BF),
            shaped((rows, KEY_VALUE_HEADS * 128), BF),
        ),
        in_specs=[sm()] + [vm()] * 4 + specs,
        out_specs=(vm(), vm(), vm()),
        scratch_shapes=scratch,
        compiler_params=params(10),
        cost_estimate=estimate(),
    )(coords, tokens, gain, cosine, sine, *arrays)


def padded_heads(wide_rows, left):
    rows = wide_rows.shape[0]
    blank = jnp.zeros((rows, HEAD_SIZE), wide_rows.dtype)
    stacked = []
    for j in range(SHARE):
        part = wide_rows[:, j * HEAD_SIZE : (j + 1) * HEAD_SIZE]
        stacked.append(jnp.concatenate([part, blank] if left else [blank, part], axis=1))
    return jnp.concatenate(stacked, axis=0)


def fill_bias(prompt, kpos_ref, live_ref, qpos_ref, bias_scr, col_scr):
    kpos = kpos_ref[...]
    klive = live_ref[...] > 0
    rows = bias_scr.shape[0]
    square = lambda axis: lax.broadcasted_iota(jnp.int32, (rows, rows), axis)
    own = jnp.where(square(0) == square(1), qpos_ref[...].astype(F32), 0.0)
    col_scr[...] = jnp.sum(own, axis=1, keepdims=True).astype(jnp.int32)
    kseg = jnp.where(kpos < prompt, 0, 1 + ((kpos - prompt) >> CONT_BITS))

    def fill(i, carry):
        at = pl.ds(pl.multiple_of(i * 8, 8), 8)
        qpos = col_scr[at, :]
        qseg = jnp.where(qpos < prompt, 0, 1 + ((qpos - prompt) >> CONT_BITS))
        earlier = kpos <= qpos
        shared = (kseg == 0) | (kseg == qseg)
        seen = earlier & shared & (klive | (kpos == qpos))
        bias_scr[at, :] = jnp.where(seen, 0.0, MASK_FLOOR)
        return carry

    lax.fori_loop(0, bias_scr.shape[0] // 8, fill, 0)


def attend_kernel(prompt, q_ref, a_ref, b_ref, kpos_ref, live_ref, qpos_ref, p_ref, o_ref, bias_scr, col_scr):
    @pl.when(pl.program_id(0) == 0)
    def _():
        fill_bias(prompt, kpos_ref, live_ref, qpos_ref, bias_scr, col_scr)

    o_ref[0] = attend_heads(q_ref, a_ref, b_ref, p_ref, bias_scr)


def attend_heads(q_ref, a_ref, b_ref, p_ref, bias_scr):
    rows = q_ref.shape[1]
    half = a_ref.shape[0]
    together = rows < 128
    if together:
        stacked = padded_heads(q_ref[0], True)
        all_a, all_b = mm(stacked, a_ref[...], NT), mm(stacked, b_ref[...], NT)
    blank = jnp.zeros((rows, HEAD_SIZE), BF)
    outs = []
    for j in range(SHARE):
        at = slice(j * rows, (j + 1) * rows)
        if together:
            s_a, s_b = all_a[at], all_b[at]
        else:
            part = jnp.concatenate([q_ref[0, :, j * HEAD_SIZE : (j + 1) * HEAD_SIZE], blank], axis=1)
            s_a, s_b = mm(part, a_ref[...], NT), mm(part, b_ref[...], NT)
        s_a = s_a + bias_scr[:, :half]
        s_b = s_b + bias_scr[:, half:]
        top = jnp.maximum(
            jnp.max(s_a, axis=-1, keepdims=True), jnp.max(s_b, axis=-1, keepdims=True)
        )
        w_a, w_b = jnp.exp(s_a - top), jnp.exp(s_b - top)
        mass = jnp.sum(w_a, axis=-1, keepdims=True) + jnp.sum(w_b, axis=-1, keepdims=True)
        inverse = 1.0 / mass
        p_a, p_b = (w_a * inverse).astype(BF), (w_b * inverse).astype(BF)
        p_ref[0, at, :half] = p_a
        p_ref[0, at, half:] = p_b
        if not together:
            outs.append((mm(p_a, a_ref[...]) + mm(p_b, b_ref[...]))[:, HEAD_SIZE:])
    if together:
        mixed = mm(p_ref[0, :, :half], a_ref[...]) + mm(p_ref[0, :, half:], b_ref[...])
        outs = [mixed[j * rows : (j + 1) * rows, HEAD_SIZE:] for j in range(SHARE)]
    return jnp.concatenate(outs, axis=1).astype(BF)


def attend_call(query, part_a, part_b, kpos, klive, qpos, prompt):
    heads, rows, wide = query.shape
    half = part_a.shape[0]
    keys = 2 * half
    return pl.pallas_call(
        functools.partial(attend_kernel, prompt),
        name="attend",
        grid=(heads,),
        out_shape=(stored((heads, SHARE * rows, keys), BF), shaped((heads, rows, wide), BF)),
        in_specs=[
            pl.BlockSpec((1, rows, wide), lambda h: (h, 0, 0)),
            pl.BlockSpec((half, 128), lambda h: (0, h)),
            pl.BlockSpec((half, 128), lambda h: (0, h)),
            pl.BlockSpec((1, keys), lambda h: (0, 0)),
            pl.BlockSpec((1, keys), lambda h: (0, 0)),
            pl.BlockSpec((1, rows), lambda h: (0, 0)),
        ],
        out_specs=(
            pl.BlockSpec((1, SHARE * rows, keys), lambda h: (h, 0, 0)),
            pl.BlockSpec((1, rows, wide), lambda h: (h, 0, 0)),
        ),
        scratch_shapes=[pltpu.VMEM((rows, keys), F32), pltpu.VMEM((rows, 1), jnp.int32)],
        compiler_params=params(12 if keys <= 2048 else 56, dimension_semantics=("arbitrary",)),
        cost_estimate=estimate(rows * keys / 17000),
    )(query, part_a, part_b, kpos, klive, qpos)


def attend_back_kernel(q_ref, do_ref, a_ref, b_ref, p_ref, dq_ref, da_ref, db_ref, dp_scr, ds_scr):
    rows = q_ref.shape[1]
    half = a_ref.shape[0]
    stacked = padded_heads(q_ref[0], True)
    grads = padded_heads(do_ref[0], False)
    dp_scr[:, :half] = mm(grads, a_ref[...], NT)
    dp_scr[:, half:] = mm(grads, b_ref[...], NT)

    for j in range(SHARE):
        at = slice(j * rows, (j + 1) * rows)
        weights = p_ref[0, at, :].astype(F32)
        dp = dp_scr[at, :]
        delta = jnp.sum(weights * dp, axis=-1, keepdims=True)
        ds_scr[at, :] = (weights * (dp - delta)).astype(BF)
    dq = (mm(ds_scr[:, :half], a_ref[...]) + mm(ds_scr[:, half:], b_ref[...])) * SCALE
    dq_ref[0] = jnp.concatenate(
        [dq[j * rows : (j + 1) * rows, :HEAD_SIZE] for j in range(SHARE)], axis=1
    )
    for at, out in ((slice(0, half), da_ref), (slice(half, 2 * half), db_ref)):
        turned = mm(stacked, ds_scr[:, at], TN) + mm(grads, p_ref[0, :, at], TN)
        out[...] = turned.T.astype(out.dtype)


def attend_back_call(query, d_out, part_a, part_b, weights):
    heads, rows, wide = query.shape
    half = part_a.shape[0]
    keys = 2 * half
    return pl.pallas_call(
        attend_back_kernel,
        name="attend_back",
        grid=(heads,),
        out_shape=(
            shaped((heads, rows, wide), F32),
            shaped((half, heads * 128), F32),
            shaped((half, heads * 128), BF),
        ),
        in_specs=[
            pl.BlockSpec((1, rows, wide), lambda h: (h, 0, 0)),
            pl.BlockSpec((1, rows, wide), lambda h: (h, 0, 0)),
            pl.BlockSpec((half, 128), lambda h: (0, h)),
            pl.BlockSpec((half, 128), lambda h: (0, h)),
            pl.BlockSpec((1, SHARE * rows, keys), lambda h: (h, 0, 0)),
        ],
        out_specs=(
            pl.BlockSpec((1, rows, wide), lambda h: (h, 0, 0)),
            pl.BlockSpec((half, 128), lambda h: (0, h)),
            pl.BlockSpec((half, 128), lambda h: (0, h)),
        ),
        scratch_shapes=[
            pltpu.VMEM((SHARE * rows, keys), F32),
            pltpu.VMEM((SHARE * rows, keys), BF),
        ],
        compiler_params=params(14 if keys <= 2048 else 60, dimension_semantics=("arbitrary",)),
        cost_estimate=estimate(rows * keys / 22000),
    )(query, d_out, part_a, part_b, *apart([weights]))


def picks(sel_ref, total_rows):
    capacity = sel_ref.shape[1]
    row = lax.broadcasted_iota(jnp.int32, (total_rows, capacity), 0)
    return row == sel_ref[...]


def live_column(live_ref, rows):
    count = jnp.sum(live_ref[:, :].astype(F32), axis=1, keepdims=True)
    return lax.broadcasted_iota(jnp.int32, (rows, 1), 0).astype(F32) < count


def feed_forward(wait, x, mixed, gain_two, wo, wg, wu, wd, ao_out, mid_ref, second_ref, g_ref, u_ref, hid_ref):
    ao_out[...] = mixed
    wait(0)
    middle = x + mm(mixed, wo[...])
    mid_ref[...] = middle
    normed, _ = normed_rows(middle)
    second = (normed * gain_two).astype(BF)
    second_ref[...] = second
    wide = wg.shape[1] // FF_CHUNKS
    for j in range(FF_CHUNKS):
        at = slice(j * wide, (j + 1) * wide)
        wait(1, j)
        g = mm(second, wg[:, at])
        wait(2, j)
        u = mm(second, wu[:, at])
        g_ref[:, at] = g.astype(BF)
        u_ref[:, at] = u.astype(BF)
        hid_ref[:, at] = (g / (1.0 + jnp.exp(-g)) * u).astype(BF)
    wait(3)
    return middle + mm(hid_ref[...], wd[...], NT)


DENSE_TURNS = ((0, 0),) + tuple((w, j) for j in range(FF_CHUNKS) for w in (1, 2)) + ((3, 0),)


def dense_body(near, step, weights, mixed, args):
    args = list(args)
    take = lambda k: [args.pop(0) for _ in range(k)]
    coords_ref, x_ref, gain1_ref, gain2_ref = take(4)
    if step == 0:
        sel_ref, cos_ref, sin_ref = take(3)
    elif step == 1:
        live_ref, cos_ref, sin_ref = take(3)
    else:
        sel_ref, live2_ref, live_ref, h1_ref, h2_ref = take(5)
    refs = take(len(arrays_of(weights)))
    ao_out, mid_ref, second_ref, g_ref, u_ref, hid_ref = take(6)
    if step < 2:
        h_ref, next_ref, first_ref, q_ref, kv_ref = take(5)
    else:
        (out_ref,) = take(1)
    turns = DENSE_TURNS + (((4, 0),) if step < 2 else ())

    def work():
        buffers, wait = weights_here(near, weights, refs, args, coords_ref, turns)
        rows = x_ref.shape[0]
        x = x_ref[...].astype(F32)
        updated = feed_forward(
            wait, x, mixed(), gain2_ref[...], *buffers[:4], ao_out, mid_ref,
            second_ref, g_ref, u_ref, hid_ref,
        )
        if step == 0:
            h_ref[...] = updated
            chosen = picks(sel_ref, rows).astype(F32)
            following = mm(chosen, updated, TN, lax.Precision.HIGHEST)
        else:
            updated = jnp.where(live_column(live_ref, rows), updated, x)
        if step == 1:
            h_ref[...] = updated
            following = updated[: next_ref.shape[0]]
        if step < 2:
            next_ref[...] = following
            wait(4)
            project(
                following, gain1_ref[...], buffers[4], cos_ref[...], sin_ref[...],
                first_ref, q_ref, kv_ref,
            )
        else:
            slots = jnp.concatenate([updated, h2_ref[rows:, :]], axis=0).astype(BF)
            hit = picks(sel_ref, h1_ref.shape[0]) & (live2_ref[...] > 0)
            placed = mm(hit.astype(BF), slots)
            any_hit = jnp.sum(hit.astype(F32), axis=1, keepdims=True) > 0.5
            out_ref[...] = jnp.where(any_hit, placed, h1_ref[...]).T.astype(BF)

    return work


def joined_heads(ao_ref):
    return jnp.concatenate([ao_ref[h] for h in range(KEY_VALUE_HEADS)], axis=1)


def dense_kernel(near, step, weights, ao_ref, *args):
    dense_body(near, step, weights, lambda: joined_heads(ao_ref), args)()


def dense_outs(step, x, weights, next_rows):
    rows, width = x.shape
    hidden = weights[1].shape[1]
    outs = [
        stored((rows, width), BF),
        stored((rows, width), F32),
        stored((rows, width), BF),
        stored((rows, hidden), BF),
        stored((rows, hidden), BF),
        stored((rows, hidden), BF),
    ]
    if step < 2:
        outs += [
            stored((rows, width), F32),
            shaped((next_rows, width), F32),
            stored((next_rows, width), BF),
            shaped((KEY_VALUE_HEADS, next_rows, SHARE * HEAD_SIZE), BF),
            shaped((next_rows, KEY_VALUE_HEADS * 128), BF),
        ]
    else:
        outs += [stored((width, next_rows), BF)]
    return outs


def dense_call(near, step, coords, x, mixed, gain1, gain2, extra, weights, next_rows):
    specs, arrays, scratch = weights_in(near, weights)
    outs = dense_outs(step, x, weights, next_rows)
    return pl.pallas_call(
        functools.partial(dense_kernel, near, step, weights),
        name=f"dense_{step}",
        out_shape=tuple(outs),
        in_specs=[vm(), sm()] + [vm()] * (3 + len(extra)) + specs,
        out_specs=tuple(vm() for _ in outs),
        scratch_shapes=scratch,
        compiler_params=params(12 if near else 50),
        cost_estimate=estimate(6),
    )(mixed, coords, x, gain1, gain2, *extra, *arrays)


def feed_back(wait, first, d_y, mid_ref, g_ref, u_ref, gain_two, wd, wg, wu, wo, dyb_ref, dg_ref, du_ref, dmid_ref, dz_ref, dao_ref, sum_ref):
    d_low = d_y.astype(BF)
    dyb_ref[...] = d_low
    wide = wg.shape[1] // FF_CHUNKS
    d_second = jnp.zeros(d_y.shape, F32)
    wait(first)
    for j in range(FF_CHUNKS):
        at = slice(j * wide, (j + 1) * wide)
        d_hidden = mm(d_low, wd[:, at])
        g, u = g_ref[:, at].astype(F32), u_ref[:, at].astype(F32)
        sigma = 1.0 / (1.0 + jnp.exp(-g))
        d_gate = (d_hidden * u * sigma * (1.0 + g * (1.0 - sigma))).astype(BF)
        d_up = (d_hidden * (g * sigma)).astype(BF)
        dg_ref[:, at] = d_gate
        du_ref[:, at] = d_up
        wait(first + 1, j)
        wait(first + 2, j)
        d_second += mm(d_gate, wg[:, at], NT) + mm(d_up, wu[:, at], NT)
    normed, inverse = normed_rows(mid_ref[...])
    sum_ref[...] = jnp.sum(d_second * normed, axis=0, keepdims=True)
    d_mid = norm_back(d_second, normed, inverse, gain_two) + d_y
    dmid_ref[...] = d_mid
    d_low = d_mid.astype(BF)
    dz_ref[...] = d_low
    wait(first + 3)
    d_mixed = mm(d_low, wo[...], NT).astype(BF)
    wide = SHARE * HEAD_SIZE
    for h in range(KEY_VALUE_HEADS):
        dao_ref[h] = d_mixed[:, h * wide : (h + 1) * wide]


def project_back(own_ref, others, dq_ref, x, dmid_ref, gain_one, cosine, sine, wait, wqkv, dqkv_ref, sum_ref):
    total = own_ref[...].astype(F32)
    for other in others:
        total = total + other[...].astype(F32)
    d_key = jnp.concatenate(
        [total[:, h * 128 : h * 128 + HEAD_SIZE] for h in range(KEY_VALUE_HEADS)], axis=1
    )
    d_value = jnp.concatenate(
        [total[:, h * 128 + HEAD_SIZE : (h + 1) * 128] for h in range(KEY_VALUE_HEADS)], axis=1
    )
    d_query = jnp.concatenate([dq_ref[h] for h in range(KEY_VALUE_HEADS)], axis=1)
    d_rows = jnp.concatenate(
        [turn(d_query, cosine, sine, True), turn(d_key, cosine, sine, True), d_value], axis=1
    ).astype(BF)
    dqkv_ref[...] = d_rows
    wait(0)
    d_first = mm(d_rows, wqkv[:, : d_rows.shape[1]], NT)
    normed, inverse = normed_rows(x)
    sum_ref[...] = jnp.sum(d_first * normed, axis=0, keepdims=True)
    return norm_back(d_first, normed, inverse, gain_one) + dmid_ref[...]


def back_kernel(near, phase, weights, n_parts, *args):
    args = list(args)
    take = lambda k: [args.pop(0) for _ in range(k)]
    (coords_ref,) = take(1)
    if phase > 0:
        gain1_ref, cos_ref, sin_ref, x_ref, dmid_in, dq_ref = take(6)
        own_ref, *others = take(n_parts)
    if phase < 3:
        gain2_ref, mid_ref, g_ref, u_ref = take(4)
    if phase == 0:
        cot_ref, sel_ref, live3_ref = take(3)
    elif phase == 1:
        slots_ref, live3_ref, live2_ref = take(3)
    elif phase == 2:
        cot_ref, sel_ref, live2_ref = take(3)
    refs = take(len(arrays_of(weights)))
    if phase > 0:
        dqkv_ref, sum1_ref = take(2)
    if phase < 3:
        outs = take(7)
    if phase == 0:
        (slots_out,) = take(1)
    elif phase == 3:
        (grad_ref,) = take(1)
    turns = ((0, 0),) if phase > 0 else ()
    first = len(turns)
    if phase < 3:
        turns += ((first, 0),)
        turns += tuple((first + w, j) for j in range(FF_CHUNKS) for w in (1, 2))
        turns += ((first + 3, 0),)
    buffers, wait = weights_here(near, weights, refs, args, coords_ref, turns)
    if phase > 0:
        d_x = project_back(
            own_ref, others, dq_ref, x_ref[...].astype(F32), dmid_in, gain1_ref[...],
            cos_ref[...], sin_ref[...], wait, buffers[0], dqkv_ref, sum1_ref,
        )
    if phase == 0:
        chosen = picks(sel_ref, cot_ref.shape[1]).astype(BF)
        slots = mm(chosen, cot_ref[...].T, TN)
        slots_out[...] = slots
        rows = mid_ref.shape[0]
        d_y = jnp.where(live_column(live3_ref, rows), slots[:rows], 0.0)
    elif phase == 1:
        rows = x_ref.shape[0]
        slots = slots_ref[...]
        head = jnp.where(live_column(live3_ref, rows), d_x, slots[:rows])
        slots = jnp.concatenate([head, slots[rows:]], axis=0)
        d_y = jnp.where(live_column(live2_ref, slots.shape[0]), slots, 0.0)
    elif phase == 2:
        hit = picks(sel_ref, cot_ref.shape[1]) & (live2_ref[...] > 0)
        placed = mm(hit.astype(F32), d_x, NN, lax.Precision.HIGHEST)
        any_hit = jnp.sum(hit.astype(F32), axis=1, keepdims=True) > 0.5
        d_y = jnp.where(any_hit, placed, cot_ref[...].astype(F32).T)
    else:
        grad_ref[...] = d_x.T.astype(BF)
        return
    feed_back(
        wait, first, d_y, mid_ref, g_ref, u_ref, gain2_ref[...],
        *buffers[first : first + 4], *outs,
    )


def back_call(near, phase, coords, before, parts, into, extra, weights, rows_next):
    specs, arrays, scratch = weights_in(near, weights)
    ins = list(before) + list(parts) + list(into) + list(extra)
    outs = []
    if phase > 0:
        rows, width = before[3].shape
        qkv_width = width + 2 * KEY_VALUE_HEADS * HEAD_SIZE
        outs += [stored((rows, qkv_width), BF), stored((1, width), F32)]
    if phase < 3:
        rows, hidden = into[2].shape
        width = into[1].shape[1]
        outs += [
            stored((rows, width), BF),
            stored((rows, hidden), BF),
            stored((rows, hidden), BF),
            stored((rows, width), F32),
            stored((rows, width), BF),
            shaped((KEY_VALUE_HEADS, rows, SHARE * HEAD_SIZE), BF),
            stored((1, width), F32),
        ]
    if phase == 0:
        outs += [stored((rows_next, width), F32)]
    elif phase == 3:
        outs += [stored((width, rows), BF)]
    return pl.pallas_call(
        functools.partial(back_kernel, near, phase, weights, len(parts)),
        name=f"back_{phase}",
        out_shape=tuple(outs),
        in_specs=[sm()] + [vm()] * len(ins) + specs,
        out_specs=tuple(vm() for _ in outs),
        scratch_shapes=scratch,
        compiler_params=params(12 if near else 50),
        cost_estimate=estimate(6),
    )(coords, *before, *parts, *into[:1], *apart(into[1:]), *extra, *arrays)


def stack_rows(refs, scratch):
    at = 0
    for ref in refs:
        scratch[at : at + ref.shape[0], :] = ref[...]
        at += ref.shape[0]


SPARE = 8


def put_blocks(value, x_of, coords, ref, spare=None):
    y, _, _, z = coords
    depth = value.shape[0] // 8
    for ya in range(2):
        for za in range(4):
            row = (ya * 4 + za) * depth
            block = value[row : row + depth].astype(BF)
            if spare is None:
                ref[y ^ ya, x_of, z ^ za] = block
            else:
                ref[y ^ ya, x_of, z ^ za, :depth] = block
                ref[y ^ ya, x_of, z ^ za, depth:] = spare(ya, za).astype(BF)


def grad_cols_kernel(n_steps, coords_ref, *args):
    left, args = args[:n_steps], args[n_steps:]
    right, args = args[:n_steps], args[n_steps:]
    keep_ref, send_ref, l_scr, r_scr = args
    coords = read_coords(coords_ref)
    _, c, x, _ = coords
    stack_rows(left, l_scr)
    stack_rows(right, r_scr)
    block = keep_ref.shape[-1]
    for far, ref in ((1, send_ref), (0, keep_ref)):

        def body(rx, carry, far=far, ref=ref):
            start = pl.multiple_of(((c ^ far) * 2 + (x ^ rx)) * block, 128)
            value = mm(l_scr[...], r_scr[:, pl.ds(start, block)], TN)
            put_blocks(value, rx, coords, ref)
            return carry

        lax.fori_loop(0, 2, body, 0)


def grad_rows_kernel(n_steps, coords_ref, *args):
    left, args = args[:n_steps], args[n_steps:]
    right, args = args[:n_steps], args[n_steps:]
    keep_ref, send_ref, l_scr, r_scr = args
    coords = read_coords(coords_ref)
    y, c, x, z = coords
    stack_rows(left, l_scr)
    stack_rows(right, r_scr)
    depth = keep_ref.shape[-2]
    span = 8 * depth
    for far, ref in ((1, send_ref), (0, keep_ref)):

        def body(ry, carry, far=far, ref=ref):
            start = pl.multiple_of(((y ^ ry) * 2 + (c ^ far)) * span, 128)
            value = mm(l_scr[:, pl.ds(start, span)], r_scr[...], TN)
            for xa in range(2):
                for za in range(4):
                    row = (xa * 4 + za) * depth
                    ref[ry, x ^ xa, z ^ za] = value[row : row + depth].astype(BF)
            return carry

        lax.fori_loop(0, 2, body, 0)


def grad_mixed_kernel(n_steps, coords_ref, sums_ref, *args):
    groups = []
    for _ in range(4):
        groups.append(args[:n_steps])
        args = args[n_steps:]
    keep_ref, send_ref, first_scr, mixed_scr, qkv_scr, z_scr, val_scr = args
    coords = read_coords(coords_ref)
    _, c, x, _ = coords
    for refs, scr in zip(groups, (first_scr, mixed_scr, qkv_scr, z_scr), strict=True):
        stack_rows(refs, scr)
    block = keep_ref.shape[-1]
    width = z_scr.shape[1]
    kv_width = (qkv_scr.shape[1] - width) // 2
    for ca in range(2):
        for xa in range(2):
            if ca == 0:
                val_scr[...] = mm(first_scr[...], qkv_scr[:, xa * block : (xa + 1) * block], TN)
            elif xa == 0:
                val_scr[...] = mm(mixed_scr[...], z_scr[:, :block], TN)
            else:
                val_scr[...] = jnp.concatenate(
                    [
                        mm(mixed_scr[...], z_scr[:, block:], TN),
                        mm(first_scr[...], qkv_scr[:, width + kv_width :], TN),
                    ],
                    axis=1,
                )

            def spare(ya, za, first=ca == 0 and xa == 0):
                if not first or za:
                    return jnp.zeros((SPARE, block), F32)
                half = width // 2
                rows = sums_ref[:, ya * half : (ya + 1) * half]
                rows = jnp.concatenate([rows, jnp.zeros((2, block - half), F32)], axis=1)
                return jnp.concatenate([rows, jnp.zeros((SPARE - 2, block), F32)], axis=0)

            @pl.when(c == ca)
            def _(xa=xa, spare=spare):
                put_blocks(val_scr[...], x ^ xa, coords, keep_ref, spare)

            @pl.when(c != ca)
            def _(xa=xa, spare=spare):
                put_blocks(val_scr[...], x ^ xa, coords, send_ref, spare)


def grad_call(kind, coords, groups, sums=None):
    n_steps = len(groups[0])
    rows = sum(a.shape[0] for a in groups[0])
    width, cols = groups[0][0].shape[1], groups[1][0].shape[1]
    scratch = [pltpu.VMEM((rows, g[0].shape[1]), BF) for g in groups]
    if kind == "rows":
        kernel, block = grad_rows_kernel, (width // 32, cols)
    elif kind == "cols":
        kernel, block = grad_cols_kernel, (width // 8, cols // 4)
    else:
        total = sum(g[0].shape[1] for g in groups[2:])
        kernel, block = grad_mixed_kernel, (width // 8 + SPARE, total // 4)
        scratch += [pltpu.VMEM((width, block[1]), F32)]
    out = shaped((2, 2, 4) + block, BF)
    ins = [a for g in groups for a in g]
    if sums is not None:
        ins = [sums, *ins]
    return pl.pallas_call(
        functools.partial(kernel, n_steps),
        name=f"grad_{kind}",
        out_shape=(out, out),
        in_specs=[sm()] + [vm()] * len(ins),
        out_specs=(vm(), vm()),
        scratch_shapes=scratch,
        compiler_params=params(16),
        cost_estimate=estimate(6),
    )(coords, *apart(ins))


def place_cols_kernel(coords_ref, near_ref, far_ref, *outs):
    _, c, x, z = read_coords(coords_ref)
    block = near_ref.shape[-1]
    mixed = len(outs) > 1
    target = outs[5] if mixed else outs[0]
    depth = target.shape[0]
    for far, ref in ((0, near_ref), (1, far_ref)):
        for rx in range(2):
            cols = pl.ds(pl.multiple_of(((c ^ far) * 2 + (x ^ rx)) * block, 128), block)
            target[:, cols] = ref[rx, 0, :depth].astype(F32)
    if mixed:
        q_ref, k_ref, o_ref, v_ref, gains_ref, _, k_scr, v_scr = outs
        width, kv_width = q_ref.shape[1], k_ref.shape[0]
        rows = pl.ds(pl.multiple_of((z ^ pl.program_id(0)) * depth, 8), depth)
        q_ref[...] = target[:, :width]
        k_scr[rows, :] = target[:, width : width + kv_width]
        o_ref[...] = target[:, width + kv_width : 2 * width + kv_width]
        v_scr[rows, :] = target[:, 2 * width + kv_width :]
        for far, ref in ((0, near_ref), (1, far_ref)):

            @pl.when((z == pl.program_id(0)) & (c == far))
            def _(ref=ref):
                spare = ref[x, 0, depth:].astype(F32)
                gains_ref[...] = spare[:2, : gains_ref.shape[1]]

        @pl.when(pl.program_id(0) == 3)
        def _():
            k_ref[...] = k_scr[...].T
            v_ref[...] = v_scr[...].T


def place_rows_kernel(coords_ref, near_ref, far_ref, out_ref, scr):
    _, _, x, z = read_coords(coords_ref)
    depth = near_ref.shape[-2]

    def put(ref):
        for rx in range(2):
            for rz in range(4):
                row = pl.multiple_of(((x ^ rx) * 4 + (z ^ rz)) * depth, 8)
                scr[pl.ds(row, depth), :] = ref[rx, rz].astype(F32)

    @pl.when(pl.program_id(0) == 0)
    def _():
        put(near_ref)

    @pl.when(pl.program_id(0) == 1)
    def _():
        put(far_ref)

    out_ref[...] = scr[...].T


def place_call(kind, coords, near, far, widths):
    depth, block = near.shape[-2:]
    scratch = []
    if kind == "rows":
        kernel, grid = place_rows_kernel, (2,)
        outs = (stored((block, 16 * depth), F32),)
        source = pl.BlockSpec((2, 4, depth, block), lambda f, k: (0, 0, 0, 0))
        targets = (pl.BlockSpec((block, 8 * depth), lambda f, k: (0, k[1] ^ f)),)
        scratch = [pltpu.VMEM((8 * depth, block), F32)]
    else:
        kernel, grid = place_cols_kernel, (4,)
        source = pl.BlockSpec((2, 1, *near.shape[-2:]), lambda i, k: (0, i, 0, 0))
        if len(widths) > 1:
            depth -= SPARE
        straight = lambda w: (
            stored((4 * depth, w), F32), pl.BlockSpec((depth, w), lambda i, k: (k[3] ^ i, 0))
        )
        turned = lambda w: (
            stored((w, 4 * depth), F32), pl.BlockSpec((w, 4 * depth), lambda i, k: (0, 0))
        )
        outs, targets = zip(
            *((turned if i % 2 else straight)(w) for i, w in enumerate(widths)), strict=True
        )
        if len(outs) > 1:
            outs += (stored((2, 4 * depth), F32),)
            targets += (pl.BlockSpec((2, 4 * depth), lambda i, k: (0, 0)),)
            scratch = [pltpu.VMEM((depth, 4 * block), F32)]
            scratch += [pltpu.VMEM((4 * depth, w), F32) for w in widths[1::2]]
    return pl.pallas_call(
        kernel,
        name=f"place_{kind}",
        grid_spec=pltpu.PrefetchScalarGridSpec(
            num_scalar_prefetch=1,
            grid=grid,
            in_specs=[source, source],
            out_specs=targets,
            scratch_shapes=scratch,
        ),
        out_shape=outs,
        compiler_params=params(12),
        cost_estimate=estimate(),
    )(coords, near, far)


def low_sum(left, right):
    return (left.astype(F32) + right.astype(F32)).astype(BF)


def split_list(values, count):
    return values[:count], values[count:]


def gather_keys(kv, order, near, meanwhile=([], [])):
    if not near:
        whole = lax.all_gather(kv, "ctx", axis=0, tiled=True)
        half = whole.shape[0] // 2
        return whole[:half], whole[half:]
    kv = order.take(kv)
    hops = [hop(kv, m) for m in (X_BIT, Y_BIT, Z1_BIT, X_BIT | Y_BIT | Z1_BIT)]
    (by_x, by_y, by_z, across), meanwhile[0][:] = split_list(order.all(*hops, *meanwhile[0]), 4)
    hops = [hop(by_x, Y_BIT), hop(by_y, Z1_BIT), hop(by_z, X_BIT)]
    hops, meanwhile[1][:] = split_list(order.all(*hops, *meanwhile[1]), 3)
    part = stack_call([kv, by_x, by_y, by_z, across, *hops])
    return part, order.take(hop(part, C_BIT))


class KeySums:
    def __init__(self, own, others):
        self.own = own
        self.near, self.across, self.beyond = others[:3], others[3], others[4:]

    def sends(self, turn):
        if turn == 0:
            return list(zip(self.beyond, (Y_BIT, Z1_BIT, X_BIT), strict=True))
        return [
            (self.across, X_BIT | Y_BIT | Z1_BIT),
            *zip(self.near, (X_BIT, Y_BIT, Z1_BIT), strict=True),
        ]

    def got(self, turn, values):
        if turn == 0:
            self.near = [low_sum(a, b) for a, b in zip(self.near, values, strict=True)]
        else:
            self.result = [self.own, *values]


class Hop:
    def __init__(self, value, mask):
        self.value, self.mask = value, mask

    def sends(self, turn):
        return [(self.value, self.mask)]

    def got(self, turn, values):
        (self.result,) = values


def scatter_keys(part_a, part_b, order, near):
    if not near:
        whole = jnp.concatenate([part_a, part_b.astype(F32)], axis=0)
        return [lax.psum_scatter(whole, "ctx", scatter_dimension=0, tiled=True)]
    far = Hop(part_b, C_BIT)
    (part_a,) = wave(order, [(far, 0)], lambda a: (a,), (part_a,))
    own, *others = split_call(part_a, far.result)
    sums = KeySums(own, others)
    wave(order, [(sums, 0)])
    wave(order, [(sums, 1)])
    return sums.result


def cut_rows(value, index, count):
    size = value.shape[0] // count
    return lax.dynamic_slice_in_dim(value, index * size, size, 0)


def cut_cols(value, index, count):
    size = value.shape[1] // count
    return lax.dynamic_slice_in_dim(value, index * size, size, 1)


class Share:
    def __init__(self, mine):
        self.mine = mine

    def sends(self, turn):
        return [(self.mine, mask) for mask in (X_BIT | Z1_BIT, X_BIT, Z1_BIT)]

    def got(self, turn, values):
        across, by_x, by_z = values
        self.result = [self.mine, by_x, by_z, across]


def pair_sum(keep, send, near):
    if near:
        return low_sum(keep, hop(send, C_BIT))
    return lax.psum(jnp.stack([keep, send]).astype(F32), AXES)


ALONG_Z = (Z1_BIT, Z2_BIT, Z1_BIT | Z2_BIT)
FAR_FIRST = (2, 1, 0)


class BlockSums:
    rounds = 6

    def __init__(self, total):
        self.total = total

    def sends(self, turn):
        if turn == 0:
            return [(self.total[1, 1], Y_BIT)]
        if turn == 1:
            return [(self.total[1, 0], Y_BIT), (low_sum(self.total[0, 1], self.came), X_BIT)]
        if turn == 2:
            return [(self.total[i + 1], ALONG_Z[i]) for i in FAR_FIRST]
        if turn == 3:
            return [(self.mine, ALONG_Z[i]) for i in FAR_FIRST]
        if turn == 4:
            return [(self.total, X_BIT)]
        return [(self.total, C_BIT)]

    def got(self, turn, values):
        if turn == 0:
            (self.came,) = values
        elif turn == 1:
            total = self.total[0, 0].astype(F32)
            for value in values:
                total = total + value.astype(F32)
            self.total = total.astype(BF)
        elif turn == 2:
            mine = self.total[0].astype(F32)
            for value in values:
                mine = mine + value.astype(F32)
            self.mine = mine.astype(BF)
        elif turn == 3:
            self.total = jnp.stack([self.mine, *values[::-1]])
        elif turn == 4:
            self.total = jnp.stack([self.total, *values])
        else:
            self.result = (self.total, *values)


class BothWays(BlockSums):
    def sends(self, turn):
        if turn == 0:
            return [(self.total[1, :, :2], Y_BIT), (self.total[:, 1, 2:], X_BIT)]
        if turn == 1:
            return [(self.first[1], X_BIT), (self.second[1], Y_BIT)]
        return super().sends(turn)

    def got(self, turn, values):
        if turn == 0:
            self.first = low_sum(self.total[0, :, :2], values[0])
            self.second = low_sum(self.total[:, 0, 2:], values[1])
        elif turn == 1:
            self.total = jnp.concatenate(
                [low_sum(self.first[0], values[0]), low_sum(self.second[0], values[1])]
            )
        else:
            super().got(turn, values)


class Move:
    rounds = 1

    def __init__(self, value):
        self.value = value

    def sends(self, turn):
        return [(self.value, None)]

    def got(self, turn, values):
        (self.result,) = values


def wave(order, steps, work=None, uses=()):
    plans = [chain.sends(turn) for chain, turn in steps]
    flat = [value for plan in plans for value, _ in plan]
    taken = order.all(*flat, *uses)
    sent, uses = taken[: len(flat)], taken[len(flat) :]
    masks = [mask for plan in plans for _, mask in plan]
    came = [move(v) if mask is None else hop(v, mask) for v, mask in zip(sent, masks, strict=True)]
    made = list(work(*uses)) if work else []
    came = order.all(*came, *made)
    came, made = came[: len(flat)], came[len(flat) :]
    for (chain, turn), plan in zip(steps, plans, strict=True):
        chain.got(turn, came[: len(plan)])
        came = came[len(plan) :]
    return made


def on_device(
    tokens, cotangent, w_query, key_weight, value_weight, w_out, w_gate, w_up, w_down,
    gain_attn, gain_ffn, block_order, sel_mid, live_mid, sel_last, live_last,
):
    ctx_count, ws_count = lax.axis_size("ctx"), lax.axis_size("ws")
    near = ctx_count == 16 and ws_count == 2
    ctx, y = lax.axis_index("ctx"), lax.axis_index("ws")
    tok_local = tokens.shape[1]
    cap_mid, cap_last = sel_mid.shape[1] // ctx_count, sel_last.shape[1] // ctx_count
    if near:
        c, x, z = ctx & 1, (ctx >> 1) & 1, ctx >> 2
        places = (y, c, x, z)
        here = (ctx & 7) | (y << 3)
        turn_order = here ^ jnp.array([ctx_mask(m) for m in NEAR] + [ctx_mask(m) | 1 for m in NEAR], jnp.int32)
        relocate = move
    else:
        zero = jnp.int32(0)
        places = (y, zero, zero, zero)
        here = ctx
        turn_order = jnp.arange(ctx_count, dtype=jnp.int32)
        relocate = lambda v: v
    coords = jnp.stack([jnp.asarray(v, jnp.int32) for v in places])
    block_coords = coords if near else jnp.zeros((4,), jnp.int32)
    width = tokens.shape[2]
    half = w_query.shape[0]
    plan = jnp.concatenate(
        [
            sel_mid.reshape(ctx_count, cap_mid),
            live_mid.reshape(ctx_count, cap_mid),
            live_last.reshape(ctx_count, cap_last),
        ],
        axis=1,
    )
    order = Order(coords)
    if near:
        assert tok_local <= 256
        own_qkv, piece = pack_call(coords, w_query, key_weight.T, value_weight.T)
        fetched = hop(piece, Y_BIT)
        tok = move(pack_rows_call(tokens[0].T, plan))
        gains = jnp.concatenate([gain_attn.reshape(1, -1), gain_ffn.reshape(1, -1)], axis=0)
        beyond = hop(gains, Y_BIT)
        quad = x * 2 + (z & 1)
        own_down = w_down.T
        fetched, cut_pair, cut_out, cut_down = order.take(
            fetched,
            jnp.concatenate([cut_cols(cut_rows(w, c, 2), quad, 4) for w in (w_gate, w_up)], axis=0),
            cut_rows(w_out, c, 2),
            cut_rows(own_down, c, 2),
        )
        far = hop(fetched, C_BIT)
        pair_mine, out_mine = hop(cut_pair, Y_BIT), hop(cut_out, Y_BIT)
        far, tok, beyond = order.take(far, tok, beyond)
        plan = tok[tok_local:, : plan.shape[1]].astype(jnp.int32)
        tok = tok[:tok_local]
        depth = half // 2
        gains = jnp.where(
            y == 0,
            jnp.concatenate([gains, beyond], axis=1),
            jnp.concatenate([beyond, gains], axis=1),
        )
        gains = [gains[0:1], gains[1:2]]
        origin = lambda *k: (0, 0)

        def in_rows(own, mine, other):
            wide = own.shape[1]
            return Weight(
                (2 * half, wide),
                [own, mine, other],
                [
                    [
                        (0, half, wide, origin, lambda ky, kc, kx, kz: (ky * half, 0)),
                        (1, depth, wide, origin, lambda ky, kc, kx, kz: ((1 - ky) * half + kc * depth, 0)),
                        (2, depth, wide, origin, lambda ky, kc, kx, kz: ((1 - ky) * half + (1 - kc) * depth, 0)),
                    ]
                ],
            )

        def in_parts(own, mine, other, which):
            wide = mine.shape[1]
            groups = []
            for j in range(FF_CHUNKS):
                column = lambda *k, j=j: part_of(j, k) * wide
                block = lambda *k, j=j: ((2 * j + which) * depth, 0)
                groups.append(
                    [
                        (0, half, wide,
                         lambda *k, column=column: (0, column(*k)),
                         lambda *k, column=column: (k[0] * half, column(*k))),
                        (1, depth, wide, block,
                         lambda *k, column=column: ((1 - k[0]) * half + k[1] * depth, column(*k))),
                        (2, depth, wide, block,
                         lambda *k, column=column: ((1 - k[0]) * half + (1 - k[1]) * depth, column(*k))),
                    ]
                )
            return Weight((2 * half, own.shape[1]), [own, mine, other], groups)

        weight_qkv = one_piece(join_call(coords, (in_rows(own_qkv, fetched, far),))[0])
        marks = {}

        def fetch_rest(pair, out, down):
            pair = stack_call(pair)
            shared = [Hop(v, C_BIT) for v in (pair, out, down)]
            wide = own_down.shape[1]

            def whole_weights(pair_far, out_far, down_far):
                weight_d = Weight(
                    (width, 2 * wide),
                    [own_down, down, down_far],
                    [
                        [
                            (0, width, wide, origin, lambda ky, kc, kx, kz: (0, ky * wide)),
                            (1, width // 2, wide, origin, lambda ky, kc, kx, kz: (kc * (width // 2), (1 - ky) * wide)),
                            (2, width // 2, wide, origin, lambda ky, kc, kx, kz: ((1 - kc) * (width // 2), (1 - ky) * wide)),
                        ]
                    ],
                )
                return (
                    in_rows(w_out, out, out_far),
                    in_parts(w_gate, pair, pair_far, 0),
                    in_parts(w_up, pair, pair_far, 1),
                    weight_d,
                )

            begun = [part_of_weight(w, True) for w in whole_weights(pair, out, down)]
            bases = wave(order, [(s, 0) for s in shared], lambda k: join_call(k, begun), (coords,))
            rest = whole_weights(*(s.result for s in shared))
            joined = join_call(coords, [part_of_weight(w, False) for w in rest], bases)
            return tuple(one_piece(w) for w in joined)
    else:
        tok = tokens[0]
        whole = lambda w: lax.all_gather(w, "ws", axis=0, tiled=True)
        weight_qkv = one_piece(whole(jnp.concatenate([w_query, key_weight, value_weight], axis=1)))
        gains = [whole(g).reshape(1, -1) for g in (gain_attn, gain_ffn)]
        far_weights = (
            one_piece(whole(w_out)), in_columns(whole(w_gate)), in_columns(whole(w_up)),
            one_piece(whole(w_down).T),
        )
        fetch_rest = lambda: far_weights
    gain1, gain2 = (g.astype(F32) for g in gains)

    per_device = tok_local // BLK
    blocks = jnp.take(block_order.reshape(ctx_count, per_device), turn_order, axis=0)
    plan_order = jnp.take(plan, turn_order, axis=0)
    sel_all = plan_order[:, :cap_mid]
    live_two = plan_order[:, cap_mid : 2 * cap_mid]
    live_three = plan_order[:, 2 * cap_mid :]
    place_one = (blocks[:, :, None] * BLK + jnp.arange(BLK, dtype=jnp.int32)).reshape(ctx_count, tok_local)
    place_two = sum(
        jnp.where(sel_all // BLK == k, blocks[:, k : k + 1], 0) for k in range(per_device)
    ) * BLK + sel_all % BLK
    place_three = place_two[:, :cap_last]
    if near:
        mine = lambda v: v[0:1]
    else:
        mine = lambda v: lax.dynamic_slice_in_dim(v, here, 1, 0)
    sel_own, live2_own, live3_own = mine(sel_all), mine(live_two), mine(live_three)
    own_places = jnp.concatenate([mine(place_one), mine(place_two)], axis=1).reshape(-1, 1)
    frequency = ROPE_BASE ** (-jnp.arange(HEAD_SIZE // 2, dtype=F32) / (HEAD_SIZE // 2))
    angles = own_places.astype(F32) * frequency[None, :]
    cosine, sine = jnp.cos(angles), jnp.sin(angles)
    cosine = jnp.concatenate([cosine] * 4, axis=1)
    sine = jnp.concatenate([-sine, sine, -sine, sine], axis=1)
    tables = [
        (cosine[:tok_local], sine[:tok_local]),
        (cosine[tok_local:], sine[tok_local:]),
        (cosine[tok_local : tok_local + cap_last], sine[tok_local : tok_local + cap_last]),
    ]
    query_places = [mine(v) for v in (place_one, place_two, place_three)]
    key_places = [v.reshape(1, -1) for v in (place_one, place_two, place_three)]
    key_live = [
        jnp.ones((1, ctx_count * tok_local), jnp.int32),
        live_two.reshape(1, -1),
        live_three.reshape(1, -1),
    ]
    prompt = ctx_count * tok_local // 2
    if near:
        key_places[0], query_places[0] = order.take(key_places[0], query_places[0])
        marks["places"] = [*query_places[1:], *key_places[1:], *key_live[1:], sel_own, live2_own, live3_own]
        marks["tables"] = [*tables[1], *tables[2]]

    firsts, mixeds, seconds, hiddens = [], [], [], []
    records = []
    xs = [tok]
    first_in, query, kv = first_call(near, coords, tok, gain1, *tables[0], (weight_qkv,))
    heights = []
    for step in range(3):
        if near and step == 0:
            waits = ([*marks["places"], pair_mine], [*marks["tables"], out_mine])
            part_a, part_b = gather_keys(kv, order, near, waits)
            *marks["places"], pair_mine = waits[0]
            *marks["tables"], out_mine = waits[1]
        else:
            part_a, part_b = gather_keys(kv, order, near)
        if near and step == 1:
            query_places[1:], key_places[1:], key_live[1:] = (marks["places"][i : i + 2] for i in (0, 2, 4))
        firsts.append(first_in)
        next_rows = (cap_mid, cap_last, tok_local)[step]
        attention = (query, part_a, part_b, key_places[step], key_live[step], query_places[step], prompt)
        if near and step == 0:
            pair, down_mine = Share(pair_mine), Hop(cut_down, Y_BIT)
            weights, mixed = wave(
                order, [(down_mine, 0), (pair, 0)], lambda *a: attend_call(*a, prompt), attention[:-1]
            )
            dense_weights = fetch_rest(pair.result, out_mine, down_mine.result)
            sel_own, live2_own, live3_own = marks["places"][6:]
            tables[1:] = [marks["tables"][:2], marks["tables"][2:]]
        elif step == 0:
            weights, mixed = attend_call(*attention)
            dense_weights = fetch_rest()
        if step == 0:
            extra = (sel_own, *tables[1])
        elif step == 1:
            extra = (live2_own, *tables[2])
        else:
            extra = (sel_own, live2_own, live3_own, heights[0], heights[1])
        mats = dense_weights + ((weight_qkv,) if step < 2 else ())

        def dense(mixed, step=step, extra=extra, mats=mats, next_rows=next_rows):
            return dense_call(
                near, step, coords, xs[step], mixed, gain1, gain2, extra, mats, next_rows
            )

        def both(*a):
            made = attend_call(*a, prompt)
            return *made, *dense(made[1])

        if step == 0:
            result = dense(mixed)
        elif step == 1 and near:
            there = Move(cotangent[0].T)
            weights, mixed, *result = wave(order, [(there, 0)], both, attention[:-1])
            cot = there.result
        else:
            weights, mixed, *result = both(*attention[:-1])
            if step == 1:
                cot = cotangent[0].T
        mixed_rows, middle, second, gate, up, hidden = result[:6]
        mixeds.append(mixed_rows)
        seconds.append(second)
        hiddens.append(hidden)
        records.append((query, part_a, part_b, weights, middle, gate, up))
        if step < 2:
            height, following, first_in, query, kv = result[6:]
            heights.append(height)
            xs.append(following)
        else:
            output = relocate(order.take(result[6]))

    d_firsts, d_seconds = [None] * 3, [None] * 3
    sums_one, sums_two = [], []
    slots = None
    parts, d_query, d_middle = (), None, None
    column = lambda rows, i: [r[i] for r in rows]

    def grads(kind, groups):
        return grad_call(kind, block_coords, groups)

    for phase in range(4):
        step = 2 - phase
        before, into = (), ()
        if phase > 0:
            before = (gain1, *tables[step + 1], xs[step + 1], d_middle, d_query)
        if phase < 3:
            into = (gain2, *records[step][4:7])
        mats = (dense_weights[3], dense_weights[1], dense_weights[2], dense_weights[0])
        if phase == 0:
            extra, mats = (cot, sel_own, live3_own), mats
        elif phase == 1:
            extra, mats = (slots, live3_own, live2_own), (weight_qkv,) + mats
        elif phase == 2:
            extra, mats = (cot, sel_own, live2_own), (weight_qkv,) + mats
        else:
            extra, mats = (), (weight_qkv,)
        last = lambda *parts: back_call(near, phase, coords, before, parts, into, extra, mats, cap_mid)
        if near and phase == 3:
            break
        result = list(last(*parts))
        if phase > 0:
            d_firsts[step + 1], total = result[:2]
            sums_one.append(total)
            result = result[2:]
        if phase == 3:
            grad_tokens = result[0]
            break
        d_low, d_gate, d_up, d_middle, d_mid_low, d_mixed, total = result[:7]
        d_seconds[step] = (d_low, d_gate, d_up, d_mid_low)
        sums_two.append(total)
        if phase == 0:
            slots = result[7]
        query, part_a, part_b, weights = records[step][:4]
        if phase < 2:
            d_mixed = order.take(d_mixed)
            d_query, term_a, term_b = attend_back_call(query, d_mixed, part_a, part_b, weights)
            if phase == 0:
                output, term_b = order.take(output, term_b)
            parts = scatter_keys(term_a, term_b, order, near)

        else:
            attend_last = lambda d: attend_back_call(query, d, part_a, part_b, weights)
            gate_grads = lambda *d: grads("cols", [seconds, list(d)])
            down_grads = grads("rows", [hiddens, column(d_seconds, 0)])
            if not near:
                d_query, term_a, term_b = attend_last(d_mixed)
                parts = scatter_keys(term_a, term_b, order, near)
                sums_of = [
                    pair_sum(*g, near)
                    for g in (down_grads, gate_grads(*column(d_seconds, 1)), gate_grads(*column(d_seconds, 2)))
                ]
                continue
            down = Hop(down_grads[1], C_BIT)
            gate_grads_made = wave(
                order, [(down, 0)], gate_grads, column(d_seconds, 1)
            )
            down = BothWays(low_sum(down_grads[0], down.result))
            gate = Hop(gate_grads_made[1], C_BIT)
            d_query, term_a, term_b = wave(order, [(down, 0), (gate, 0)], attend_last, (d_mixed,))
            gate = BlockSums(low_sum(gate_grads_made[0], gate.result))
            far = Hop(term_b, C_BIT)
            up_made = wave(order, [(down, 1), (far, 0)], gate_grads, column(d_seconds, 2))
            own, *others = split_call(term_a, far.result)
            keys, up = KeySums(own, others), Hop(up_made[1], C_BIT)
            wave(order, [(keys, 0), (up, 0)])
            wave(order, [(keys, 1)])
            up = BlockSums(low_sum(up_made[0], up.result))
            parts = keys.result

    kv_width = key_weight.shape[1]
    hidden_width = w_gate.shape[1]

    def mixed_grads(*d):
        sums = jnp.concatenate([sum(sums_one), sum(sums_two)], axis=0)
        return grad_call("mixed", block_coords, [firsts, mixeds, list(d), column(d_seconds, 3)], sums)

    def last_grads(*parts):
        d_firsts[0], total, grad_tokens = last(*parts)
        sums_one.append(total)
        return *mixed_grads(*d_firsts), grad_tokens

    placed = {}

    if near:
        def place(kind, widths):
            return lambda near_blocks, far_blocks, at: place_call(kind, at, near_blocks, far_blocks, widths)

        placing = lambda chain: (*chain.result, coords)
        *rest_made, grad_tokens = wave(order, [(gate, 0), (down, 2)], last_grads, parts)
        rest = Hop(rest_made[1], C_BIT)
        wave(order, [(gate, 1), (down, 3), (rest, 0)])
        rest = BlockSums(low_sum(rest_made[0], rest.result))
        wave(order, [(up, 0), (gate, 2), (down, 4)])
        wave(order, [(up, 1), (gate, 3)])
        wave(order, [(rest, 0), (up, 2), (gate, 4)])
        wave(order, [(rest, 1), (up, 3)])
        wave(order, [(rest, 2), (up, 4), (down, 5)])
        placed["down"] = wave(
            order, [(rest, 3), (up, 5), (gate, 5)], place("rows", None), placing(down)
        )
        tokens_back = Move(grad_tokens)

        def place_two(*arrays):
            cols = place("cols", (hidden_width,))
            return *cols(*arrays[:3]), *cols(*arrays[3:])

        placed["gate"], placed["up"] = wave(
            order, [(rest, 4), (tokens_back, 0)], place_two, (*placing(gate), *placing(up))
        )
        grad_tokens = tokens_back.result.astype(F32)
        wave(order, [(rest, 5)])
        placed["rest"] = order.all(
            *place("cols", (width, kv_width, width, kv_width))(*rest.result, order.token)
        )
        (placed["down"],) = placed["down"]
    else:
        sums_of.append(pair_sum(*mixed_grads(*d_firsts), near))
        for name, kind, widths, total in zip(
            ("down", "gate", "up", "rest"),
            ("rows", "cols", "cols", "cols"),
            (None, (hidden_width,), (hidden_width,), (width, kv_width, width, kv_width)),
            sums_of,
            strict=True,
        ):
            mine = lax.dynamic_index_in_dim(total, y, 1, keepdims=False)
            placed[name] = place_call(kind, block_coords, mine[0], mine[1], widths)
        for name in ("down", "gate", "up"):
            (placed[name],) = placed[name]
        grad_tokens = grad_tokens.astype(F32)
    grad_down, grad_gate, grad_up = placed["down"].T, placed["gate"], placed["up"]
    grad_query, grad_key, grad_out, grad_value, gain_sums = placed["rest"]
    grad_key, grad_value = grad_key.T, grad_value.T
    return (
        output.T[None],
        grad_tokens.T[None],
        grad_query,
        grad_key,
        grad_value,
        grad_out,
        grad_gate,
        grad_up,
        grad_down,
        gain_sums[0],
        gain_sums[1],
    )


def solution(mesh):
    rows = P("ws", "ctx", None)
    flat = P("ws", None)
    in_specs = (rows, rows) + (flat,) * 7 + (P("ws"), P("ws"), P()) + (flat,) * 4
    out_specs = (rows, rows) + (flat,) * 7 + (P("ws"), P("ws"))
    return jax.shard_map(
        on_device, mesh=mesh, in_specs=in_specs, out_specs=out_specs, check_vma=False
    )
```
